256 devices in a mesh: seq: 64 (over y, x_hi, z), head: 4 (over x_lo, core).
Axes of the slice: x: 4 (x_hi: 2, x_lo: 2; x = x_hi * 2 + x_lo), y: 4, z: 8, core: 2. Of those that a mesh axis runs over, the one named last changes fastest.
Arguments:
- qkv: bfloat16 [3, 49152, 1536], P(None, ('seq', 'head')), may hold values from -5 to 5
- key_tiles: int32 [12, 128, 27], P('head', 'seq'), may hold values from -1 to 127, as said below
Outputs:
- attended: bfloat16 [49152, 1536], P(('seq', 'head'))
The draws below stay inside these ranges and needn't reach their ends.
Inputs may be any that keep to these rules, and one draw needn't show every extreme that they name: Each list key_tiles[n, g] names distinct tiles, the query tile g among them, each differing from g by at most 1 in the time tile, the tile row and the tile column; named tiles come first and -1 fills the rest of the list.
All inputs are finite; a program needn't handle non-finite values.
Results may differ from the reference program's by a relative error of at most 0.0035.
Values may be sent and summed in bfloat16 or wider, within the bound.
No kernel may reach another device: no remote copies, remote signals or barrier semaphores. Data moves between devices by JAX's collectives and lax.ppermute only.
A program may use at most 192 MiB of HBM per device.

```python
import jax
import jax.numpy as jnp
from jax import lax

HEADS = 12
HEAD_DIM = 128
KMAX = 27
TIME_TILES = 4
TILE_ROWS = 4
TILE_COLS = 8
NTILES = 128
TOKENS = 49152


def draw_qkv(key, part):
    columns = HEADS * HEAD_DIM
    values = jnp.clip(1.6 * jax.random.normal(key, (3, TOKENS, columns), jnp.float32), -5.0, 5.0)
    return values.astype(jnp.bfloat16)


def draw_key_tiles(key, part):
    col_count = TILE_COLS
    reaches = jax.random.randint(jax.random.fold_in(key, 1), (HEADS, 3), 0, 2)
    widest = jax.random.randint(jax.random.fold_in(key, 2), (), 0, HEADS)
    reaches = jnp.where(jnp.arange(HEADS)[:, None] == widest, 1, reaches)
    offsets = jnp.arange(KMAX, dtype=jnp.int32)
    move_time = offsets // 9 - 1
    move_row = offsets // 3 % 3 - 1
    move_col = offsets % 3 - 1
    tile_number = jnp.arange(NTILES, dtype=jnp.int32)
    own_time = tile_number // 2 % TIME_TILES
    own_row = tile_number // (2 * TIME_TILES) % 2 * 2 + tile_number % 2
    own_col = tile_number // (4 * TIME_TILES)
    near_time = own_time[:, None] + move_time[None, :]
    near_row = own_row[:, None] + move_row[None, :]
    near_col = own_col[:, None] + move_col[None, :]
    inside = (near_time >= 0) & (near_time < TIME_TILES) & (near_row >= 0) & (near_row < TILE_ROWS) & (near_col >= 0) & (near_col < col_count)
    within = (jnp.abs(move_time)[None, :] <= reaches[:, 0:1]) & (jnp.abs(move_row)[None, :] <= reaches[:, 1:2]) & (jnp.abs(move_col)[None, :] <= reaches[:, 2:3])
    named_mask = inside[None, :, :] & within[:, None, :]
    safe_row = jnp.clip(near_row, 0, TILE_ROWS - 1)
    target = ((near_col * 2 + safe_row // 2) * TIME_TILES + near_time) * 2 + safe_row % 2
    target_all = jnp.broadcast_to(target[None, :, :], named_mask.shape)
    noise_draw = jax.random.randint(jax.random.fold_in(key, 3), named_mask.shape, 0, 1 << 20)
    sort_score = (1 - named_mask.astype(jnp.int32)) * (1 << 26) + noise_draw * 32 + offsets[None, None, :]
    sort_order = jnp.argsort(sort_score, axis=-1, stable=True)
    named_sorted = jnp.take_along_axis(named_mask, sort_order, axis=-1)
    target_sorted = jnp.take_along_axis(target_all, sort_order, axis=-1)
    return jnp.where(named_sorted, target_sorted, -1).astype(jnp.int32)


def setup_inputs(seed: int = 0) -> dict:
    key_of = jax.random.split(jax.random.key(seed), 3)
    return {
        "qkv": draw_qkv(jax.random.fold_in(key_of[2], 71), 0),
        "key_tiles": draw_key_tiles(jax.random.fold_in(key_of[2], 71), 0),
    }


def attend(query_rows, keys, values, named_mask):
    blocks, slot_count, row_count, head_feature_width = keys.shape
    key_matrix_rows = keys.reshape(blocks, slot_count * row_count, head_feature_width).astype(jnp.float32)
    value_matrix_rows = values.reshape(blocks, slot_count * row_count, head_feature_width).astype(jnp.float32)
    logit_matrix = jnp.einsum("jxg,jog->jxo", query_rows.astype(jnp.float32), key_matrix_rows, precision=lax.Precision.HIGHEST) * (head_feature_width ** -0.5)
    score_mask = jnp.repeat(named_mask, row_count, axis=1)[:, None, :]
    logit_matrix = jnp.where(score_mask, logit_matrix, -jnp.inf)
    row_max = jnp.max(logit_matrix, axis=-1, keepdims=True)
    weights = jnp.exp(logit_matrix - row_max)
    row_total = jnp.sum(weights, axis=-1, keepdims=True)
    lowered_precision = lax.optimization_barrier(weights.astype(jnp.bfloat16))
    weighted_value_sum = jnp.einsum("aop,ape->aoe", lowered_precision.astype(jnp.float32), value_matrix_rows, precision=lax.Precision.HIGHEST)
    return (weighted_value_sum / row_total).astype(jnp.bfloat16)


def reference(qkv, key_tiles):
    head_count = key_tiles.shape[0]
    tile_count = key_tiles.shape[1]
    tile_tokens = qkv.shape[1] // tile_count
    head_feature_width = qkv.shape[2] // head_count
    brick_count = tile_count // 2

    def tiles_of(stacked):
        return stacked.reshape(tile_count, tile_tokens, head_count, head_feature_width).transpose(2, 0, 1, 3)

    query_tiles = tiles_of(qkv[0])
    key_pool = tiles_of(qkv[1])
    value_pool = tiles_of(qkv[2])

    def per_head(operands):
        head_queries, head_keys, head_values, head_lists = operands

        def per_brick(brick_operands):
            brick_queries, brick_lists = brick_operands
            named_mask = brick_lists >= 0
            safe_index = jnp.where(named_mask, brick_lists, 0).astype(jnp.int32)
            return attend(brick_queries, head_keys[safe_index], head_values[safe_index], named_mask)

        return lax.map(per_brick, (head_queries.reshape(brick_count, 2, tile_tokens, head_feature_width), head_lists.reshape(brick_count, 2, KMAX)))

    result = lax.map(per_head, (query_tiles, key_pool, value_pool, key_tiles))
    reshaped = result.reshape(head_count, tile_count, tile_tokens, head_feature_width)
    return reshaped.transpose(1, 2, 0, 3).reshape(tile_count * tile_tokens, head_count * head_feature_width)
```

```python
import functools
import math

import jax
import jax.numpy as jnp
from jax import lax
from jax.experimental import pallas as pl
from jax.experimental.pallas import tpu as pltpu
from jax.sharding import PartitionSpec as P

TIME_TILES = 4
ROWS_PER_BRICK = 2
AXES = ("seq", "head")
FAR = -1e30
VMEM_LIMIT = 40 * 2**20


def linear(y, xh, z, xl, core):
    return ((y * 2 + xh) * 8 + z) * 4 + xl * 2 + core


def devices():
    for y in range(4):
        for xh in range(2):
            for z in range(8):
                for xl in range(2):
                    for core in range(2):
                        yield y, xh, z, xl, core


def spread_pairs(k):
    pairs = []
    for y, xh, z, xl, core in devices():
        group = (2 * xl + core) ^ k
        pairs.append((linear(y, xh, z, xl, core), linear(y, group >> 1, z, group & 1, xh)))
    return pairs


def gather_pairs(k):
    return [(b, a) for a, b in spread_pairs(k)]


def edge_pairs(k):
    pairs = []
    for y, xh, z, xl, core in devices():
        if xl == 1 - z // 4:
            group = (2 * xl + core) ^ k
            pairs.append((linear(y, xh, z, xl, core), linear(y, group >> 1, z ^ 4, group & 1, xh)))
    return pairs


def core_pairs():
    return [(linear(y, xh, z, xl, c), linear(y, xh, z, xl, 1 - c)) for y, xh, z, xl, c in devices()]


def column_pairs():
    pairs = []
    for y, xh, z, xl, core in devices():
        to = y + (1 if core == 1 else -1)
        if 0 <= to < 4:
            pairs.append((linear(y, xh, z, xl, core), linear(to, xh, z, xl, 1 - core)))
    return pairs


def time_pairs(by):
    pairs = []
    for y, xh, z, xl, core in devices():
        if 0 <= z % TIME_TILES + by < TIME_TILES:
            pairs.append((linear(y, xh, z, xl, core), linear(y, xh, z + by, xl, core)))
    return pairs


def list_pairs(by):
    pairs = []
    for y, xh, z, xl, core in devices():
        if 0 <= z % TIME_TILES + by < TIME_TILES:
            pairs.append((linear(y, xh, z, xl, core), linear(y, xl, z + by, core, xh)))
    return pairs


def send(x, pairs):
    return lax.ppermute(x, AXES, pairs)


def split_kernel(at_ref, qkv_ref, *rest):
    outs, sems = rest[:8], rest[8]
    width = outs[0].shape[-1]
    copies = []
    for k in range(4):
        start = pl.multiple_of((at_ref[0] ^ k) * width, 128)
        copies.append(pltpu.make_async_copy(qkv_ref.at[0, :, pl.ds(start, width)], outs[k], sems.at[k]))
        copies.append(
            pltpu.make_async_copy(qkv_ref.at[pl.ds(1, 2), :, pl.ds(start, width)], outs[4 + k], sems.at[4 + k])
        )
    for copy in copies:
        copy.start()
    for copy in copies:
        copy.wait()


def split(at, qkv):
    _, rows, columns = qkv.shape
    width = columns // 4
    hbm = pl.BlockSpec(memory_space=pl.ANY)
    shapes = [jax.ShapeDtypeStruct((rows, width), qkv.dtype)] * 4
    shapes += [jax.ShapeDtypeStruct((2, rows, width), qkv.dtype)] * 4
    return pl.pallas_call(
        split_kernel,
        out_shape=shapes,
        in_specs=[pl.BlockSpec(memory_space=pltpu.SMEM), hbm],
        out_specs=[hbm] * 8,
        scratch_shapes=[pltpu.SemaphoreType.DMA((8,))],
        name="split",
    )(at, qkv)


def join_kernel(at_ref, *rest):
    parts, out_ref, sems = rest[:4], rest[4], rest[5]
    width = parts[0].shape[-1]
    copies = []
    for k in range(4):
        start = pl.multiple_of((at_ref[0] ^ k) * width, 128)
        copies.append(pltpu.make_async_copy(parts[k], out_ref.at[:, pl.ds(start, width)], sems.at[k]))
    for copy in copies:
        copy.start()
    for copy in copies:
        copy.wait()


def join(at, parts):
    rows, width = parts[0].shape
    hbm = pl.BlockSpec(memory_space=pl.ANY)
    return pl.pallas_call(
        join_kernel,
        out_shape=jax.ShapeDtypeStruct((rows, 4 * width), parts[0].dtype),
        in_specs=[pl.BlockSpec(memory_space=pltpu.SMEM)] + [hbm] * 4,
        out_specs=hbm,
        scratch_shapes=[pltpu.SemaphoreType.DMA((4,))],
        name="join",
    )(at, *parts)


def attend_kernel(mask_ref, *refs, sets, heads, tile, dim, sub):
    queries = refs[:sets]
    bodies = refs[sets : sets + 3]
    edges = refs[sets + 3 : sets + 6]
    outs = refs[sets + 6 : 2 * sets + 6]
    lses = refs[2 * sets + 6 : 3 * sets + 6]
    pool, held, max_ref, sum_ref, acc_ref, sems = refs[3 * sets + 6 :]
    copies = []
    for n in range(sets):
        copies.append(pltpu.make_async_copy(queries[n], held.at[n], sems.at[n]))
    for c in range(3):
        copies.append(pltpu.make_async_copy(bodies[c], pool.at[c, :, pl.ds(0, 2 * tile)], sems.at[sets + c]))
        copies.append(pltpu.make_async_copy(edges[c], pool.at[c, :, pl.ds(2 * tile, tile)], sems.at[sets + 3 + c]))
    for copy in copies:
        copy.start()
    for copy in copies:
        copy.wait()
    scale = dim**-0.5
    factor = scale * math.log2(math.e)
    for n in range(sets):
        lses[n][...] = jnp.zeros_like(lses[n])

        def per_head(h, carry, n=n):
            lanes = pl.ds(pl.multiple_of(h * dim, dim), dim)

            def per_tile(p, carry):
                max_ref[...] = jnp.full_like(max_ref, FAR)
                sum_ref[...] = jnp.zeros_like(sum_ref)
                acc_ref[...] = jnp.zeros_like(acc_ref)

                def per_key_tile(j, carry):
                    c = j // 3
                    start = pl.multiple_of((j - 3 * c) * tile, tile)

                    @pl.when(mask_ref[((n * heads + h) * 2 + p) * 9 + j] > 0)
                    def _():
                        keys = pool[c, 0, pl.ds(start, tile), lanes]
                        values = pool[c, 1, pl.ds(start, tile), lanes]
                        for b in range(tile // sub):
                            rows = pl.ds(b * sub, sub)
                            q = held[n, pl.ds(pl.multiple_of(p * tile + b * sub, sub), sub), lanes]
                            scores = lax.dot_general(
                                q, keys, (((1,), (1,)), ((), ())), preferred_element_type=jnp.float32
                            )
                            old = max_ref[rows, :]
                            new = jnp.maximum(old, jnp.max(scores, axis=1, keepdims=True))
                            shrink = jnp.exp2((old - new) * factor)
                            weights = jnp.exp2((scores - new[:, :1]) * factor)
                            total = sum_ref[rows, :] * shrink
                            for i in range(tile // dim):
                                total = total + weights[:, i * dim : (i + 1) * dim]
                            max_ref[rows, :] = new
                            sum_ref[rows, :] = total
                            acc_ref[rows, :] = acc_ref[rows, :] * shrink + lax.dot_general(
                                weights.astype(jnp.bfloat16),
                                values,
                                (((1,), (0,)), ((), ())),
                                preferred_element_type=jnp.float32,
                            )

                    return carry

                lax.fori_loop(0, 9, per_key_tile, 0)
                total = jnp.maximum(jnp.sum(sum_ref[...], axis=1, keepdims=True), 1e-30)
                at = pl.multiple_of(p * tile, tile)
                outs[n][pl.ds(at, tile), lanes] = (acc_ref[...] / total).astype(outs[n].dtype)
                lse = max_ref[...] * scale + jnp.log(total)
                lses[n][pl.ds(h, 1), pl.ds(at, tile)] = jnp.transpose(lse)[:1, :]
                return carry

            return lax.fori_loop(0, 2, per_tile, carry)

        lax.fori_loop(0, heads, per_head, 0)


def attend(mask, queries, bodies, edges, heads, out_dtype):
    sets = len(queries)
    brick, width = queries[0].shape
    tile = brick // 2
    dim = width // heads
    hbm = pl.BlockSpec(memory_space=pl.ANY)
    vmem = pl.BlockSpec(memory_space=pltpu.VMEM)
    outs = pl.pallas_call(
        functools.partial(attend_kernel, sets=sets, heads=heads, tile=tile, dim=dim, sub=tile // 3),
        out_shape=[jax.ShapeDtypeStruct((brick, width), out_dtype)] * sets
        + [jax.ShapeDtypeStruct((8, brick), jnp.float32)] * sets,
        in_specs=[pl.BlockSpec(memory_space=pltpu.SMEM)] + [hbm] * (sets + 6),
        out_specs=[vmem] * (2 * sets),
        scratch_shapes=[
            pltpu.VMEM((3, 2, 3 * tile, width), jnp.bfloat16),
            pltpu.VMEM((sets, brick, width), jnp.bfloat16),
            pltpu.VMEM((tile, dim), jnp.float32),
            pltpu.VMEM((tile, dim), jnp.float32),
            pltpu.VMEM((tile, dim), jnp.float32),
            pltpu.SemaphoreType.DMA((sets + 6,)),
        ],
        compiler_params=pltpu.CompilerParams(vmem_limit_bytes=VMEM_LIMIT),
        name=f"attend{sets}",
    )(mask, *queries, *bodies, *edges)
    return outs[:sets], outs[sets:]


def merge_kernel(valid_ref, own, before, after, own_lse, before_lse, after_lse, *outs, heads):
    brick, width = own.shape
    dim = width // heads
    quarter = brick // 4
    lse = [
        own_lse[...],
        jnp.where(valid_ref[0] > 0, before_lse[...], FAR),
        jnp.where(valid_ref[1] > 0, after_lse[...], FAR),
    ]
    top = jnp.maximum(jnp.maximum(lse[0], lse[1]), lse[2])
    shares = [jnp.exp(x - top) for x in lse]
    total = shares[0] + shares[1] + shares[2]
    shares = [x / total for x in shares]
    spare = jnp.zeros((128 - 24, brick), jnp.float32)
    columns = jnp.transpose(jnp.concatenate(shares + [spare], axis=0))
    for k in range(4):
        rows = slice(k * quarter, (k + 1) * quarter)
        for h in range(heads):
            lanes = slice(h * dim, (h + 1) * dim)
            merged = own[rows, lanes].astype(jnp.float32) * columns[rows, h : h + 1]
            merged += before[rows, lanes].astype(jnp.float32) * columns[rows, 8 + h : 9 + h]
            merged += after[rows, lanes].astype(jnp.float32) * columns[rows, 16 + h : 17 + h]
            outs[k][:, lanes] = merged.astype(outs[k].dtype)


def merge(valid, parts, lses, heads):
    brick, width = parts[0].shape
    vmem = pl.BlockSpec(memory_space=pltpu.VMEM)
    return pl.pallas_call(
        functools.partial(merge_kernel, heads=heads),
        out_shape=[jax.ShapeDtypeStruct((brick // 4, width), jnp.bfloat16)] * 4,
        in_specs=[pl.BlockSpec(memory_space=pltpu.SMEM)] + [vmem] * 6,
        out_specs=[vmem] * 4,
        compiler_params=pltpu.CompilerParams(vmem_limit_bytes=VMEM_LIMIT),
        name="merge",
    )(valid, *parts, *lses)


def named(key_tiles, y, xh, z, xl):
    pair = z // TIME_TILES
    time = z % TIME_TILES
    column = 2 * y + xh
    tile_time = key_tiles // 2 % TIME_TILES
    tile_pair = key_tiles // (2 * TIME_TILES) % 2
    tile_column = key_tiles // (4 * TIME_TILES)
    beside = jnp.where(tile_column == column + 1 - 2 * xh, 1, 2)
    column_slot = jnp.where(tile_column == column, 0, beside)
    row_slot = jnp.where(tile_pair == pair, (key_tiles % 2) ^ xl, 2)
    slot = (tile_time - time + 1) * 9 + column_slot * 3 + row_slot
    slot = jnp.where(key_tiles >= 0, slot, -1)
    mask = jnp.any(slot[..., None] == jnp.arange(27, dtype=jnp.int32), axis=2)
    mask = jnp.where(xl == 1, mask[:, ::-1], mask).astype(jnp.int32)
    return mask[..., 0:9], mask[..., 9:18], mask[..., 18:27]


def local(qkv, key_tiles):
    heads = key_tiles.shape[0]
    seq = lax.axis_index("seq")
    head = lax.axis_index("head")
    y, xh, z = seq // 16, seq // 8 % 2, seq % 8
    xl = head // 2
    pair, time = z // TIME_TILES, z % TIME_TILES
    at = head.astype(jnp.int32).reshape(1)

    early, same, late = named(key_tiles, y, xh, z, xl)
    mask_own = send(same, list_pairs(0))
    mask_next = send(early, list_pairs(-1))
    mask_prev = send(late, list_pairs(1))

    pieces = split(at, qkv)
    q_parts = [send(pieces[k], spread_pairs(k)) for k in range(4)]
    kv_parts = [send(pieces[4 + k], spread_pairs(k)) for k in range(4)]
    edge_parts = [send(pieces[4 + k], edge_pairs(k)) for k in range(4)]

    q_own = jnp.concatenate(q_parts, axis=0)
    q_prev = send(q_own, time_pairs(1))
    q_next = send(q_own, time_pairs(-1))

    kv_own = jnp.concatenate(kv_parts, axis=1)
    kv_core = send(kv_own, core_pairs())
    kv_column = send(kv_own, column_pairs())
    low = (pair ^ xh) == 0
    edge_own = jnp.concatenate(
        [jnp.where(low, edge_parts[0], edge_parts[2]), jnp.where(low, edge_parts[1], edge_parts[3])], axis=1
    )
    edge_core = send(edge_own, core_pairs())
    edge_column = send(edge_own, column_pairs())

    bodies = (kv_own, kv_core, kv_column)
    edges = (edge_own, edge_core, edge_column)
    mask_away = jnp.concatenate([mask_prev.reshape(-1), mask_next.reshape(-1)])
    (o_prev, o_next), (l_prev, l_next) = attend(mask_away, (q_prev, q_next), bodies, edges, heads, jnp.bfloat16)
    o_before = send(o_next, time_pairs(1))
    l_before = send(l_next, time_pairs(1))
    o_after = send(o_prev, time_pairs(-1))
    l_after = send(l_prev, time_pairs(-1))
    (o_own,), (l_own,) = attend(mask_own.reshape(-1), (q_own,), bodies, edges, heads, jnp.float32)

    valid = jnp.stack([time > 0, time < TIME_TILES - 1]).astype(jnp.int32)
    chunks = merge(valid, (o_own, o_before, o_after), (l_own, l_before, l_after), heads)
    home = [send(chunks[k], gather_pairs(k)) for k in range(4)]
    return join(at, home)


def solution(mesh):
    placed = (P(None, ("seq", "head"), None), P("head", "seq", None))
    return jax.shard_map(
        local, mesh=mesh, in_specs=placed, out_specs=P(("seq", "head"), None), check_vma=False
    )
```

```python
import functools
import math

import jax
import jax.numpy as jnp
from jax import lax
from jax.experimental import pallas as pl
from jax.experimental.pallas import tpu as pltpu
from jax.sharding import PartitionSpec as P

TIME_TILES = 4
ROWS_PER_BRICK = 2
AXES = ("seq", "head")
FAR = -1e30
VMEM_LIMIT = 40 * 2**20
BATCH = 2


def linear(y, xh, z, xl, core):
    return ((y * 2 + xh) * 8 + z) * 4 + xl * 2 + core


def devices():
    for y in range(4):
        for xh in range(2):
            for z in range(8):
                for xl in range(2):
                    for core in range(2):
                        yield y, xh, z, xl, core


def spread_pairs(k):
    pairs = []
    for y, xh, z, xl, core in devices():
        group = (2 * xl + core) ^ k
        pairs.append((linear(y, xh, z, xl, core), linear(y, group >> 1, z, group & 1, xh)))
    return pairs


def gather_pairs(k):
    return [(b, a) for a, b in spread_pairs(k)]


def edge_pairs(k):
    pairs = []
    for y, xh, z, xl, core in devices():
        if xl == 1 - z // 4:
            group = (2 * xl + core) ^ k
            pairs.append((linear(y, xh, z, xl, core), linear(y, group >> 1, z ^ 4, group & 1, xh)))
    return pairs


def core_pairs():
    return [(linear(y, xh, z, xl, c), linear(y, xh, z, xl, 1 - c)) for y, xh, z, xl, c in devices()]


def column_pairs():
    pairs = []
    for y, xh, z, xl, core in devices():
        to = y + (1 if core == 1 else -1)
        if 0 <= to < 4:
            pairs.append((linear(y, xh, z, xl, core), linear(to, xh, z, xl, 1 - core)))
    return pairs


def time_pairs(by):
    pairs = []
    for y, xh, z, xl, core in devices():
        if 0 <= z % TIME_TILES + by < TIME_TILES:
            pairs.append((linear(y, xh, z, xl, core), linear(y, xh, z + by, xl, core)))
    return pairs


def list_pairs(by):
    pairs = []
    for y, xh, z, xl, core in devices():
        if 0 <= z % TIME_TILES + by < TIME_TILES:
            pairs.append((linear(y, xh, z, xl, core), linear(y, xl, z + by, core, xh)))
    return pairs


def send(x, pairs):
    return lax.ppermute(x, AXES, pairs)


def split_kernel(at_ref, qkv_ref, *outs):
    width = outs[0].shape[-1]
    for k in range(4):
        lanes = pl.ds(pl.multiple_of((at_ref[0] ^ k) * width, 128), width)
        outs[k][...] = qkv_ref[0, :, lanes]
        outs[4 + k][...] = qkv_ref[1:3, :, lanes]


def split(at, qkv):
    _, rows, columns = qkv.shape
    width = columns // 4
    vmem = pl.BlockSpec(memory_space=pltpu.VMEM)
    shapes = [jax.ShapeDtypeStruct((rows, width), qkv.dtype)] * 4
    shapes += [jax.ShapeDtypeStruct((2, rows, width), qkv.dtype)] * 4
    return pl.pallas_call(
        split_kernel,
        out_shape=shapes,
        in_specs=[pl.BlockSpec(memory_space=pltpu.SMEM), vmem],
        out_specs=[vmem] * 8,
        compiler_params=pltpu.CompilerParams(vmem_limit_bytes=VMEM_LIMIT),
        name="split",
    )(at, qkv)


def join_kernel(at_ref, *refs):
    parts, out_ref = refs[:4], refs[4]
    width = parts[0].shape[-1]
    for k in range(4):
        out_ref[:, pl.ds(pl.multiple_of((at_ref[0] ^ k) * width, 128), width)] = parts[k][...]


def join(at, parts):
    rows, width = parts[0].shape
    vmem = pl.BlockSpec(memory_space=pltpu.VMEM)
    return pl.pallas_call(
        join_kernel,
        out_shape=jax.ShapeDtypeStruct((rows, 4 * width), parts[0].dtype),
        in_specs=[pl.BlockSpec(memory_space=pltpu.SMEM)] + [vmem] * 4,
        out_specs=vmem,
        compiler_params=pltpu.CompilerParams(vmem_limit_bytes=VMEM_LIMIT),
        name="join",
    )(at, *parts)


def attend_kernel(mask_ref, *refs, sets, heads, tile, dim):
    queries = refs[:sets]
    bodies = refs[sets : sets + 3]
    edges = refs[sets + 3 : sets + 6]
    outs = refs[sets + 6 : 2 * sets + 6]
    lses = refs[2 * sets + 6 : 3 * sets + 6]
    pool, held, turned_q, turned_v, max_ref, sum_ref, acc_ref, of_query, of_key = refs[3 * sets + 6 : 3 * sets + 15]
    rest = refs[3 * sets + 15 :]
    score_refs = (rest[:BATCH], rest[BATCH : 2 * BATCH])
    top_refs = (rest[2 * BATCH : 3 * BATCH], rest[3 * BATCH : 4 * BATCH])
    sems = rest[4 * BATCH]
    count_q = sets * heads * 2

    copies = []
    for n in range(sets):
        copies.append(pltpu.make_async_copy(queries[n], held.at[n], sems.at[n]))
    for c in range(3):
        copies.append(pltpu.make_async_copy(bodies[c], pool.at[c, :, pl.ds(0, 2 * tile)], sems.at[sets + c]))
        copies.append(pltpu.make_async_copy(edges[c], pool.at[c, :, pl.ds(2 * tile, tile)], sems.at[sets + 3 + c]))
    for copy in copies:
        copy.start()

    def list_pairs_of(s, count):
        for j in range(9):
            of_query[count] = s
            of_key[count] = j
            count = count + mask_ref[s * 9 + j]
        return count

    count = lax.fori_loop(0, count_q, list_pairs_of, 0)
    for i in range(4 * BATCH):
        of_query[count + i] = count_q
        of_key[count + i] = 0
    max_ref[...] = jnp.full_like(max_ref, FAR)
    sum_ref[...] = jnp.zeros_like(sum_ref)
    acc_ref[...] = jnp.zeros_like(acc_ref)
    for copy in copies:
        copy.wait()
    for n in range(sets):
        for h in range(heads):
            for p in range(2):
                turned_q[(n * heads + h) * 2 + p] = jnp.transpose(
                    held[n, p * tile : (p + 1) * tile, h * dim : (h + 1) * dim]
                )
    turned_q[count_q] = turned_q[0]
    for h in range(heads):
        for j in range(9):
            c, r = divmod(j, 3)
            turned_v[h * 9 + j] = jnp.transpose(pool[c, 1, r * tile : (r + 1) * tile, h * dim : (h + 1) * dim])

    scale = dim**-0.5
    factor = scale * math.log2(math.e)

    def score(i, out_ref, top_ref):
        s, j = of_query[i], of_key[i]
        h = lax.rem(s // 2, heads)
        c = j // 3
        rows = pl.ds(pl.multiple_of((j - 3 * c) * tile, 128), tile)
        keys = pool[c, 0, rows, pl.ds(pl.multiple_of(h * dim, dim), dim)]
        scores = jnp.dot(keys, turned_q[s], preferred_element_type=jnp.float32)
        out_ref[...] = scores
        top_ref[...] = jnp.max(scores.reshape(tile // 8, 8, tile), axis=0)

    def weigh(i, in_ref, top_ref):
        s, j = of_query[i], of_key[i]
        h = lax.rem(s // 2, heads)
        old = max_ref[s, :1, :]
        new = jnp.maximum(old, jnp.max(top_ref[...], axis=0, keepdims=True))
        shrink = jnp.exp2((old - new) * factor)
        max_ref[s, :1, :] = new
        weights = jnp.exp2((in_ref[...] - new) * factor)
        sum_ref[s] = sum_ref[s] * shrink + jnp.sum(weights.reshape(tile // 8, 8, tile), axis=0)
        acc_ref[s] = acc_ref[s] * shrink + jnp.dot(
            turned_v[h * 9 + j], weights.astype(jnp.bfloat16), preferred_element_type=jnp.float32
        )

    for u in range(BATCH):
        score(u, score_refs[0][u], top_refs[0][u])

    def step(t, carry):
        for half in range(2):
            base = (2 * t + half) * BATCH
            for u in range(BATCH):
                score(base + BATCH + u, score_refs[1 - half][u], top_refs[1 - half][u])
            for u in range(BATCH):
                weigh(base + u, score_refs[half][u], top_refs[half][u])
        return carry

    lax.fori_loop(0, (count + 2 * BATCH - 1) // (2 * BATCH), step, 0)

    for n in range(sets):
        lses[n][...] = jnp.zeros_like(lses[n])
        for h in range(heads):
            for p in range(2):
                s = (n * heads + h) * 2 + p
                at = slice(p * tile, (p + 1) * tile)
                total = jnp.maximum(jnp.sum(sum_ref[s], axis=0, keepdims=True), 1e-30)
                outs[n][h * dim : (h + 1) * dim, at] = (acc_ref[s] / total).astype(outs[n].dtype)
                lses[n][h : h + 1, at] = max_ref[s, :1, :] * scale + jnp.log(total)


def attend(mask, queries, bodies, edges, heads, out_dtype):
    sets = len(queries)
    brick, width = queries[0].shape
    tile = brick // 2
    dim = width // heads
    count_q = sets * heads * 2
    hbm = pl.BlockSpec(memory_space=pl.ANY)
    vmem = pl.BlockSpec(memory_space=pltpu.VMEM)
    outs = pl.pallas_call(
        functools.partial(attend_kernel, sets=sets, heads=heads, tile=tile, dim=dim),
        out_shape=[jax.ShapeDtypeStruct((width, brick), out_dtype)] * sets
        + [jax.ShapeDtypeStruct((8, brick), jnp.float32)] * sets,
        in_specs=[pl.BlockSpec(memory_space=pltpu.SMEM)] + [hbm] * (sets + 6),
        out_specs=[vmem] * (2 * sets),
        scratch_shapes=[
            pltpu.VMEM((3, 2, 3 * tile, width), jnp.bfloat16),
            pltpu.VMEM((sets, brick, width), jnp.bfloat16),
            pltpu.VMEM((count_q + 1, dim, tile), jnp.bfloat16),
            pltpu.VMEM((9 * heads, dim, tile), jnp.bfloat16),
            pltpu.VMEM((count_q + 1, 8, tile), jnp.float32),
            pltpu.VMEM((count_q + 1, 8, tile), jnp.float32),
            pltpu.VMEM((count_q + 1, dim, tile), jnp.float32),
            pltpu.SMEM((count_q * 9 + 8 * BATCH,), jnp.int32),
            pltpu.SMEM((count_q * 9 + 8 * BATCH,), jnp.int32),
        ]
        + [pltpu.VMEM((tile, tile), jnp.float32)] * (2 * BATCH)
        + [pltpu.VMEM((8, tile), jnp.float32)] * (2 * BATCH)
        + [pltpu.SemaphoreType.DMA((sets + 6,))],
        compiler_params=pltpu.CompilerParams(vmem_limit_bytes=VMEM_LIMIT),
        name=f"attend{sets}",
    )(mask, *queries, *bodies, *edges)
    return outs[:sets], outs[sets:]


def merge_kernel(valid_ref, own, before, after, own_lse, before_lse, after_lse, *outs, heads):
    width, brick = own.shape
    dim = width // heads
    quarter = brick // 4
    lse = [
        own_lse[...],
        jnp.where(valid_ref[0] > 0, before_lse[...], FAR),
        jnp.where(valid_ref[1] > 0, after_lse[...], FAR),
    ]
    top = jnp.maximum(jnp.maximum(lse[0], lse[1]), lse[2])
    shares = [jnp.exp(x - top) for x in lse]
    total = shares[0] + shares[1] + shares[2]
    shares = [x / total for x in shares]
    for h in range(heads):
        lanes = slice(h * dim, (h + 1) * dim)
        merged = own[lanes, :].astype(jnp.float32) * shares[0][h : h + 1, :]
        merged += before[lanes, :].astype(jnp.float32) * shares[1][h : h + 1, :]
        merged += after[lanes, :].astype(jnp.float32) * shares[2][h : h + 1, :]
        merged = jnp.transpose(merged).astype(jnp.bfloat16)
        for k in range(4):
            outs[k][:, lanes] = merged[k * quarter : (k + 1) * quarter, :]


def merge(valid, parts, lses, heads):
    width, brick = parts[0].shape
    vmem = pl.BlockSpec(memory_space=pltpu.VMEM)
    return pl.pallas_call(
        functools.partial(merge_kernel, heads=heads),
        out_shape=[jax.ShapeDtypeStruct((brick // 4, width), jnp.bfloat16)] * 4,
        in_specs=[pl.BlockSpec(memory_space=pltpu.SMEM)] + [vmem] * 6,
        out_specs=[vmem] * 4,
        compiler_params=pltpu.CompilerParams(vmem_limit_bytes=VMEM_LIMIT),
        name="merge",
    )(valid, *parts, *lses)


def named(key_tiles, y, xh, z, xl):
    pair = z // TIME_TILES
    time = z % TIME_TILES
    column = 2 * y + xh
    tile_time = key_tiles // 2 % TIME_TILES
    tile_pair = key_tiles // (2 * TIME_TILES) % 2
    tile_column = key_tiles // (4 * TIME_TILES)
    beside = jnp.where(tile_column == column + 1 - 2 * xh, 1, 2)
    column_slot = jnp.where(tile_column == column, 0, beside)
    row_slot = jnp.where(tile_pair == pair, (key_tiles % 2) ^ xl, 2)
    slot = (tile_time - time + 1) * 9 + column_slot * 3 + row_slot
    slot = jnp.where(key_tiles >= 0, slot, -1)
    mask = jnp.any(slot[..., None] == jnp.arange(27, dtype=jnp.int32), axis=2)
    mask = jnp.where(xl == 1, mask[:, ::-1], mask).astype(jnp.int32)
    return mask[..., 0:9], mask[..., 9:18], mask[..., 18:27]


def local(qkv, key_tiles):
    heads = key_tiles.shape[0]
    seq = lax.axis_index("seq")
    head = lax.axis_index("head")
    y, xh, z = seq // 16, seq // 8 % 2, seq % 8
    xl = head // 2
    pair, time = z // TIME_TILES, z % TIME_TILES
    at = head.astype(jnp.int32).reshape(1)

    early, same, late = named(key_tiles, y, xh, z, xl)
    mask_own = send(same, list_pairs(0))
    mask_next = send(early, list_pairs(-1))
    mask_prev = send(late, list_pairs(1))

    pieces = split(at, qkv)
    q_parts = [send(pieces[k], spread_pairs(k)) for k in range(4)]
    kv_parts = [send(pieces[4 + k], spread_pairs(k)) for k in range(4)]
    edge_parts = [send(pieces[4 + k], edge_pairs(k)) for k in range(4)]

    q_own = jnp.concatenate(q_parts, axis=0)
    q_prev = send(q_own, time_pairs(1))
    q_next = send(q_own, time_pairs(-1))

    kv_own = jnp.concatenate(kv_parts, axis=1)
    kv_core = send(kv_own, core_pairs())
    kv_column = send(kv_own, column_pairs())
    low = (pair ^ xh) == 0
    edge_own = jnp.concatenate(
        [jnp.where(low, edge_parts[0], edge_parts[2]), jnp.where(low, edge_parts[1], edge_parts[3])], axis=1
    )
    edge_core = send(edge_own, core_pairs())
    edge_column = send(edge_own, column_pairs())

    bodies = (kv_own, kv_core, kv_column)
    edges = (edge_own, edge_core, edge_column)
    mask_away = jnp.concatenate([mask_prev.reshape(-1), mask_next.reshape(-1)])
    (o_prev, o_next), (l_prev, l_next) = attend(mask_away, (q_prev, q_next), bodies, edges, heads, jnp.bfloat16)
    o_before = send(o_next, time_pairs(1))
    l_before = send(l_next, time_pairs(1))
    o_after = send(o_prev, time_pairs(-1))
    l_after = send(l_prev, time_pairs(-1))
    (o_own,), (l_own,) = attend(mask_own.reshape(-1), (q_own,), bodies, edges, heads, jnp.float32)

    valid = jnp.stack([time > 0, time < TIME_TILES - 1]).astype(jnp.int32)
    chunks = merge(valid, (o_own, o_before, o_after), (l_own, l_before, l_after), heads)
    home = [send(chunks[k], gather_pairs(k)) for k in range(4)]
    return join(at, home)


def solution(mesh):
    placed = (P(None, ("seq", "head"), None), P("head", "seq", None))
    return jax.shard_map(
        local, mesh=mesh, in_specs=placed, out_specs=P(("seq", "head"), None), check_vma=False
    )
```

```python
import functools
import math

import jax
import jax.numpy as jnp
from jax import lax
from jax.experimental import pallas as pl
from jax.experimental.pallas import tpu as pltpu
from jax.sharding import PartitionSpec as P

TIME_TILES = 4
AXES = ("seq", "head")
FAR = -1e30
VMEM_LIMIT = 40 * 2**20
BATCH = 2
EXTRA = 16


def linear(y, xh, z, xl, core):
    return ((y * 2 + xh) * 8 + z) * 4 + xl * 2 + core


def devices():
    for y in range(4):
        for xh in range(2):
            for z in range(8):
                for xl in range(2):
                    for core in range(2):
                        yield y, xh, z, xl, core


def spread_pairs(k):
    pairs = []
    for y, xh, z, xl, core in devices():
        group = (2 * xl + core) ^ k
        pairs.append((linear(y, xh, z, xl, core), linear(y, group >> 1, z, group & 1, xh)))
    return pairs


def gather_pairs(k):
    return [(b, a) for a, b in spread_pairs(k)]


def edge_pairs(k):
    pairs = []
    for y, xh, z, xl, core in devices():
        if xl == 1 - z // 4:
            group = (2 * xl + core) ^ k
            pairs.append((linear(y, xh, z, xl, core), linear(y, group >> 1, z ^ 4, group & 1, xh)))
    return pairs


def core_pairs():
    return [(linear(y, xh, z, xl, c), linear(y, xh, z, xl, 1 - c)) for y, xh, z, xl, c in devices()]


def column_pairs():
    pairs = []
    for y, xh, z, xl, core in devices():
        to = y + (1 if core == 1 else -1)
        if 0 <= to < 4:
            pairs.append((linear(y, xh, z, xl, core), linear(to, xh, z, xl, 1 - core)))
    return pairs


def time_pairs(by):
    pairs = []
    for y, xh, z, xl, core in devices():
        if 0 <= z % TIME_TILES + by < TIME_TILES:
            pairs.append((linear(y, xh, z, xl, core), linear(y, xh, z + by, xl, core)))
    return pairs


def list_pairs(by):
    pairs = []
    for y, xh, z, xl, core in devices():
        if 0 <= z % TIME_TILES + by < TIME_TILES:
            pairs.append((linear(y, xh, z, xl, core), linear(y, xl, z + by, core, xh)))
    return pairs


def send(x, pairs):
    return lax.ppermute(x, AXES, pairs)


def split_kernel(at_ref, qkv_ref, *outs):
    width = outs[0].shape[-1]
    for k in range(4):
        lanes = pl.ds(pl.multiple_of((at_ref[0] ^ k) * width, 128), width)
        outs[k][...] = qkv_ref[:, :, lanes]
        outs[4 + k][...] = qkv_ref[1:3, :, lanes]


def split(at, qkv):
    _, rows, columns = qkv.shape
    width = columns // 4
    vmem = pl.BlockSpec(memory_space=pltpu.VMEM)
    shapes = [jax.ShapeDtypeStruct((3, rows, width), qkv.dtype)] * 4
    shapes += [jax.ShapeDtypeStruct((2, rows, width), qkv.dtype)] * 4
    return pl.pallas_call(
        split_kernel,
        out_shape=shapes,
        in_specs=[pl.BlockSpec(memory_space=pltpu.SMEM), vmem],
        out_specs=[vmem] * 8,
        compiler_params=pltpu.CompilerParams(vmem_limit_bytes=VMEM_LIMIT),
        name="split",
    )(at, qkv)


def stack_kernel(*refs):
    parts, q_ref, kv_ref, sems = refs[:4], refs[4], refs[5], refs[6]
    rows = parts[0].shape[1]
    copies = []
    for k in range(4):
        at = pl.ds(k * rows, rows)
        copies.append(pltpu.make_async_copy(parts[k].at[0], q_ref.at[at], sems.at[k]))
        copies.append(pltpu.make_async_copy(parts[k].at[pl.ds(1, 2)], kv_ref.at[:, at], sems.at[4 + k]))
    for copy in copies:
        copy.start()
    for copy in copies:
        copy.wait()


def stack(parts):
    _, rows, width = parts[0].shape
    vmem = pl.BlockSpec(memory_space=pltpu.VMEM)
    return pl.pallas_call(
        stack_kernel,
        out_shape=[
            jax.ShapeDtypeStruct((4 * rows, width), parts[0].dtype),
            jax.ShapeDtypeStruct((2, 4 * rows, width), parts[0].dtype),
        ],
        in_specs=[pl.BlockSpec(memory_space=pl.ANY)] * 4,
        out_specs=[vmem] * 2,
        scratch_shapes=[pltpu.SemaphoreType.DMA((8,))],
        compiler_params=pltpu.CompilerParams(vmem_limit_bytes=VMEM_LIMIT),
        name="stack",
    )(*parts)


def choose_kernel(high_ref, *refs):
    parts, out_ref, sems = refs[:4], refs[4], refs[5]
    rows = parts[0].shape[1]
    for half in range(2):

        @pl.when(high_ref[0] == half)
        def _():
            copies = []
            for b in range(2):
                into = out_ref.at[:, pl.ds(b * rows, rows)]
                copies.append(pltpu.make_async_copy(parts[2 * half + b], into, sems.at[2 * half + b]))
            for copy in copies:
                copy.start()
            for copy in copies:
                copy.wait()


def choose(high, parts):
    _, rows, width = parts[0].shape
    vmem = pl.BlockSpec(memory_space=pltpu.VMEM)
    return pl.pallas_call(
        choose_kernel,
        out_shape=jax.ShapeDtypeStruct((2, 2 * rows, width), parts[0].dtype),
        in_specs=[pl.BlockSpec(memory_space=pltpu.SMEM)] + [pl.BlockSpec(memory_space=pl.ANY)] * 4,
        out_specs=vmem,
        scratch_shapes=[pltpu.SemaphoreType.DMA((4,))],
        compiler_params=pltpu.CompilerParams(vmem_limit_bytes=VMEM_LIMIT),
        name="choose",
    )(high, *parts)


def join_kernel(at_ref, *refs):
    parts, out_ref = refs[:4], refs[4]
    width = parts[0].shape[-1]
    for k in range(4):
        out_ref[:, pl.ds(pl.multiple_of((at_ref[0] ^ k) * width, 128), width)] = parts[k][...]


def join(at, parts):
    rows, width = parts[0].shape
    vmem = pl.BlockSpec(memory_space=pltpu.VMEM)
    return pl.pallas_call(
        join_kernel,
        out_shape=jax.ShapeDtypeStruct((rows, 4 * width), parts[0].dtype),
        in_specs=[pl.BlockSpec(memory_space=pltpu.SMEM)] + [vmem] * 4,
        out_specs=vmem,
        compiler_params=pltpu.CompilerParams(vmem_limit_bytes=VMEM_LIMIT),
        name="join",
    )(at, *parts)


def attend_kernel(mask_ref, *refs, sets, heads, tile, dim):
    queries = refs[:sets]
    bodies = refs[sets : sets + 3]
    edges = refs[sets + 3 : sets + 6]
    outs = refs[sets + 6 : 2 * sets + 6]
    pool, held, turned_q, turned_v, max_ref, sum_ref, acc_ref, of_query, of_key = refs[2 * sets + 6 : 2 * sets + 15]
    rest = refs[2 * sets + 15 :]
    score_refs = (rest[:BATCH], rest[BATCH : 2 * BATCH])
    top_refs = (rest[2 * BATCH : 3 * BATCH], rest[3 * BATCH : 4 * BATCH])
    sems = rest[4 * BATCH]
    count_q = sets * heads * 2

    copies = []
    for n in range(sets):
        copies.append(pltpu.make_async_copy(queries[n], held.at[n], sems.at[n]))
    for c in range(3):
        copies.append(pltpu.make_async_copy(bodies[c], pool.at[c, :, pl.ds(0, 2 * tile)], sems.at[sets + c]))
        copies.append(pltpu.make_async_copy(edges[c], pool.at[c, :, pl.ds(2 * tile, tile)], sems.at[sets + 3 + c]))
    for copy in copies:
        copy.start()

    def list_pairs_of(s, count):
        for j in range(9):
            of_query[count] = s
            of_key[count] = j
            count = count + mask_ref[s * 9 + j]
        return count

    count = lax.fori_loop(0, count_q, list_pairs_of, 0)
    for i in range(4 * BATCH):
        of_query[count + i] = count_q
        of_key[count + i] = 0
    max_ref[...] = jnp.full_like(max_ref, FAR)
    sum_ref[...] = jnp.zeros_like(sum_ref)
    acc_ref[...] = jnp.zeros_like(acc_ref)
    for copy in copies:
        copy.wait()
    for n in range(sets):
        for h in range(heads):
            for p in range(2):
                turned_q[(n * heads + h) * 2 + p] = jnp.transpose(
                    held[n, p * tile : (p + 1) * tile, h * dim : (h + 1) * dim]
                )
    turned_q[count_q] = turned_q[0]
    for h in range(heads):
        for j in range(9):
            c, r = divmod(j, 3)
            turned_v[h * 9 + j] = jnp.transpose(pool[c, 1, r * tile : (r + 1) * tile, h * dim : (h + 1) * dim])

    scale = dim**-0.5
    factor = scale * math.log2(math.e)

    def score(i, out_ref, top_ref):
        s, j = of_query[i], of_key[i]
        h = lax.rem(s // 2, heads)
        c = j // 3
        rows = pl.ds(pl.multiple_of((j - 3 * c) * tile, 128), tile)
        keys = pool[c, 0, rows, pl.ds(pl.multiple_of(h * dim, dim), dim)]
        scores = jnp.dot(keys, turned_q[s], preferred_element_type=jnp.float32)
        out_ref[...] = scores
        top_ref[...] = jnp.max(scores.reshape(tile // 8, 8, tile), axis=0)

    def weigh(i, in_ref, top_ref):
        s, j = of_query[i], of_key[i]
        h = lax.rem(s // 2, heads)
        old = max_ref[s, :1, :]
        new = jnp.maximum(old, jnp.max(top_ref[...], axis=0, keepdims=True))
        shrink = jnp.exp2((old - new) * factor)
        max_ref[s, :1, :] = new
        weights = jnp.exp2((in_ref[...] - new) * factor)
        sum_ref[s] = sum_ref[s] * shrink + jnp.sum(weights.reshape(tile // 8, 8, tile), axis=0)
        acc_ref[s] = acc_ref[s] * shrink + jnp.dot(
            turned_v[h * 9 + j], weights.astype(jnp.bfloat16), preferred_element_type=jnp.float32
        )

    for u in range(BATCH):
        score(u, score_refs[0][u], top_refs[0][u])

    def step(t, carry):
        for half in range(2):
            base = (2 * t + half) * BATCH
            for u in range(BATCH):
                score(base + BATCH + u, score_refs[1 - half][u], top_refs[1 - half][u])
            for u in range(BATCH):
                weigh(base + u, score_refs[half][u], top_refs[half][u])
        return carry

    lax.fori_loop(0, (count + 2 * BATCH - 1) // (2 * BATCH), step, 0)

    width = heads * dim
    for n in range(sets):
        outs[n][width : width + EXTRA, :] = jnp.zeros((EXTRA, 2 * tile), outs[n].dtype)
        for h in range(heads):
            for p in range(2):
                s = (n * heads + h) * 2 + p
                at = slice(p * tile, (p + 1) * tile)
                total = jnp.maximum(jnp.sum(sum_ref[s], axis=0, keepdims=True), 1e-30)
                outs[n][h * dim : (h + 1) * dim, at] = (acc_ref[s] / total).astype(outs[n].dtype)
                left = max_ref[s, :1, :] * scale + jnp.log(total)
                for i in range(3):
                    part = left.astype(outs[n].dtype)
                    outs[n][width + 3 * h + i : width + 3 * h + i + 1, at] = part
                    left = left - part.astype(jnp.float32)


def attend(mask, queries, bodies, edges, heads, out_dtype):
    sets = len(queries)
    brick, width = queries[0].shape
    tile = brick // 2
    dim = width // heads
    count_q = sets * heads * 2
    hbm = pl.BlockSpec(memory_space=pl.ANY)
    vmem = pl.BlockSpec(memory_space=pltpu.VMEM)
    return pl.pallas_call(
        functools.partial(attend_kernel, sets=sets, heads=heads, tile=tile, dim=dim),
        out_shape=[jax.ShapeDtypeStruct((width + EXTRA, brick), out_dtype)] * sets,
        in_specs=[pl.BlockSpec(memory_space=pltpu.SMEM)] + [hbm] * (sets + 6),
        out_specs=[vmem] * sets,
        scratch_shapes=[
            pltpu.VMEM((3, 2, 3 * tile, width), jnp.bfloat16),
            pltpu.VMEM((sets, brick, width), jnp.bfloat16),
            pltpu.VMEM((count_q + 1, dim, tile), jnp.bfloat16),
            pltpu.VMEM((9 * heads, dim, tile), jnp.bfloat16),
            pltpu.VMEM((count_q + 1, 8, tile), jnp.float32),
            pltpu.VMEM((count_q + 1, 8, tile), jnp.float32),
            pltpu.VMEM((count_q + 1, dim, tile), jnp.float32),
            pltpu.SMEM((count_q * 9 + 8 * BATCH,), jnp.int32),
            pltpu.SMEM((count_q * 9 + 8 * BATCH,), jnp.int32),
        ]
        + [pltpu.VMEM((tile, tile), jnp.float32)] * (2 * BATCH)
        + [pltpu.VMEM((8, tile), jnp.float32)] * (2 * BATCH)
        + [pltpu.SemaphoreType.DMA((sets + 6,))],
        compiler_params=pltpu.CompilerParams(vmem_limit_bytes=VMEM_LIMIT),
        name=f"attend{sets}",
    )(mask, *queries, *bodies, *edges)


def merge_kernel(valid_ref, *refs, heads):
    parts, outs = refs[:3], refs[3:]
    width, brick = parts[0].shape[0] - EXTRA, parts[0].shape[1]
    dim = width // heads
    quarter = brick // 4
    for h in range(heads):
        lse = []
        for i in range(3):
            rows = parts[i][width : width + EXTRA, :].astype(jnp.float32)
            lse.append(rows[3 * h : 3 * h + 1] + rows[3 * h + 1 : 3 * h + 2] + rows[3 * h + 2 : 3 * h + 3])
        lse[1] = jnp.where(valid_ref[0] > 0, lse[1], FAR)
        lse[2] = jnp.where(valid_ref[1] > 0, lse[2], FAR)
        top = jnp.maximum(jnp.maximum(lse[0], lse[1]), lse[2])
        shares = [jnp.exp(x - top) for x in lse]
        total = shares[0] + shares[1] + shares[2]
        lanes = slice(h * dim, (h + 1) * dim)
        merged = parts[0][lanes, :].astype(jnp.float32) * (shares[0] / total)
        merged += parts[1][lanes, :].astype(jnp.float32) * (shares[1] / total)
        merged += parts[2][lanes, :].astype(jnp.float32) * (shares[2] / total)
        merged = jnp.transpose(merged).astype(jnp.bfloat16)
        for k in range(4):
            outs[k][:, lanes] = merged[k * quarter : (k + 1) * quarter, :]


def merge(valid, parts, heads):
    width, brick = parts[0].shape[0] - EXTRA, parts[0].shape[1]
    vmem = pl.BlockSpec(memory_space=pltpu.VMEM)
    return pl.pallas_call(
        functools.partial(merge_kernel, heads=heads),
        out_shape=[jax.ShapeDtypeStruct((brick // 4, width), jnp.bfloat16)] * 4,
        in_specs=[pl.BlockSpec(memory_space=pltpu.SMEM)] + [vmem] * 3,
        out_specs=[vmem] * 4,
        compiler_params=pltpu.CompilerParams(vmem_limit_bytes=VMEM_LIMIT),
        name="merge",
    )(valid, *parts)


def named(lists, column, pair, time, xh):
    tile_time = lists // 2 % TIME_TILES
    tile_pair = lists // (2 * TIME_TILES) % 2
    tile_column = lists // (4 * TIME_TILES)
    beside = jnp.where(tile_column == column + 1 - 2 * (column % 2), 1, 2)
    column_slot = jnp.where(tile_column == column, 0, beside)
    row_slot = jnp.where(tile_pair == pair, (lists % 2) ^ xh, 2)
    slot = jnp.where((lists >= 0) & (tile_time == time), column_slot * 3 + row_slot, -1)
    mask = jnp.any(slot[..., None] == jnp.arange(9, dtype=jnp.int32), axis=-2)
    return jnp.where(xh == 1, mask[..., ::-1, :], mask)


def local(qkv, key_tiles):
    heads = key_tiles.shape[0]
    seq = lax.axis_index("seq")
    head = lax.axis_index("head")
    y, xh, z = seq // 16, seq // 8 % 2, seq % 8
    core = head % 2
    pair, time = z // TIME_TILES, z % TIME_TILES
    at = head.astype(jnp.int32).reshape(1)
    high = (pair ^ xh).astype(jnp.int32).reshape(1)
    valid = jnp.stack([time > 0, time < TIME_TILES - 1])

    lists = [send(key_tiles, list_pairs(by)) for by in (0, 1, -1)]
    lists, qkv = lax.optimization_barrier((lists, qkv))
    lists = jnp.stack(lists)
    mask = named(lists, 2 * y + core, pair, time, xh)
    here = jnp.concatenate([jnp.ones((1,), bool), valid])
    mask = (mask & here[:, None, None, None]).astype(jnp.int32)
    mask_own, mask_away = mask[0].reshape(-1), mask[1:].reshape(-1)

    pieces = split(at, qkv)
    parts = [send(pieces[k], spread_pairs(k)) for k in range(4)]
    edge_parts = [send(pieces[4 + k], edge_pairs(k)) for k in range(4)]

    q_own, kv_own = stack(parts)
    q_prev = send(q_own, time_pairs(1))
    q_next = send(q_own, time_pairs(-1))
    kv_core = send(kv_own, core_pairs())
    kv_column = send(kv_own, column_pairs())
    edge_own = choose(high, edge_parts)
    edge_core = send(edge_own, core_pairs())
    edge_column = send(edge_own, column_pairs())

    bodies = (kv_own, kv_core, kv_column)
    edges = (edge_own, edge_core, edge_column)
    o_prev, o_next = attend(mask_away, (q_prev, q_next), bodies, edges, heads, jnp.bfloat16)
    o_before = send(o_next, time_pairs(1))
    o_after = send(o_prev, time_pairs(-1))
    (o_own,) = attend(mask_own, (q_own,), bodies, edges, heads, jnp.float32)

    chunks = merge(valid.astype(jnp.int32), (o_own, o_before, o_after), heads)
    home = [send(chunks[k], gather_pairs(k)) for k in range(4)]
    return join(at, home)


def solution(mesh):
    placed = (P(None, ("seq", "head"), None), P("head", "seq", None))
    return jax.shard_map(
        local, mesh=mesh, in_specs=placed, out_specs=P(("seq", "head"), None), check_vma=False
    )
```

```python
import functools
import math

import jax
import jax.numpy as jnp
from jax import lax
from jax.experimental import pallas as pl
from jax.experimental.pallas import tpu as pltpu
from jax.sharding import PartitionSpec as P

TIME_TILES = 4
AXES = ("seq", "head")
FAR = -1e30
VMEM_LIMIT = 40 * 2**20
BATCH = 2
EXTRA = 16
POOL = 9


def linear(y, xh, z, xl, core):
    return ((y * 2 + xh) * 8 + z) * 4 + xl * 2 + core


def devices():
    for y in range(4):
        for xh in range(2):
            for z in range(8):
                for xl in range(2):
                    for core in range(2):
                        yield y, xh, z, xl, core


def spread_pairs(k):
    pairs = []
    for y, xh, z, xl, core in devices():
        group = (2 * xl + core) ^ k
        pairs.append((linear(y, xh, z, xl, core), linear(y, group >> 1, z, group & 1, xh)))
    return pairs


def gather_pairs(k):
    return [(b, a) for a, b in spread_pairs(k)]


def edge_pairs():
    return [(linear(y, xh, z, xl, c), linear(y, xh, z ^ 4, xl, c)) for y, xh, z, xl, c in devices()]


def core_pairs():
    return [(linear(y, xh, z, xl, c), linear(y, xh, z, xl, 1 - c)) for y, xh, z, xl, c in devices()]


def column_pairs():
    pairs = []
    for y, xh, z, xl, core in devices():
        to = y + (1 if core == 1 else -1)
        if 0 <= to < 4:
            pairs.append((linear(y, xh, z, xl, core), linear(to, xh, z, xl, 1 - core)))
    return pairs


def time_pairs(by):
    pairs = []
    for y, xh, z, xl, core in devices():
        if 0 <= z % TIME_TILES + by < TIME_TILES:
            pairs.append((linear(y, xh, z, xl, core), linear(y, xh, z + by, xl, core)))
    return pairs


def list_pairs(by):
    pairs = []
    for y, xh, z, xl, core in devices():
        if 0 <= z % TIME_TILES + by < TIME_TILES:
            pairs.append((linear(y, xh, z, xl, core), linear(y, xl, z + by, core, xh)))
    return pairs


def send(x, pairs):
    return lax.ppermute(x, AXES, pairs)


def split_kernel(at_ref, qkv_ref, *refs):
    outs, sems = refs[:8], refs[8]
    width = outs[0].shape[-1]
    copies = []
    for k in range(4):
        lanes = pl.ds(pl.multiple_of((at_ref[0] ^ k) * width, 128), width)
        copies.append(pltpu.make_async_copy(qkv_ref.at[0, :, lanes], outs[k], sems.at[k]))
    for copy in copies:
        copy.start()
    for k in range(4):
        lanes = pl.ds(pl.multiple_of((at_ref[0] ^ k) * width, 128), width)
        outs[4 + k][...] = qkv_ref[1:3, :, lanes]
    for copy in copies:
        copy.wait()


def split(at, qkv):
    _, rows, columns = qkv.shape
    width = columns // 4
    vmem = pl.BlockSpec(memory_space=pltpu.VMEM)
    shapes = [jax.ShapeDtypeStruct((rows, width), qkv.dtype)] * 4
    shapes += [jax.ShapeDtypeStruct((2, rows, width), qkv.dtype)] * 4
    return pl.pallas_call(
        split_kernel,
        out_shape=shapes,
        in_specs=[pl.BlockSpec(memory_space=pltpu.SMEM), vmem],
        out_specs=[pl.BlockSpec(memory_space=pl.ANY)] * 4 + [vmem] * 4,
        scratch_shapes=[pltpu.SemaphoreType.DMA((4,))],
        compiler_params=pltpu.CompilerParams(vmem_limit_bytes=VMEM_LIMIT),
        name="split",
    )(at, qkv)


def stack_kernel(place_ref, *refs):
    parts, kv_ref, edge_ref, sems = refs[:4], refs[4], refs[5], refs[6]
    rows = parts[0].shape[1]
    copies = []
    for k in range(4):
        copies.append(pltpu.make_async_copy(parts[k], kv_ref.at[:, pl.ds(k * rows, rows)], sems.at[k]))
    for copy in copies:
        copy.start()
    for copy in copies:
        copy.wait()
    edge_ref[...] = kv_ref[:, pl.ds(pl.multiple_of(place_ref[0] * (2 * rows), 128), 2 * rows), :]


def stack(place, parts):
    _, rows, width = parts[0].shape
    vmem = pl.BlockSpec(memory_space=pltpu.VMEM)
    return pl.pallas_call(
        stack_kernel,
        out_shape=[
            jax.ShapeDtypeStruct((2, 4 * rows, width), parts[0].dtype),
            jax.ShapeDtypeStruct((2, 2 * rows, width), parts[0].dtype),
        ],
        in_specs=[pl.BlockSpec(memory_space=pltpu.SMEM)] + [pl.BlockSpec(memory_space=pl.ANY)] * 4,
        out_specs=[vmem] * 2,
        scratch_shapes=[pltpu.SemaphoreType.DMA((4,))],
        compiler_params=pltpu.CompilerParams(vmem_limit_bytes=VMEM_LIMIT),
        name="stack",
    )(place, *parts)


def stack_queries_kernel(*refs):
    parts, q_ref, sems = refs[:4], refs[4], refs[5]
    rows = parts[0].shape[0]
    copies = []
    for k in range(4):
        copies.append(pltpu.make_async_copy(parts[k], q_ref.at[pl.ds(k * rows, rows)], sems.at[k]))
    for copy in copies:
        copy.start()
    for copy in copies:
        copy.wait()


def stack_queries(parts):
    rows, width = parts[0].shape
    return pl.pallas_call(
        stack_queries_kernel,
        out_shape=jax.ShapeDtypeStruct((4 * rows, width), parts[0].dtype),
        in_specs=[pl.BlockSpec(memory_space=pl.ANY)] * 4,
        out_specs=pl.BlockSpec(memory_space=pltpu.VMEM),
        scratch_shapes=[pltpu.SemaphoreType.DMA((4,))],
        compiler_params=pltpu.CompilerParams(vmem_limit_bytes=VMEM_LIMIT),
        name="stack_queries",
    )(*parts)


def join_kernel(at_ref, *refs):
    parts, out_ref = refs[:4], refs[4]
    width = parts[0].shape[-1]
    for k in range(4):
        out_ref[:, pl.ds(pl.multiple_of((at_ref[0] ^ k) * width, 128), width)] = parts[k][...]


def join(at, parts):
    rows, width = parts[0].shape
    vmem = pl.BlockSpec(memory_space=pltpu.VMEM)
    return pl.pallas_call(
        join_kernel,
        out_shape=jax.ShapeDtypeStruct((rows, 4 * width), parts[0].dtype),
        in_specs=[pl.BlockSpec(memory_space=pltpu.SMEM)] + [vmem] * 4,
        out_specs=vmem,
        compiler_params=pltpu.CompilerParams(vmem_limit_bytes=VMEM_LIMIT),
        name="join",
    )(at, *parts)


def attend_kernel(mask_ref, *refs, sets, tiles, first_set, first_tile, heads, tile, dim):
    pieces = 3 if tiles != POOL else 6
    queries = refs[:sets]
    sources = refs[sets : sets + pieces]
    refs = refs[sets + pieces :]
    outs = refs[:sets]
    pool, held, turned_q, turned_v, max_ref, sum_ref, acc_ref, of_query, of_key = refs[sets : sets + 9]
    rest = refs[sets + 9 :]
    score_refs = (rest[:BATCH], rest[BATCH : 2 * BATCH])
    top_refs = (rest[2 * BATCH : 3 * BATCH], rest[3 * BATCH : 4 * BATCH])
    sems = rest[4 * BATCH]
    count_q = sets * heads * 2

    copies = []
    for n in range(sets):
        copies.append(pltpu.make_async_copy(queries[n], held.at[n], sems.at[n]))
    at = 0
    for source in sources:
        for r in range(source.shape[1] // tile):
            copies.append(
                pltpu.make_async_copy(source.at[:, pl.ds(r * tile, tile)], pool.at[at], sems.at[sets + at])
            )
            at += 1
    for copy in copies:
        copy.start()

    def list_pairs_of(s, count):
        for j in range(tiles):
            of_query[count] = s
            of_key[count] = j
            count = count + mask_ref[(first_set * heads * 2 + s) * POOL + first_tile + j]
        return count

    count = lax.fori_loop(0, count_q, list_pairs_of, 0)
    for i in range(4 * BATCH):
        of_query[count + i] = count_q
        of_key[count + i] = 0
    max_ref[...] = jnp.full_like(max_ref, FAR)
    sum_ref[...] = jnp.zeros_like(sum_ref)
    acc_ref[...] = jnp.zeros_like(acc_ref)
    for copy in copies:
        copy.wait()
    for n in range(sets):
        for h in range(heads):
            for p in range(2):
                turned_q[(n * heads + h) * 2 + p] = jnp.transpose(
                    held[n, p * tile : (p + 1) * tile, h * dim : (h + 1) * dim]
                )
    turned_q[count_q] = turned_q[0]
    for h in range(heads):
        for j in range(tiles):
            turned_v[h * tiles + j] = jnp.transpose(pool[j, 1, :, h * dim : (h + 1) * dim])

    scale = dim**-0.5
    factor = scale * math.log2(math.e)

    def score(i, out_ref, top_ref):
        s, j = of_query[i], of_key[i]
        h = lax.rem(s // 2, heads)
        keys = pool[j, 0, :, pl.ds(pl.multiple_of(h * dim, dim), dim)]
        scores = jnp.dot(keys, turned_q[s], preferred_element_type=jnp.float32)
        out_ref[...] = scores
        top_ref[...] = jnp.max(scores.reshape(tile // 8, 8, tile), axis=0)

    def weigh(i, in_ref, top_ref):
        s, j = of_query[i], of_key[i]
        h = lax.rem(s // 2, heads)
        old = max_ref[s, :1, :]
        new = jnp.maximum(old, jnp.max(top_ref[...], axis=0, keepdims=True))
        shrink = jnp.exp2((old - new) * factor)
        max_ref[s, :1, :] = new
        weights = jnp.exp2((in_ref[...] - new) * factor)
        sum_ref[s] = sum_ref[s] * shrink + jnp.sum(weights.reshape(tile // 8, 8, tile), axis=0)
        acc_ref[s] = acc_ref[s] * shrink + jnp.dot(
            turned_v[h * tiles + j], weights.astype(jnp.bfloat16), preferred_element_type=jnp.float32
        )

    for u in range(BATCH):
        score(u, score_refs[0][u], top_refs[0][u])

    def step(t, carry):
        for half in range(2):
            base = (2 * t + half) * BATCH
            for u in range(BATCH):
                score(base + BATCH + u, score_refs[1 - half][u], top_refs[1 - half][u])
            for u in range(BATCH):
                weigh(base + u, score_refs[half][u], top_refs[half][u])
        return carry

    lax.fori_loop(0, (count + 2 * BATCH - 1) // (2 * BATCH), step, 0)

    width = heads * dim
    for n in range(sets):
        outs[n][width : width + EXTRA, :] = jnp.zeros((EXTRA, 2 * tile), outs[n].dtype)
        for h in range(heads):
            for p in range(2):
                s = (n * heads + h) * 2 + p
                at = slice(p * tile, (p + 1) * tile)
                total = jnp.maximum(jnp.sum(sum_ref[s], axis=0, keepdims=True), 1e-30)
                outs[n][h * dim : (h + 1) * dim, at] = (acc_ref[s] / total).astype(outs[n].dtype)
                left = max_ref[s, :1, :] * scale + jnp.log(total)
                for i in range(3):
                    part = left.astype(outs[n].dtype)
                    outs[n][width + 3 * h + i : width + 3 * h + i + 1, at] = part
                    left = left - part.astype(jnp.float32)


def attend(mask, queries, sources, heads, first_set, first_tile, out_dtype):
    sets = len(queries)
    brick, width = queries[0].shape
    tile = brick // 2
    dim = width // heads
    tiles = sum(source.shape[1] for source in sources) // tile
    count_q = sets * heads * 2
    hbm = pl.BlockSpec(memory_space=pl.ANY)
    vmem = pl.BlockSpec(memory_space=pltpu.VMEM)
    return pl.pallas_call(
        functools.partial(
            attend_kernel,
            sets=sets,
            tiles=tiles,
            first_set=first_set,
            first_tile=first_tile,
            heads=heads,
            tile=tile,
            dim=dim,
        ),
        out_shape=[jax.ShapeDtypeStruct((width + EXTRA, brick), out_dtype)] * sets,
        in_specs=[pl.BlockSpec(memory_space=pltpu.SMEM)] + [hbm] * (sets + len(sources)),
        out_specs=[vmem] * sets,
        scratch_shapes=[
            pltpu.VMEM((tiles, 2, tile, width), jnp.bfloat16),
            pltpu.VMEM((sets, brick, width), jnp.bfloat16),
            pltpu.VMEM((count_q + 1, dim, tile), jnp.bfloat16),
            pltpu.VMEM((tiles * heads, dim, tile), jnp.bfloat16),
            pltpu.VMEM((count_q + 1, 8, tile), jnp.float32),
            pltpu.VMEM((count_q + 1, 8, tile), jnp.float32),
            pltpu.VMEM((count_q + 1, dim, tile), jnp.float32),
            pltpu.SMEM((count_q * tiles + 8 * BATCH,), jnp.int32),
            pltpu.SMEM((count_q * tiles + 8 * BATCH,), jnp.int32),
        ]
        + [pltpu.VMEM((tile, tile), jnp.float32)] * (2 * BATCH)
        + [pltpu.VMEM((8, tile), jnp.float32)] * (2 * BATCH)
        + [pltpu.SemaphoreType.DMA((sets + tiles,))],
        compiler_params=pltpu.CompilerParams(vmem_limit_bytes=VMEM_LIMIT),
        name=f"attend_{sets}_{tiles}",
    )(mask, *queries, *sources)


def merge_kernel(valid_ref, *refs, heads):
    parts, outs = refs[:4], refs[4:]
    width, brick = parts[0].shape[0] - EXTRA, parts[0].shape[1]
    dim = width // heads
    quarter = brick // 4
    for h in range(heads):
        lse = []
        for i in range(4):
            rows = parts[i][width : width + EXTRA, :].astype(jnp.float32)
            lse.append(rows[3 * h : 3 * h + 1] + rows[3 * h + 1 : 3 * h + 2] + rows[3 * h + 2 : 3 * h + 3])
        lse[2] = jnp.where(valid_ref[0] > 0, lse[2], FAR)
        lse[3] = jnp.where(valid_ref[1] > 0, lse[3], FAR)
        top = jnp.maximum(jnp.maximum(lse[0], lse[1]), jnp.maximum(lse[2], lse[3]))
        shares = [jnp.exp(x - top) for x in lse]
        total = shares[0] + shares[1] + shares[2] + shares[3]
        lanes = slice(h * dim, (h + 1) * dim)
        merged = parts[0][lanes, :].astype(jnp.float32) * (shares[0] / total)
        merged += parts[1][lanes, :].astype(jnp.float32) * (shares[1] / total)
        merged += parts[2][lanes, :].astype(jnp.float32) * (shares[2] / total)
        merged += parts[3][lanes, :].astype(jnp.float32) * (shares[3] / total)
        merged = jnp.transpose(merged).astype(jnp.bfloat16)
        for k in range(4):
            outs[k][:, lanes] = merged[k * quarter : (k + 1) * quarter, :]


def merge(valid, parts, heads):
    width, brick = parts[0].shape[0] - EXTRA, parts[0].shape[1]
    vmem = pl.BlockSpec(memory_space=pltpu.VMEM)
    return pl.pallas_call(
        functools.partial(merge_kernel, heads=heads),
        out_shape=[jax.ShapeDtypeStruct((brick // 4, width), jnp.bfloat16)] * 4,
        in_specs=[pl.BlockSpec(memory_space=pltpu.SMEM)] + [vmem] * 4,
        out_specs=[vmem] * 4,
        compiler_params=pltpu.CompilerParams(vmem_limit_bytes=VMEM_LIMIT),
        name="merge",
    )(valid, *parts)


def named(lists, column, pair, time, xh):
    tile_time = lists // 2 % TIME_TILES
    tile_pair = lists // (2 * TIME_TILES) % 2
    tile_column = lists // (4 * TIME_TILES)
    beside = jnp.where(tile_column == column + 1 - 2 * (column % 2), 1, 2)
    column_slot = jnp.where(tile_column == column, 0, beside)
    slot = jnp.where(tile_pair == pair, column_slot * 2 + ((lists % 2) ^ xh), 6 + column_slot)
    slot = jnp.where((lists >= 0) & (tile_time == time), slot, -1)
    mask = jnp.any(slot[..., None] == jnp.arange(POOL, dtype=jnp.int32), axis=-2)
    return jnp.where(xh == 1, mask[..., ::-1, :], mask)


def local(qkv, key_tiles):
    heads = key_tiles.shape[0]
    seq = lax.axis_index("seq")
    head = lax.axis_index("head")
    y, xh, z = seq // 16, seq // 8 % 2, seq % 8
    core = head % 2
    pair, time = z // TIME_TILES, z % TIME_TILES
    at = head.astype(jnp.int32).reshape(1)
    place = ((1 - pair) ^ xh).astype(jnp.int32).reshape(1)
    valid = jnp.stack([time > 0, time < TIME_TILES - 1])

    lists = [send(key_tiles, list_pairs(by)) for by in (0, 1, -1)]
    lists, qkv = lax.optimization_barrier((lists, qkv))
    lists = jnp.stack(lists)
    mask = named(lists, 2 * y + core, pair, time, xh)
    here = jnp.concatenate([jnp.ones((1,), bool), valid])
    mask = (mask & here[:, None, None, None]).astype(jnp.int32).reshape(-1)

    pieces = split(at, qkv)
    kv_parts = [send(pieces[4 + k], spread_pairs(k)) for k in range(4)]
    kv_parts[0], q_pieces = lax.optimization_barrier((kv_parts[0], pieces[:4]))
    q_parts = [send(q_pieces[k], spread_pairs(k)) for k in range(4)]
    kv_own, edge = stack(place, kv_parts)
    kv_core = send(kv_own, core_pairs())
    kv_column = send(kv_own, column_pairs())
    edge_own = send(edge, edge_pairs())
    q_own = stack_queries(q_parts)
    q_prev = send(q_own, time_pairs(1))
    q_next = send(q_own, time_pairs(-1))

    bodies = (kv_own, kv_core, kv_column)
    (o_body,) = attend(mask, (q_own,), bodies, heads, 0, 0, jnp.float32)
    o_body, edge_own = lax.optimization_barrier((o_body, edge_own))
    edges = (edge_own, send(edge_own, core_pairs()), send(edge_own, column_pairs()))
    o_prev, o_next = attend(mask, (q_prev, q_next), bodies + edges, heads, 1, 0, jnp.bfloat16)
    o_before = send(o_next, time_pairs(1))
    o_after = send(o_prev, time_pairs(-1))
    (o_edge,) = attend(mask, (q_own,), edges, heads, 0, 6, jnp.float32)

    chunks = merge(valid.astype(jnp.int32), (o_body, o_edge, o_before, o_after), heads)
    home = [send(chunks[k], gather_pairs(k)) for k in range(4)]
    return join(at, home)


def solution(mesh):
    placed = (P(None, ("seq", "head"), None), P("head", "seq", None))
    return jax.shard_map(
        local, mesh=mesh, in_specs=placed, out_specs=P(("seq", "head"), None), check_vma=False
    )
```

```python
import functools
import math

import jax
import jax.numpy as jnp
from jax import lax
from jax.experimental import pallas as pl
from jax.experimental.pallas import tpu as pltpu
from jax.sharding import PartitionSpec as P

TIME_TILES = 4
AXES = ("seq", "head")
FAR = -1e30
VMEM_LIMIT = 28 * 2**20
VMEM_SMALL = 12 * 2**20
BATCH = 2
EXTRA = 16
POOL = 9


def linear(y, xh, z, xl, core):
    return ((y * 2 + xh) * 8 + z) * 4 + xl * 2 + core


def devices():
    for y in range(4):
        for xh in range(2):
            for z in range(8):
                for xl in range(2):
                    for core in range(2):
                        yield y, xh, z, xl, core


def spread_pairs(k):
    pairs = []
    for y, xh, z, xl, core in devices():
        group = (2 * xl + core) ^ k
        pairs.append((linear(y, xh, z, xl, core), linear(y, group >> 1, z, group & 1, xh)))
    return pairs


def gather_pairs(k):
    return [(b, a) for a, b in spread_pairs(k)]


def edge_pairs():
    return [(linear(y, xh, z, xl, c), linear(y, xh, z ^ 4, xl, c)) for y, xh, z, xl, c in devices()]


def core_pairs():
    return [(linear(y, xh, z, xl, c), linear(y, xh, z, xl, 1 - c)) for y, xh, z, xl, c in devices()]


def column_pairs():
    pairs = []
    for y, xh, z, xl, core in devices():
        to = y + (1 if core == 1 else -1)
        if 0 <= to < 4:
            pairs.append((linear(y, xh, z, xl, core), linear(to, xh, z, xl, 1 - core)))
    return pairs


def time_pairs(by):
    pairs = []
    for y, xh, z, xl, core in devices():
        if 0 <= z % TIME_TILES + by < TIME_TILES:
            pairs.append((linear(y, xh, z, xl, core), linear(y, xh, z + by, xl, core)))
    return pairs


def list_pairs(by):
    pairs = []
    for y, xh, z, xl, core in devices():
        if 0 <= z % TIME_TILES + by < TIME_TILES:
            pairs.append((linear(y, xh, z, xl, core), linear(y, xl, z + by, core, xh)))
    return pairs


def send(x, pairs):
    return lax.ppermute(x, AXES, pairs)


def split_kernel(at_ref, qkv_ref, *outs):
    width = outs[0].shape[-1]
    for k in range(4):
        outs[k][...] = qkv_ref[:, :, pl.ds(pl.multiple_of((at_ref[0] ^ k) * width, 128), width)]


def split(at, qkv):
    count, rows, columns = qkv.shape
    vmem = pl.BlockSpec(memory_space=pltpu.VMEM)
    return pl.pallas_call(
        split_kernel,
        out_shape=[jax.ShapeDtypeStruct((count, rows, columns // 4), qkv.dtype)] * 4,
        in_specs=[pl.BlockSpec(memory_space=pltpu.SMEM), vmem],
        out_specs=[vmem] * 4,
        compiler_params=pltpu.CompilerParams(vmem_limit_bytes=VMEM_SMALL),
        name="split",
    )(at, qkv)


def stack_kernel(place_ref, *refs):
    parts, (q_ref, kv_ref, edge_ref), sems = refs[:4], refs[4:7], refs[7]
    rows = parts[0].shape[1]
    copies = []
    for k in range(4):
        at = pl.ds(k * rows, rows)
        copies.append(pltpu.make_async_copy(parts[k].at[pl.ds(1, 2)], kv_ref.at[:, at], sems.at[k]))
        copies.append(pltpu.make_async_copy(parts[k].at[0], q_ref.at[at], sems.at[4 + k]))
    for copy in copies:
        copy.start()
    for copy in copies:
        copy.wait()
    edge_ref[...] = kv_ref[:, pl.ds(pl.multiple_of(place_ref[0] * (2 * rows), 128), 2 * rows), :]


def stack(place, parts):
    _, rows, width = parts[0].shape
    vmem = pl.BlockSpec(memory_space=pltpu.VMEM)
    return pl.pallas_call(
        stack_kernel,
        out_shape=[
            jax.ShapeDtypeStruct((4 * rows, width), parts[0].dtype),
            jax.ShapeDtypeStruct((2, 4 * rows, width), parts[0].dtype),
            jax.ShapeDtypeStruct((2, 2 * rows, width), parts[0].dtype),
        ],
        in_specs=[pl.BlockSpec(memory_space=pltpu.SMEM)] + [pl.BlockSpec(memory_space=pl.ANY)] * 4,
        out_specs=[vmem] * 3,
        scratch_shapes=[pltpu.SemaphoreType.DMA((8,))],
        compiler_params=pltpu.CompilerParams(vmem_limit_bytes=VMEM_SMALL),
        name="stack",
    )(place, *parts)


def join_kernel(at_ref, *refs):
    parts, out_ref = refs[:4], refs[4]
    width = parts[0].shape[-1]
    for k in range(4):
        out_ref[:, pl.ds(pl.multiple_of((at_ref[0] ^ k) * width, 128), width)] = parts[k][...]


def join(at, parts):
    rows, width = parts[0].shape
    vmem = pl.BlockSpec(memory_space=pltpu.VMEM)
    return pl.pallas_call(
        join_kernel,
        out_shape=jax.ShapeDtypeStruct((rows, 4 * width), parts[0].dtype),
        in_specs=[pl.BlockSpec(memory_space=pltpu.SMEM)] + [vmem] * 4,
        out_specs=vmem,
        compiler_params=pltpu.CompilerParams(vmem_limit_bytes=VMEM_SMALL),
        name="join",
    )(at, *parts)


def attend_kernel(mask_ref, *refs, sets, tiles, first_set, first_tile, heads, tile, dim):
    pieces = 3 if tiles != POOL else 6
    queries = refs[:sets]
    sources = refs[sets : sets + pieces]
    refs = refs[sets + pieces :]
    outs = refs[:sets]
    pool, held, turned_q, turned_v, max_ref, sum_ref, acc_ref, of_query, of_key = refs[sets : sets + 9]
    rest = refs[sets + 9 :]
    score_refs = (rest[:BATCH], rest[BATCH : 2 * BATCH])
    top_refs = (rest[2 * BATCH : 3 * BATCH], rest[3 * BATCH : 4 * BATCH])
    sems = rest[4 * BATCH]
    count_q = sets * heads * 2

    copies = []
    for n in range(sets):
        copies.append(pltpu.make_async_copy(queries[n], held.at[n], sems.at[n]))
    at = 0
    for source in sources:
        for r in range(source.shape[1] // tile):
            copies.append(
                pltpu.make_async_copy(source.at[:, pl.ds(r * tile, tile)], pool.at[at], sems.at[sets + at])
            )
            at += 1
    for copy in copies:
        copy.start()

    def list_pairs_of(s, count):
        for j in range(tiles):
            of_query[count] = s
            of_key[count] = j
            count = count + mask_ref[(first_set * heads * 2 + s) * POOL + first_tile + j]
        return count

    count = lax.fori_loop(0, count_q, list_pairs_of, 0)
    for i in range(4 * BATCH):
        of_query[count + i] = count_q
        of_key[count + i] = 0
    max_ref[...] = jnp.full_like(max_ref, FAR)
    sum_ref[...] = jnp.zeros_like(sum_ref)
    acc_ref[...] = jnp.zeros_like(acc_ref)
    for copy in copies:
        copy.wait()
    for n in range(sets):
        for h in range(heads):
            for p in range(2):
                turned_q[(n * heads + h) * 2 + p] = jnp.transpose(
                    held[n, p * tile : (p + 1) * tile, h * dim : (h + 1) * dim]
                )
    turned_q[count_q] = turned_q[0]
    for h in range(heads):
        for j in range(tiles):
            turned_v[h * tiles + j] = jnp.transpose(pool[j, 1, :, h * dim : (h + 1) * dim])

    scale = dim**-0.5
    factor = scale * math.log2(math.e)

    def score(i, out_ref, top_ref):
        s, j = of_query[i], of_key[i]
        h = lax.rem(s // 2, heads)
        keys = pool[j, 0, :, pl.ds(pl.multiple_of(h * dim, dim), dim)]
        scores = jnp.dot(keys, turned_q[s], preferred_element_type=jnp.float32)
        out_ref[...] = scores
        top_ref[...] = jnp.max(scores.reshape(tile // 8, 8, tile), axis=0)

    def weigh(i, in_ref, top_ref):
        s, j = of_query[i], of_key[i]
        h = lax.rem(s // 2, heads)
        old = max_ref[s, :1, :]
        new = jnp.maximum(old, jnp.max(top_ref[...], axis=0, keepdims=True))
        shrink = jnp.exp2((old - new) * factor)
        max_ref[s, :1, :] = new
        weights = jnp.exp2((in_ref[...] - new) * factor)
        sum_ref[s] = sum_ref[s] * shrink + jnp.sum(weights.reshape(tile // 8, 8, tile), axis=0)
        acc_ref[s] = acc_ref[s] * shrink + jnp.dot(
            turned_v[h * tiles + j], weights.astype(jnp.bfloat16), preferred_element_type=jnp.float32
        )

    for u in range(BATCH):
        score(u, score_refs[0][u], top_refs[0][u])

    def step(t, carry):
        for half in range(2):
            base = (2 * t + half) * BATCH
            for u in range(BATCH):
                score(base + BATCH + u, score_refs[1 - half][u], top_refs[1 - half][u])
            for u in range(BATCH):
                weigh(base + u, score_refs[half][u], top_refs[half][u])
        return carry

    lax.fori_loop(0, (count + 2 * BATCH - 1) // (2 * BATCH), step, 0)

    width = heads * dim
    for n in range(sets):
        outs[n][width : width + EXTRA, :] = jnp.zeros((EXTRA, 2 * tile), outs[n].dtype)
        for h in range(heads):
            for p in range(2):
                s = (n * heads + h) * 2 + p
                at = slice(p * tile, (p + 1) * tile)
                total = jnp.maximum(jnp.sum(sum_ref[s], axis=0, keepdims=True), 1e-30)
                outs[n][h * dim : (h + 1) * dim, at] = (acc_ref[s] / total).astype(outs[n].dtype)
                left = max_ref[s, :1, :] * scale + jnp.log(total)
                for i in range(3):
                    part = left.astype(outs[n].dtype)
                    outs[n][width + 3 * h + i : width + 3 * h + i + 1, at] = part
                    left = left - part.astype(jnp.float32)


def attend(mask, queries, sources, heads, first_set, first_tile, out_dtype):
    sets = len(queries)
    brick, width = queries[0].shape
    tile = brick // 2
    dim = width // heads
    tiles = sum(source.shape[1] for source in sources) // tile
    count_q = sets * heads * 2
    hbm = pl.BlockSpec(memory_space=pl.ANY)
    vmem = pl.BlockSpec(memory_space=pltpu.VMEM)
    return pl.pallas_call(
        functools.partial(
            attend_kernel,
            sets=sets,
            tiles=tiles,
            first_set=first_set,
            first_tile=first_tile,
            heads=heads,
            tile=tile,
            dim=dim,
        ),
        out_shape=[jax.ShapeDtypeStruct((width + EXTRA, brick), out_dtype)] * sets,
        in_specs=[pl.BlockSpec(memory_space=pltpu.SMEM)] + [hbm] * (sets + len(sources)),
        out_specs=[vmem] * sets,
        scratch_shapes=[
            pltpu.VMEM((tiles, 2, tile, width), jnp.bfloat16),
            pltpu.VMEM((sets, brick, width), jnp.bfloat16),
            pltpu.VMEM((count_q + 1, dim, tile), jnp.bfloat16),
            pltpu.VMEM((tiles * heads, dim, tile), jnp.bfloat16),
            pltpu.VMEM((count_q + 1, 8, tile), jnp.float32),
            pltpu.VMEM((count_q + 1, 8, tile), jnp.float32),
            pltpu.VMEM((count_q + 1, dim, tile), jnp.float32),
            pltpu.SMEM((count_q * tiles + 8 * BATCH,), jnp.int32),
            pltpu.SMEM((count_q * tiles + 8 * BATCH,), jnp.int32),
        ]
        + [pltpu.VMEM((tile, tile), jnp.float32)] * (2 * BATCH)
        + [pltpu.VMEM((8, tile), jnp.float32)] * (2 * BATCH)
        + [pltpu.SemaphoreType.DMA((sets + tiles,))],
        compiler_params=pltpu.CompilerParams(vmem_limit_bytes=VMEM_LIMIT),
        name=f"attend_{sets}_{tiles}",
    )(mask, *queries, *sources)


def merge_kernel(valid_ref, *refs, heads):
    parts, outs = refs[:4], refs[4:]
    width, brick = parts[0].shape[0] - EXTRA, parts[0].shape[1]
    dim = width // heads
    quarter = brick // 4
    for h in range(heads):
        lse = []
        for i in range(4):
            rows = parts[i][width : width + EXTRA, :].astype(jnp.float32)
            lse.append(rows[3 * h : 3 * h + 1] + rows[3 * h + 1 : 3 * h + 2] + rows[3 * h + 2 : 3 * h + 3])
        lse[2] = jnp.where(valid_ref[0] > 0, lse[2], FAR)
        lse[3] = jnp.where(valid_ref[1] > 0, lse[3], FAR)
        top = jnp.maximum(jnp.maximum(lse[0], lse[1]), jnp.maximum(lse[2], lse[3]))
        shares = [jnp.exp(x - top) for x in lse]
        total = shares[0] + shares[1] + shares[2] + shares[3]
        lanes = slice(h * dim, (h + 1) * dim)
        merged = parts[0][lanes, :].astype(jnp.float32) * (shares[0] / total)
        merged += parts[1][lanes, :].astype(jnp.float32) * (shares[1] / total)
        merged += parts[2][lanes, :].astype(jnp.float32) * (shares[2] / total)
        merged += parts[3][lanes, :].astype(jnp.float32) * (shares[3] / total)
        merged = jnp.transpose(merged).astype(jnp.bfloat16)
        for k in range(4):
            outs[k][:, lanes] = merged[k * quarter : (k + 1) * quarter, :]


def merge(valid, parts, heads):
    width, brick = parts[0].shape[0] - EXTRA, parts[0].shape[1]
    vmem = pl.BlockSpec(memory_space=pltpu.VMEM)
    return pl.pallas_call(
        functools.partial(merge_kernel, heads=heads),
        out_shape=[jax.ShapeDtypeStruct((brick // 4, width), jnp.bfloat16)] * 4,
        in_specs=[pl.BlockSpec(memory_space=pltpu.SMEM)] + [vmem] * 4,
        out_specs=[vmem] * 4,
        compiler_params=pltpu.CompilerParams(vmem_limit_bytes=VMEM_SMALL),
        name="merge",
    )(valid, *parts)


def named(lists, column, pair, time, xh):
    tile_time = lists // 2 % TIME_TILES
    tile_pair = lists // (2 * TIME_TILES) % 2
    tile_column = lists // (4 * TIME_TILES)
    beside = jnp.where(tile_column == column + 1 - 2 * (column % 2), 1, 2)
    column_slot = jnp.where(tile_column == column, 0, beside)
    slot = jnp.where(tile_pair == pair, column_slot * 2 + ((lists % 2) ^ xh), 6 + column_slot)
    slot = jnp.where((lists >= 0) & (tile_time == time), slot, -1)
    mask = jnp.any(slot[..., None] == jnp.arange(POOL, dtype=jnp.int32), axis=-2)
    return jnp.where(xh == 1, mask[..., ::-1, :], mask)


def local(qkv, key_tiles):
    heads = key_tiles.shape[0]
    seq = lax.axis_index("seq")
    head = lax.axis_index("head")
    y, xh, z = seq // 16, seq // 8 % 2, seq % 8
    core = head % 2
    pair, time = z // TIME_TILES, z % TIME_TILES
    at = head.astype(jnp.int32).reshape(1)
    place = ((1 - pair) ^ xh).astype(jnp.int32).reshape(1)
    valid = jnp.stack([time > 0, time < TIME_TILES - 1])

    lists = [send(key_tiles, list_pairs(by)) for by in (0, 1, -1)]
    lists = jnp.stack(lists)
    mask = named(lists, 2 * y + core, pair, time, xh)
    here = jnp.concatenate([jnp.ones((1,), bool), valid])
    mask = (mask & here[:, None, None, None]).astype(jnp.int32).reshape(-1)

    pieces = split(at, qkv)
    parts = [send(pieces[k], spread_pairs(k)) for k in range(4)]
    parts, mask = lax.optimization_barrier((parts, mask))
    q_own, kv_own, edge = stack(place, parts)
    edge_own = send(edge, edge_pairs())
    kv_core = send(kv_own, core_pairs())
    kv_column = send(kv_own, column_pairs())

    bodies = (kv_own, kv_core, kv_column)
    (o_body,) = attend(mask, (q_own,), bodies, heads, 0, 0, jnp.float32)
    o_body, edge_own, q_away = lax.optimization_barrier((o_body, edge_own, q_own))
    q_prev = send(q_away, time_pairs(1))
    q_next = send(q_away, time_pairs(-1))
    edges = (edge_own, send(edge_own, core_pairs()), send(edge_own, column_pairs()))
    o_prev, o_next = attend(mask, (q_prev, q_next), bodies + edges, heads, 1, 0, jnp.bfloat16)
    o_before = send(o_next, time_pairs(1))
    o_after = send(o_prev, time_pairs(-1))
    (o_edge,) = attend(mask, (q_own,), edges, heads, 0, 6, jnp.float32)

    chunks = merge(valid.astype(jnp.int32), (o_body, o_edge, o_before, o_after), heads)
    home = [send(chunks[k], gather_pairs(k)) for k in range(4)]
    return join(at, home)


def solution(mesh):
    placed = (P(None, ("seq", "head"), None), P("head", "seq", None))
    return jax.shard_map(
        local, mesh=mesh, in_specs=placed, out_specs=P(("seq", "head"), None), check_vma=False
    )
```

```python
import functools
import math

import jax
import jax.numpy as jnp
from jax import lax
from jax.experimental import pallas as pl
from jax.experimental.pallas import tpu as pltpu
from jax.sharding import PartitionSpec as P

TIME_TILES = 4
AXES = ("seq", "head")
FAR = -1e30
VMEM_LIMIT = 28 * 2**20
VMEM_SMALL = 12 * 2**20
BATCH = 2
EXTRA = 16
POOL = 9


def linear(y, xh, z, xl, core):
    return ((y * 2 + xh) * 8 + z) * 4 + xl * 2 + core


def devices():
    for y in range(4):
        for xh in range(2):
            for z in range(8):
                for xl in range(2):
                    for core in range(2):
                        yield y, xh, z, xl, core


def spread_pairs(k):
    pairs = []
    for y, xh, z, xl, core in devices():
        group = (2 * xl + core) ^ k
        pairs.append((linear(y, xh, z, xl, core), linear(y, group >> 1, z, group & 1, xh)))
    return pairs


def gather_pairs(k):
    return [(b, a) for a, b in spread_pairs(k)]


def edge_pairs():
    return [(linear(y, xh, z, xl, c), linear(y, xh, z ^ 4, xl, c)) for y, xh, z, xl, c in devices()]


def core_pairs():
    return [(linear(y, xh, z, xl, c), linear(y, xh, z, xl, 1 - c)) for y, xh, z, xl, c in devices()]


def column_pairs():
    pairs = []
    for y, xh, z, xl, core in devices():
        to = y + (1 if core == 1 else -1)
        if 0 <= to < 4:
            pairs.append((linear(y, xh, z, xl, core), linear(to, xh, z, xl, 1 - core)))
    return pairs


def time_pairs(by):
    pairs = []
    for y, xh, z, xl, core in devices():
        if 0 <= z % TIME_TILES + by < TIME_TILES:
            pairs.append((linear(y, xh, z, xl, core), linear(y, xh, z + by, xl, core)))
    return pairs


def list_pairs(by):
    pairs = []
    for y, xh, z, xl, core in devices():
        if 0 <= z % TIME_TILES + by < TIME_TILES:
            pairs.append((linear(y, xh, z, xl, core), linear(y, xl, z + by, core, xh)))
    return pairs


def send(x, pairs):
    return lax.ppermute(x, AXES, pairs)


def split_kernel(at_ref, qkv_ref, *outs):
    width = outs[0].shape[-1]
    for k in range(4):
        lanes = pl.ds(pl.multiple_of((at_ref[0] ^ k) * width, 128), width)
        outs[k][...] = qkv_ref[0, :, lanes]
        outs[4 + k][...] = qkv_ref[1:3, :, lanes]


def split(at, qkv):
    _, rows, columns = qkv.shape
    width = columns // 4
    vmem = pl.BlockSpec(memory_space=pltpu.VMEM)
    shapes = [jax.ShapeDtypeStruct((rows, width), qkv.dtype)] * 4
    shapes += [jax.ShapeDtypeStruct((2, rows, width), qkv.dtype)] * 4
    return pl.pallas_call(
        split_kernel,
        out_shape=shapes,
        in_specs=[pl.BlockSpec(memory_space=pltpu.SMEM), vmem],
        out_specs=[vmem] * 8,
        compiler_params=pltpu.CompilerParams(vmem_limit_bytes=VMEM_SMALL),
        name="split",
    )(at, qkv)


def stack_kernel(place_ref, *refs):
    parts, kv_ref, edge_ref, sems = refs[:4], refs[4], refs[5], refs[6]
    rows = parts[0].shape[1]
    copies = []
    for k in range(4):
        copies.append(pltpu.make_async_copy(parts[k], kv_ref.at[:, pl.ds(k * rows, rows)], sems.at[k]))
    for copy in copies:
        copy.start()
    for copy in copies:
        copy.wait()
    edge_ref[...] = kv_ref[:, pl.ds(pl.multiple_of(place_ref[0] * (2 * rows), 128), 2 * rows), :]


def stack(place, parts):
    _, rows, width = parts[0].shape
    vmem = pl.BlockSpec(memory_space=pltpu.VMEM)
    return pl.pallas_call(
        stack_kernel,
        out_shape=[
            jax.ShapeDtypeStruct((2, 4 * rows, width), parts[0].dtype),
            jax.ShapeDtypeStruct((2, 2 * rows, width), parts[0].dtype),
        ],
        in_specs=[pl.BlockSpec(memory_space=pltpu.SMEM)] + [pl.BlockSpec(memory_space=pl.ANY)] * 4,
        out_specs=[vmem] * 2,
        scratch_shapes=[pltpu.SemaphoreType.DMA((4,))],
        compiler_params=pltpu.CompilerParams(vmem_limit_bytes=VMEM_SMALL),
        name="stack",
    )(place, *parts)


def stack_queries_kernel(*refs):
    parts, q_ref, sems = refs[:4], refs[4], refs[5]
    rows = parts[0].shape[0]
    copies = []
    for k in range(4):
        copies.append(pltpu.make_async_copy(parts[k], q_ref.at[pl.ds(k * rows, rows)], sems.at[k]))
    for copy in copies:
        copy.start()
    for copy in copies:
        copy.wait()


def stack_queries(parts):
    rows, width = parts[0].shape
    return pl.pallas_call(
        stack_queries_kernel,
        out_shape=jax.ShapeDtypeStruct((4 * rows, width), parts[0].dtype),
        in_specs=[pl.BlockSpec(memory_space=pl.ANY)] * 4,
        out_specs=pl.BlockSpec(memory_space=pltpu.VMEM),
        scratch_shapes=[pltpu.SemaphoreType.DMA((4,))],
        compiler_params=pltpu.CompilerParams(vmem_limit_bytes=VMEM_SMALL),
        name="stack_queries",
    )(*parts)


def join_kernel(at_ref, *refs):
    parts, out_ref = refs[:4], refs[4]
    width = parts[0].shape[-1]
    for k in range(4):
        out_ref[:, pl.ds(pl.multiple_of((at_ref[0] ^ k) * width, 128), width)] = parts[k][...]


def join(at, parts):
    rows, width = parts[0].shape
    vmem = pl.BlockSpec(memory_space=pltpu.VMEM)
    return pl.pallas_call(
        join_kernel,
        out_shape=jax.ShapeDtypeStruct((rows, 4 * width), parts[0].dtype),
        in_specs=[pl.BlockSpec(memory_space=pltpu.SMEM)] + [vmem] * 4,
        out_specs=vmem,
        compiler_params=pltpu.CompilerParams(vmem_limit_bytes=VMEM_SMALL),
        name="join",
    )(at, *parts)


def attend_kernel(mask_ref, *refs, sets, pieces, begun, tiles, first_set, first_tile, heads, tile, dim):
    queries = refs[:sets]
    sources = refs[sets : sets + pieces]
    starts = refs[sets + pieces : sets + pieces + begun]
    refs = refs[sets + pieces + begun :]
    outs = refs[:sets]
    pool, held, turned_q, turned_v, max_ref, sum_ref, acc_ref, of_query, of_key = refs[sets : sets + 9]
    rest = refs[sets + 9 :]
    score_refs = (rest[:BATCH], rest[BATCH : 2 * BATCH])
    top_refs = (rest[2 * BATCH : 3 * BATCH], rest[3 * BATCH : 4 * BATCH])
    sems = rest[4 * BATCH]
    count_q = sets * heads * 2

    copies = []
    for n in range(sets):
        copies.append(pltpu.make_async_copy(queries[n], held.at[n], sems.at[n]))
    at = 0
    for source in sources:
        for r in range(source.shape[1] // tile):
            copies.append(
                pltpu.make_async_copy(source.at[:, pl.ds(r * tile, tile)], pool.at[at], sems.at[sets + at])
            )
            at += 1
    for copy in copies:
        copy.start()

    def list_pairs_of(s, count):
        for j in range(tiles):
            of_query[count] = s
            of_key[count] = j
            count = count + mask_ref[(first_set * heads * 2 + s) * POOL + first_tile + j]
        return count

    count = lax.fori_loop(0, count_q, list_pairs_of, 0)
    for i in range(4 * BATCH):
        of_query[count + i] = count_q
        of_key[count + i] = 0
    scale = dim**-0.5
    factor = scale * math.log2(math.e)
    width = heads * dim
    if begun:
        sum_ref[...] = jnp.full_like(sum_ref, 0.125)
        for n in range(sets):
            for h in range(heads):
                lse = starts[n][width + 3 * h : width + 3 * h + 1, :]
                for i in range(1, 3):
                    lse = lse + starts[n][width + 3 * h + i : width + 3 * h + i + 1, :]
                for p in range(2):
                    s = (n * heads + h) * 2 + p
                    at = slice(p * tile, (p + 1) * tile)
                    max_ref[s, :1, :] = lse[:, at] / scale
                    acc_ref[s] = starts[n][h * dim : (h + 1) * dim, at]
        max_ref[count_q] = jnp.zeros((8, tile), jnp.float32)
        acc_ref[count_q] = jnp.zeros((dim, tile), jnp.float32)
    else:
        max_ref[...] = jnp.full_like(max_ref, FAR)
        sum_ref[...] = jnp.zeros_like(sum_ref)
        acc_ref[...] = jnp.zeros_like(acc_ref)
    for copy in copies:
        copy.wait()
    for n in range(sets):
        for h in range(heads):
            for p in range(2):
                turned_q[(n * heads + h) * 2 + p] = jnp.transpose(
                    held[n, p * tile : (p + 1) * tile, h * dim : (h + 1) * dim]
                )
    turned_q[count_q] = turned_q[0]
    for h in range(heads):
        for j in range(tiles):
            turned_v[h * tiles + j] = jnp.transpose(pool[j, 1, :, h * dim : (h + 1) * dim])

    def score(i, out_ref, top_ref):
        s, j = of_query[i], of_key[i]
        h = lax.rem(s // 2, heads)
        keys = pool[j, 0, :, pl.ds(pl.multiple_of(h * dim, dim), dim)]
        scores = jnp.dot(keys, turned_q[s], preferred_element_type=jnp.float32)
        out_ref[...] = scores
        top_ref[...] = jnp.max(scores.reshape(tile // 8, 8, tile), axis=0)

    def weigh(i, in_ref, top_ref):
        s, j = of_query[i], of_key[i]
        h = lax.rem(s // 2, heads)
        old = max_ref[s, :1, :]
        new = jnp.maximum(old, jnp.max(top_ref[...], axis=0, keepdims=True))
        shrink = jnp.exp2((old - new) * factor)
        max_ref[s, :1, :] = new
        weights = jnp.exp2((in_ref[...] - new) * factor)
        sum_ref[s] = sum_ref[s] * shrink + jnp.sum(weights.reshape(tile // 8, 8, tile), axis=0)
        acc_ref[s] = acc_ref[s] * shrink + jnp.dot(
            turned_v[h * tiles + j], weights.astype(jnp.bfloat16), preferred_element_type=jnp.float32
        )

    for u in range(BATCH):
        score(u, score_refs[0][u], top_refs[0][u])

    def step(t, carry):
        for half in range(2):
            base = (2 * t + half) * BATCH
            for u in range(BATCH):
                score(base + BATCH + u, score_refs[1 - half][u], top_refs[1 - half][u])
            for u in range(BATCH):
                weigh(base + u, score_refs[half][u], top_refs[half][u])
        return carry

    lax.fori_loop(0, (count + 2 * BATCH - 1) // (2 * BATCH), step, 0)

    for n in range(sets):
        outs[n][width : width + EXTRA, :] = jnp.zeros((EXTRA, 2 * tile), outs[n].dtype)
        for h in range(heads):
            for p in range(2):
                s = (n * heads + h) * 2 + p
                at = slice(p * tile, (p + 1) * tile)
                total = jnp.maximum(jnp.sum(sum_ref[s], axis=0, keepdims=True), 1e-30)
                outs[n][h * dim : (h + 1) * dim, at] = (acc_ref[s] / total).astype(outs[n].dtype)
                left = max_ref[s, :1, :] * scale + jnp.log(total)
                for i in range(3):
                    part = left.astype(outs[n].dtype)
                    outs[n][width + 3 * h + i : width + 3 * h + i + 1, at] = part
                    left = left - part.astype(jnp.float32)


def attend(mask, queries, sources, starts, heads, first_set, first_tile, out_dtype):
    sets = len(queries)
    brick, width = queries[0].shape
    tile = brick // 2
    dim = width // heads
    tiles = sum(source.shape[1] for source in sources) // tile
    count_q = sets * heads * 2
    hbm = pl.BlockSpec(memory_space=pl.ANY)
    vmem = pl.BlockSpec(memory_space=pltpu.VMEM)
    return pl.pallas_call(
        functools.partial(
            attend_kernel,
            sets=sets,
            pieces=len(sources),
            begun=len(starts),
            tiles=tiles,
            first_set=first_set,
            first_tile=first_tile,
            heads=heads,
            tile=tile,
            dim=dim,
        ),
        out_shape=[jax.ShapeDtypeStruct((width + EXTRA, brick), out_dtype)] * sets,
        in_specs=[pl.BlockSpec(memory_space=pltpu.SMEM)] + [hbm] * (sets + len(sources)) + [vmem] * len(starts),
        out_specs=[vmem] * sets,
        scratch_shapes=[
            pltpu.VMEM((tiles, 2, tile, width), jnp.bfloat16),
            pltpu.VMEM((sets, brick, width), jnp.bfloat16),
            pltpu.VMEM((count_q + 1, dim, tile), jnp.bfloat16),
            pltpu.VMEM((tiles * heads, dim, tile), jnp.bfloat16),
            pltpu.VMEM((count_q + 1, 8, tile), jnp.float32),
            pltpu.VMEM((count_q + 1, 8, tile), jnp.float32),
            pltpu.VMEM((count_q + 1, dim, tile), jnp.float32),
            pltpu.SMEM((count_q * tiles + 8 * BATCH,), jnp.int32),
            pltpu.SMEM((count_q * tiles + 8 * BATCH,), jnp.int32),
        ]
        + [pltpu.VMEM((tile, tile), jnp.float32)] * (2 * BATCH)
        + [pltpu.VMEM((8, tile), jnp.float32)] * (2 * BATCH)
        + [pltpu.SemaphoreType.DMA((sets + tiles,))],
        compiler_params=pltpu.CompilerParams(vmem_limit_bytes=VMEM_LIMIT),
        name=f"attend_{sets}_{tiles}",
    )(mask, *queries, *sources, *starts)


def merge_kernel(valid_ref, *refs, heads):
    parts, outs = refs[:3], refs[3:]
    width, brick = parts[0].shape[0] - EXTRA, parts[0].shape[1]
    dim = width // heads
    quarter = brick // 4
    for h in range(heads):
        lse = []
        for i in range(3):
            rows = parts[i][width : width + EXTRA, :].astype(jnp.float32)
            lse.append(rows[3 * h : 3 * h + 1] + rows[3 * h + 1 : 3 * h + 2] + rows[3 * h + 2 : 3 * h + 3])
        lse[1] = jnp.where(valid_ref[0] > 0, lse[1], FAR)
        lse[2] = jnp.where(valid_ref[1] > 0, lse[2], FAR)
        top = jnp.maximum(jnp.maximum(lse[0], lse[1]), lse[2])
        shares = [jnp.exp(x - top) for x in lse]
        total = shares[0] + shares[1] + shares[2]
        lanes = slice(h * dim, (h + 1) * dim)
        merged = parts[0][lanes, :].astype(jnp.float32) * (shares[0] / total)
        merged += parts[1][lanes, :].astype(jnp.float32) * (shares[1] / total)
        merged += parts[2][lanes, :].astype(jnp.float32) * (shares[2] / total)
        merged = jnp.transpose(merged).astype(jnp.bfloat16)
        for k in range(4):
            outs[k][:, lanes] = merged[k * quarter : (k + 1) * quarter, :]


def merge(valid, parts, heads):
    width, brick = parts[0].shape[0] - EXTRA, parts[0].shape[1]
    vmem = pl.BlockSpec(memory_space=pltpu.VMEM)
    return pl.pallas_call(
        functools.partial(merge_kernel, heads=heads),
        out_shape=[jax.ShapeDtypeStruct((brick // 4, width), jnp.bfloat16)] * 4,
        in_specs=[pl.BlockSpec(memory_space=pltpu.SMEM)] + [vmem] * 3,
        out_specs=[vmem] * 4,
        compiler_params=pltpu.CompilerParams(vmem_limit_bytes=VMEM_SMALL),
        name="merge",
    )(valid, *parts)


def named(lists, column, pair, time, xh):
    tile_time = lists // 2 % TIME_TILES
    tile_pair = lists // (2 * TIME_TILES) % 2
    tile_column = lists // (4 * TIME_TILES)
    beside = jnp.where(tile_column == column + 1 - 2 * (column % 2), 1, 2)
    column_slot = jnp.where(tile_column == column, 0, beside)
    slot = jnp.where(tile_pair == pair, column_slot * 2 + ((lists % 2) ^ xh), 6 + column_slot)
    slot = jnp.where((lists >= 0) & (tile_time == time), slot, -1)
    mask = jnp.any(slot[..., None] == jnp.arange(POOL, dtype=jnp.int32), axis=-2)
    return jnp.where(xh == 1, mask[..., ::-1, :], mask)


def local(qkv, key_tiles):
    heads = key_tiles.shape[0]
    seq = lax.axis_index("seq")
    head = lax.axis_index("head")
    y, xh, z = seq // 16, seq // 8 % 2, seq % 8
    core = head % 2
    pair, time = z // TIME_TILES, z % TIME_TILES
    at = head.astype(jnp.int32).reshape(1)
    place = ((1 - pair) ^ xh).astype(jnp.int32).reshape(1)
    valid = jnp.stack([time > 0, time < TIME_TILES - 1])

    pieces = split(at, qkv)
    q_parts = [send(pieces[k], spread_pairs(k)) for k in range(4)]
    kv_pieces = list(pieces[4:])
    for k in range(1, 4):
        q_parts[k], kv_pieces[k] = lax.optimization_barrier((q_parts[k], kv_pieces[k]))
    kv_parts = [send(kv_pieces[k], spread_pairs(k)) for k in range(4)]
    q_own = stack_queries(q_parts)
    q_prev = send(q_own, time_pairs(1))
    q_next = send(q_own, time_pairs(-1))
    place, q_prev, q_next = lax.optimization_barrier((place, q_prev, q_next))
    kv_own, edge = stack(place, kv_parts)
    kv_own, edge, key_tiles = lax.optimization_barrier((kv_own, edge, key_tiles))
    edge_own = send(edge, edge_pairs())
    bodies = (kv_own, send(kv_own, core_pairs()), send(kv_own, column_pairs()))

    lists = [send(key_tiles, list_pairs(by)) for by in (0, 1, -1)]
    lists = jnp.stack(lists)
    mask = named(lists, 2 * y + core, pair, time, xh)
    here = jnp.concatenate([jnp.ones((1,), bool), valid])
    mask = (mask & here[:, None, None, None]).astype(jnp.int32).reshape(-1)

    begun = attend(mask, (q_own, q_prev, q_next), bodies, (), heads, 0, 0, jnp.float32)
    begun, edge_own = lax.optimization_barrier((begun, edge_own))
    edges = (edge_own, send(edge_own, core_pairs()), send(edge_own, column_pairs()))
    o_prev, o_next = attend(mask, (q_prev, q_next), edges, begun[1:], heads, 1, 6, jnp.bfloat16)
    o_before = send(o_next, time_pairs(1))
    o_after = send(o_prev, time_pairs(-1))
    (o_own,) = attend(mask, (q_own,), edges, begun[:1], heads, 0, 6, jnp.float32)

    chunks = merge(valid.astype(jnp.int32), (o_own, o_before, o_after), heads)
    home = [send(chunks[k], gather_pairs(k)) for k in range(4)]
    return join(at, home)


def solution(mesh):
    placed = (P(None, ("seq", "head"), None), P("head", "seq", None))
    return jax.shard_map(
        local, mesh=mesh, in_specs=placed, out_specs=P(("seq", "head"), None), check_vma=False
    )
```

```python
import functools
import math

import jax
import jax.numpy as jnp
from jax import lax
from jax.experimental import pallas as pl
from jax.experimental.pallas import tpu as pltpu
from jax.sharding import PartitionSpec as P

TIME_TILES = 4
AXES = ("seq", "head")
FAR = -1e30
VMEM_LIMIT = 28 * 2**20
VMEM_SMALL = 12 * 2**20
BATCH = 2
EXTRA = 16
POOL = 9


def linear(y, xh, z, xl, core):
    return ((y * 2 + xh) * 8 + z) * 4 + xl * 2 + core


def devices():
    for y in range(4):
        for xh in range(2):
            for z in range(8):
                for xl in range(2):
                    for core in range(2):
                        yield y, xh, z, xl, core


def spread_pairs(k):
    pairs = []
    for y, xh, z, xl, core in devices():
        group = (2 * xl + core) ^ k
        pairs.append((linear(y, xh, z, xl, core), linear(y, group >> 1, z, group & 1, xh)))
    return pairs


def gather_pairs(k):
    return [(b, a) for a, b in spread_pairs(k)]


def edge_pairs():
    return [(linear(y, xh, z, xl, c), linear(y, xh, z ^ 4, xl, c)) for y, xh, z, xl, c in devices()]


def core_pairs():
    return [(linear(y, xh, z, xl, c), linear(y, xh, z, xl, 1 - c)) for y, xh, z, xl, c in devices()]


def column_pairs():
    pairs = []
    for y, xh, z, xl, core in devices():
        to = y + (1 if core == 1 else -1)
        if 0 <= to < 4:
            pairs.append((linear(y, xh, z, xl, core), linear(to, xh, z, xl, 1 - core)))
    return pairs


def time_pairs(by):
    pairs = []
    for y, xh, z, xl, core in devices():
        if 0 <= z % TIME_TILES + by < TIME_TILES:
            pairs.append((linear(y, xh, z, xl, core), linear(y, xh, z + by, xl, core)))
    return pairs


def send(x, pairs):
    return lax.ppermute(x, AXES, pairs)


def split_kernel(at_ref, qkv_ref, names_ref, *outs):
    width = outs[0].shape[-1]
    rows = qkv_ref.shape[1]
    for k in range(4):
        lanes = pl.ds(pl.multiple_of((at_ref[0] ^ k) * width, 128), width)
        outs[k][:rows, :] = qkv_ref[0, :, lanes]
        outs[k][rows:, :] = names_ref[...]
        outs[4 + k][...] = qkv_ref[1:3, :, lanes]


def split(at, qkv, names):
    _, rows, columns = qkv.shape
    width = columns // 4
    vmem = pl.BlockSpec(memory_space=pltpu.VMEM)
    shapes = [jax.ShapeDtypeStruct((rows + EXTRA, width), qkv.dtype)] * 4
    shapes += [jax.ShapeDtypeStruct((2, rows, width), qkv.dtype)] * 4
    return pl.pallas_call(
        split_kernel,
        out_shape=shapes,
        in_specs=[pl.BlockSpec(memory_space=pltpu.SMEM), vmem, vmem],
        out_specs=[vmem] * 8,
        compiler_params=pltpu.CompilerParams(vmem_limit_bytes=VMEM_SMALL),
        name="split",
    )(at, qkv, names)


def stack_kernel(place_ref, *refs):
    parts, kv_ref, edge_ref, sems = refs[:4], refs[4], refs[5], refs[6]
    rows = parts[0].shape[1]
    copies = []
    for k in range(4):
        copies.append(pltpu.make_async_copy(parts[k], kv_ref.at[:, pl.ds(k * rows, rows)], sems.at[k]))
    for copy in copies:
        copy.start()
    for copy in copies:
        copy.wait()
    edge_ref[...] = kv_ref[:, pl.ds(pl.multiple_of(place_ref[0] * (2 * rows), 128), 2 * rows), :]


def stack(place, parts):
    _, rows, width = parts[0].shape
    vmem = pl.BlockSpec(memory_space=pltpu.VMEM)
    return pl.pallas_call(
        stack_kernel,
        out_shape=[
            jax.ShapeDtypeStruct((2, 4 * rows, width), parts[0].dtype),
            jax.ShapeDtypeStruct((2, 2 * rows, width), parts[0].dtype),
        ],
        in_specs=[pl.BlockSpec(memory_space=pltpu.SMEM)] + [pl.BlockSpec(memory_space=pl.ANY)] * 4,
        out_specs=[vmem] * 2,
        scratch_shapes=[pltpu.SemaphoreType.DMA((4,))],
        compiler_params=pltpu.CompilerParams(vmem_limit_bytes=VMEM_SMALL),
        name="stack",
    )(place, *parts)


def stack_queries_kernel(*refs):
    parts, q_ref, sems = refs[:4], refs[4], refs[5]
    rows = parts[0].shape[0] - EXTRA
    copies = []
    for k in range(4):
        into = q_ref.at[pl.ds(k * rows, rows)]
        copies.append(pltpu.make_async_copy(parts[k].at[pl.ds(0, rows)], into, sems.at[k]))
    into = q_ref.at[pl.ds(4 * rows, EXTRA)]
    copies.append(pltpu.make_async_copy(parts[0].at[pl.ds(rows, EXTRA)], into, sems.at[4]))
    for copy in copies:
        copy.start()
    for copy in copies:
        copy.wait()


def stack_queries(parts):
    rows, width = parts[0].shape[0] - EXTRA, parts[0].shape[1]
    return pl.pallas_call(
        stack_queries_kernel,
        out_shape=jax.ShapeDtypeStruct((4 * rows + EXTRA, width), parts[0].dtype),
        in_specs=[pl.BlockSpec(memory_space=pl.ANY)] * 4,
        out_specs=pl.BlockSpec(memory_space=pltpu.VMEM),
        scratch_shapes=[pltpu.SemaphoreType.DMA((5,))],
        compiler_params=pltpu.CompilerParams(vmem_limit_bytes=VMEM_SMALL),
        name="stack_queries",
    )(*parts)


def join_kernel(at_ref, *refs):
    parts, out_ref = refs[:4], refs[4]
    width = parts[0].shape[-1]
    for k in range(4):
        out_ref[:, pl.ds(pl.multiple_of((at_ref[0] ^ k) * width, 128), width)] = parts[k][...]


def join(at, parts):
    rows, width = parts[0].shape
    vmem = pl.BlockSpec(memory_space=pltpu.VMEM)
    return pl.pallas_call(
        join_kernel,
        out_shape=jax.ShapeDtypeStruct((rows, 4 * width), parts[0].dtype),
        in_specs=[pl.BlockSpec(memory_space=pltpu.SMEM)] + [vmem] * 4,
        out_specs=vmem,
        compiler_params=pltpu.CompilerParams(vmem_limit_bytes=VMEM_SMALL),
        name="join",
    )(at, *parts)


def attend_kernel(mask_ref, *refs, sets, pieces, begun, tiles, first_set, first_tile, heads, tile, dim):
    queries = refs[:sets]
    sources = refs[sets : sets + pieces]
    starts = refs[sets + pieces : sets + pieces + begun]
    refs = refs[sets + pieces + begun :]
    outs = refs[:sets]
    pool, held, turned_q, turned_v, max_ref, sum_ref, acc_ref, of_query, of_key = refs[sets : sets + 9]
    rest = refs[sets + 9 :]
    score_refs = (rest[:BATCH], rest[BATCH : 2 * BATCH])
    top_refs = (rest[2 * BATCH : 3 * BATCH], rest[3 * BATCH : 4 * BATCH])
    sems = rest[4 * BATCH]
    count_q = sets * heads * 2

    copies = []
    for n in range(sets):
        copies.append(pltpu.make_async_copy(queries[n].at[pl.ds(0, 2 * tile)], held.at[n], sems.at[n]))
    at = 0
    for source in sources:
        for r in range(source.shape[1] // tile):
            copies.append(
                pltpu.make_async_copy(source.at[:, pl.ds(r * tile, tile)], pool.at[at], sems.at[sets + at])
            )
            at += 1
    for copy in copies:
        copy.start()

    def list_pairs_of(s, count):
        for j in range(tiles):
            of_query[count] = s
            of_key[count] = j
            count = count + mask_ref[(first_set * heads * 2 + s) * POOL + first_tile + j]
        return count

    count = lax.fori_loop(0, count_q, list_pairs_of, 0)
    for i in range(4 * BATCH):
        of_query[count + i] = count_q
        of_key[count + i] = 0
    scale = dim**-0.5
    factor = scale * math.log2(math.e)
    width = heads * dim
    if begun:
        sum_ref[...] = jnp.full_like(sum_ref, 0.125)
        for n in range(sets):
            for h in range(heads):
                lse = starts[n][width + 3 * h : width + 3 * h + 1, :]
                for i in range(1, 3):
                    lse = lse + starts[n][width + 3 * h + i : width + 3 * h + i + 1, :]
                for p in range(2):
                    s = (n * heads + h) * 2 + p
                    at = slice(p * tile, (p + 1) * tile)
                    max_ref[s, :1, :] = lse[:, at] / scale
                    acc_ref[s] = starts[n][h * dim : (h + 1) * dim, at]
        max_ref[count_q] = jnp.zeros((8, tile), jnp.float32)
        acc_ref[count_q] = jnp.zeros((dim, tile), jnp.float32)
    else:
        max_ref[...] = jnp.full_like(max_ref, FAR)
        sum_ref[...] = jnp.zeros_like(sum_ref)
        acc_ref[...] = jnp.zeros_like(acc_ref)
    for copy in copies:
        copy.wait()
    for n in range(sets):
        for h in range(heads):
            for p in range(2):
                turned_q[(n * heads + h) * 2 + p] = jnp.transpose(
                    held[n, p * tile : (p + 1) * tile, h * dim : (h + 1) * dim]
                )
    turned_q[count_q] = turned_q[0]
    for h in range(heads):
        for j in range(tiles):
            turned_v[h * tiles + j] = jnp.transpose(pool[j, 1, :, h * dim : (h + 1) * dim])

    def score(i, out_ref, top_ref):
        s, j = of_query[i], of_key[i]
        h = lax.rem(s // 2, heads)
        keys = pool[j, 0, :, pl.ds(pl.multiple_of(h * dim, dim), dim)]
        scores = jnp.dot(keys, turned_q[s], preferred_element_type=jnp.float32)
        out_ref[...] = scores
        top_ref[...] = jnp.max(scores.reshape(tile // 8, 8, tile), axis=0)

    def weigh(i, in_ref, top_ref):
        s, j = of_query[i], of_key[i]
        h = lax.rem(s // 2, heads)
        old = max_ref[s, :1, :]
        new = jnp.maximum(old, jnp.max(top_ref[...], axis=0, keepdims=True))
        shrink = jnp.exp2((old - new) * factor)
        max_ref[s, :1, :] = new
        weights = jnp.exp2((in_ref[...] - new) * factor)
        sum_ref[s] = sum_ref[s] * shrink + jnp.sum(weights.reshape(tile // 8, 8, tile), axis=0)
        acc_ref[s] = acc_ref[s] * shrink + jnp.dot(
            turned_v[h * tiles + j], weights.astype(jnp.bfloat16), preferred_element_type=jnp.float32
        )

    for u in range(BATCH):
        score(u, score_refs[0][u], top_refs[0][u])

    def step(t, carry):
        for half in range(2):
            base = (2 * t + half) * BATCH
            for u in range(BATCH):
                score(base + BATCH + u, score_refs[1 - half][u], top_refs[1 - half][u])
            for u in range(BATCH):
                weigh(base + u, score_refs[half][u], top_refs[half][u])
        return carry

    lax.fori_loop(0, (count + 2 * BATCH - 1) // (2 * BATCH), step, 0)

    for n in range(sets):
        outs[n][width : width + EXTRA, :] = jnp.zeros((EXTRA, 2 * tile), outs[n].dtype)
        for h in range(heads):
            for p in range(2):
                s = (n * heads + h) * 2 + p
                at = slice(p * tile, (p + 1) * tile)
                total = jnp.maximum(jnp.sum(sum_ref[s], axis=0, keepdims=True), 1e-30)
                outs[n][h * dim : (h + 1) * dim, at] = (acc_ref[s] / total).astype(outs[n].dtype)
                left = max_ref[s, :1, :] * scale + jnp.log(total)
                for i in range(3):
                    part = left.astype(outs[n].dtype)
                    outs[n][width + 3 * h + i : width + 3 * h + i + 1, at] = part
                    left = left - part.astype(jnp.float32)


def attend(mask, queries, sources, starts, heads, first_set, first_tile, out_dtype):
    sets = len(queries)
    brick, width = queries[0].shape[0] - EXTRA, queries[0].shape[1]
    tile = brick // 2
    dim = width // heads
    tiles = sum(source.shape[1] for source in sources) // tile
    count_q = sets * heads * 2
    hbm = pl.BlockSpec(memory_space=pl.ANY)
    vmem = pl.BlockSpec(memory_space=pltpu.VMEM)
    return pl.pallas_call(
        functools.partial(
            attend_kernel,
            sets=sets,
            pieces=len(sources),
            begun=len(starts),
            tiles=tiles,
            first_set=first_set,
            first_tile=first_tile,
            heads=heads,
            tile=tile,
            dim=dim,
        ),
        out_shape=[jax.ShapeDtypeStruct((width + EXTRA, brick), out_dtype)] * sets,
        in_specs=[pl.BlockSpec(memory_space=pltpu.SMEM)] + [hbm] * (sets + len(sources)) + [vmem] * len(starts),
        out_specs=[vmem] * sets,
        scratch_shapes=[
            pltpu.VMEM((tiles, 2, tile, width), jnp.bfloat16),
            pltpu.VMEM((sets, brick, width), jnp.bfloat16),
            pltpu.VMEM((count_q + 1, dim, tile), jnp.bfloat16),
            pltpu.VMEM((tiles * heads, dim, tile), jnp.bfloat16),
            pltpu.VMEM((count_q + 1, 8, tile), jnp.float32),
            pltpu.VMEM((count_q + 1, 8, tile), jnp.float32),
            pltpu.VMEM((count_q + 1, dim, tile), jnp.float32),
            pltpu.SMEM((count_q * tiles + 8 * BATCH,), jnp.int32),
            pltpu.SMEM((count_q * tiles + 8 * BATCH,), jnp.int32),
        ]
        + [pltpu.VMEM((tile, tile), jnp.float32)] * (2 * BATCH)
        + [pltpu.VMEM((8, tile), jnp.float32)] * (2 * BATCH)
        + [pltpu.SemaphoreType.DMA((sets + tiles,))],
        compiler_params=pltpu.CompilerParams(vmem_limit_bytes=VMEM_LIMIT),
        name=f"attend_{sets}_{tiles}",
    )(mask, *queries, *sources, *starts)


def merge_kernel(valid_ref, *refs, heads):
    parts, outs = refs[:3], refs[3:]
    width, brick = parts[0].shape[0] - EXTRA, parts[0].shape[1]
    dim = width // heads
    quarter = brick // 4
    for h in range(heads):
        lse = []
        for i in range(3):
            rows = parts[i][width : width + EXTRA, :].astype(jnp.float32)
            lse.append(rows[3 * h : 3 * h + 1] + rows[3 * h + 1 : 3 * h + 2] + rows[3 * h + 2 : 3 * h + 3])
        lse[1] = jnp.where(valid_ref[0] > 0, lse[1], FAR)
        lse[2] = jnp.where(valid_ref[1] > 0, lse[2], FAR)
        top = jnp.maximum(jnp.maximum(lse[0], lse[1]), lse[2])
        shares = [jnp.exp(x - top) for x in lse]
        total = shares[0] + shares[1] + shares[2]
        lanes = slice(h * dim, (h + 1) * dim)
        merged = parts[0][lanes, :].astype(jnp.float32) * (shares[0] / total)
        merged += parts[1][lanes, :].astype(jnp.float32) * (shares[1] / total)
        merged += parts[2][lanes, :].astype(jnp.float32) * (shares[2] / total)
        merged = jnp.transpose(merged).astype(jnp.bfloat16)
        for k in range(4):
            outs[k][:, lanes] = merged[k * quarter : (k + 1) * quarter, :]


def merge(valid, parts, heads):
    width, brick = parts[0].shape[0] - EXTRA, parts[0].shape[1]
    vmem = pl.BlockSpec(memory_space=pltpu.VMEM)
    return pl.pallas_call(
        functools.partial(merge_kernel, heads=heads),
        out_shape=[jax.ShapeDtypeStruct((brick // 4, width), jnp.bfloat16)] * 4,
        in_specs=[pl.BlockSpec(memory_space=pltpu.SMEM)] + [vmem] * 3,
        out_specs=[vmem] * 4,
        compiler_params=pltpu.CompilerParams(vmem_limit_bytes=VMEM_SMALL),
        name="merge",
    )(valid, *parts)


def named(lists, column, pair, time, xh):
    tile_time = lists // 2 % TIME_TILES
    tile_pair = lists // (2 * TIME_TILES) % 2
    tile_column = lists // (4 * TIME_TILES)
    beside = jnp.where(tile_column == column + 1 - 2 * (column % 2), 1, 2)
    column_slot = jnp.where(tile_column == column, 0, beside)
    slot = jnp.where(tile_pair == pair, column_slot * 2 + ((lists % 2) ^ xh), 6 + column_slot)
    slot = jnp.where((lists >= 0) & (tile_time == time), slot, -1)
    mask = jnp.any(slot[..., None] == jnp.arange(POOL, dtype=jnp.int32), axis=-2)
    return jnp.where(xh == 1, mask[..., ::-1, :], mask)


def local(qkv, key_tiles):
    heads = key_tiles.shape[0]
    seq = lax.axis_index("seq")
    head = lax.axis_index("head")
    y, xh, z = seq // 16, seq // 8 % 2, seq % 8
    core = head % 2
    pair, time = z // TIME_TILES, z % TIME_TILES
    at = head.astype(jnp.int32).reshape(1)
    place = ((1 - pair) ^ xh).astype(jnp.int32).reshape(1)
    valid = jnp.stack([time > 0, time < TIME_TILES - 1])

    entries = key_tiles.size
    names = key_tiles.astype(jnp.bfloat16).reshape(1, entries)
    names = jnp.pad(names, ((0, EXTRA - 1), (0, qkv.shape[2] // 4 - entries)))
    pieces = split(at, qkv, names)
    q_parts = [send(pieces[k], spread_pairs(k)) for k in range(4)]
    kv_pieces = list(pieces[4:])
    for k in range(1, 4):
        q_parts[k], kv_pieces[k] = lax.optimization_barrier((q_parts[k], kv_pieces[k]))
    kv_parts = [send(kv_pieces[k], spread_pairs(k)) for k in range(4)]
    q_own = stack_queries(q_parts)
    q_prev = send(q_own, time_pairs(1))
    q_next = send(q_own, time_pairs(-1))
    place, q_prev, q_next = lax.optimization_barrier((place, q_prev, q_next))
    lists = jnp.stack([q[-EXTRA, :entries] for q in (q_own, q_prev, q_next)])
    lists = lists.astype(jnp.int32).reshape((3,) + key_tiles.shape)
    mask = named(lists, 2 * y + core, pair, time, xh)
    here = jnp.concatenate([jnp.ones((1,), bool), valid])
    mask = (mask & here[:, None, None, None]).astype(jnp.int32).reshape(-1)
    kv_own, edge = stack(place, kv_parts)
    edge_own = send(edge, edge_pairs())
    bodies = (kv_own, send(kv_own, core_pairs()), send(kv_own, column_pairs()))

    begun = attend(mask, (q_own, q_prev, q_next), bodies, (), heads, 0, 0, jnp.float32)
    begun, edge_own = lax.optimization_barrier((begun, edge_own))
    edges = (edge_own, send(edge_own, core_pairs()), send(edge_own, column_pairs()))
    o_prev, o_next = attend(mask, (q_prev, q_next), edges, begun[1:], heads, 1, 6, jnp.bfloat16)
    o_before = send(o_next, time_pairs(1))
    o_after = send(o_prev, time_pairs(-1))
    (o_own,) = attend(mask, (q_own,), edges, begun[:1], heads, 0, 6, jnp.float32)

    chunks = merge(valid.astype(jnp.int32), (o_own, o_before, o_after), heads)
    home = [send(chunks[k], gather_pairs(k)) for k in range(4)]
    return join(at, home)


def solution(mesh):
    placed = (P(None, ("seq", "head"), None), P("head", "seq", None))
    return jax.shard_map(
        local, mesh=mesh, in_specs=placed, out_specs=P(("seq", "head"), None), check_vma=False
    )
```

```python
import functools
import math

import jax
import jax.numpy as jnp
from jax import lax
from jax.experimental import pallas as pl
from jax.experimental.pallas import tpu as pltpu
from jax.sharding import PartitionSpec as P

TIME_TILES = 4
AXES = ("seq", "head")
FAR = -1e30
VMEM_LIMIT = 28 * 2**20
VMEM_SMALL = 12 * 2**20
BATCH = 2
EXTRA = 16
POOL = 9


def linear(y, xh, z, xl, core):
    return ((y * 2 + xh) * 8 + z) * 4 + xl * 2 + core


def devices():
    for y in range(4):
        for xh in range(2):
            for z in range(8):
                for xl in range(2):
                    for core in range(2):
                        yield y, xh, z, xl, core


def spread_pairs(k):
    pairs = []
    for y, xh, z, xl, core in devices():
        group = (2 * xl + core) ^ k
        pairs.append((linear(y, xh, z, xl, core), linear(y, group >> 1, z, group & 1, xh)))
    return pairs


def gather_pairs(k):
    return [(b, a) for a, b in spread_pairs(k)]


def edge_pairs():
    return [(linear(y, xh, z, xl, c), linear(y, xh, z ^ 4, xl, c)) for y, xh, z, xl, c in devices()]


def core_pairs():
    return [(linear(y, xh, z, xl, c), linear(y, xh, z, xl, 1 - c)) for y, xh, z, xl, c in devices()]


def column_pairs():
    pairs = []
    for y, xh, z, xl, core in devices():
        to = y + (1 if core == 1 else -1)
        if 0 <= to < 4:
            pairs.append((linear(y, xh, z, xl, core), linear(to, xh, z, xl, 1 - core)))
    return pairs


def time_pairs(by):
    pairs = []
    for y, xh, z, xl, core in devices():
        if 0 <= z % TIME_TILES + by < TIME_TILES:
            pairs.append((linear(y, xh, z, xl, core), linear(y, xh, z + by, xl, core)))
    return pairs


def send(x, pairs):
    return lax.ppermute(x, AXES, pairs)


def split_kernel(at_ref, qkv_ref, names_ref, *outs):
    width = outs[0].shape[-1]
    rows = qkv_ref.shape[1]
    for k in range(4):
        lanes = pl.ds(pl.multiple_of((at_ref[0] ^ k) * width, 128), width)
        for i in range(3):
            outs[k][i * rows : (i + 1) * rows, :] = qkv_ref[i, :, lanes]
        outs[k][3 * rows :, :] = names_ref[...]


def split(at, qkv, names):
    _, rows, columns = qkv.shape
    vmem = pl.BlockSpec(memory_space=pltpu.VMEM)
    return pl.pallas_call(
        split_kernel,
        out_shape=[jax.ShapeDtypeStruct((3 * rows + EXTRA, columns // 4), qkv.dtype)] * 4,
        in_specs=[pl.BlockSpec(memory_space=pltpu.SMEM), vmem, vmem],
        out_specs=[vmem] * 4,
        compiler_params=pltpu.CompilerParams(vmem_limit_bytes=VMEM_SMALL),
        name="split",
    )(at, qkv, names)


def stack_kernel(place_ref, *refs):
    parts, (q_ref, kv_ref, edge_ref), sems = refs[:4], refs[4:7], refs[7]
    rows = (parts[0].shape[0] - EXTRA) // 3
    copies = []
    for k in range(4):
        at = pl.ds(k * rows, rows)
        targets = (q_ref.at[at], kv_ref.at[0, at], kv_ref.at[1, at])
        for i in range(3):
            copies.append(
                pltpu.make_async_copy(parts[k].at[pl.ds(i * rows, rows)], targets[i], sems.at[3 * k + i])
            )
    into = q_ref.at[pl.ds(4 * rows, EXTRA)]
    copies.append(pltpu.make_async_copy(parts[0].at[pl.ds(3 * rows, EXTRA)], into, sems.at[12]))
    for copy in copies:
        copy.start()
    for copy in copies:
        copy.wait()
    edge_ref[...] = kv_ref[:, pl.ds(pl.multiple_of(place_ref[0] * (2 * rows), 128), 2 * rows), :]


def stack(place, parts):
    rows, width = (parts[0].shape[0] - EXTRA) // 3, parts[0].shape[1]
    vmem = pl.BlockSpec(memory_space=pltpu.VMEM)
    return pl.pallas_call(
        stack_kernel,
        out_shape=[
            jax.ShapeDtypeStruct((4 * rows + EXTRA, width), parts[0].dtype),
            jax.ShapeDtypeStruct((2, 4 * rows, width), parts[0].dtype),
            jax.ShapeDtypeStruct((2, 2 * rows, width), parts[0].dtype),
        ],
        in_specs=[pl.BlockSpec(memory_space=pltpu.SMEM)] + [pl.BlockSpec(memory_space=pl.ANY)] * 4,
        out_specs=[vmem] * 3,
        scratch_shapes=[pltpu.SemaphoreType.DMA((13,))],
        compiler_params=pltpu.CompilerParams(vmem_limit_bytes=VMEM_SMALL),
        name="stack",
    )(place, *parts)


def join_kernel(at_ref, *refs):
    parts, out_ref = refs[:4], refs[4]
    width = parts[0].shape[-1]
    for k in range(4):
        out_ref[:, pl.ds(pl.multiple_of((at_ref[0] ^ k) * width, 128), width)] = parts[k][...]


def join(at, parts):
    rows, width = parts[0].shape
    vmem = pl.BlockSpec(memory_space=pltpu.VMEM)
    return pl.pallas_call(
        join_kernel,
        out_shape=jax.ShapeDtypeStruct((rows, 4 * width), parts[0].dtype),
        in_specs=[pl.BlockSpec(memory_space=pltpu.SMEM)] + [vmem] * 4,
        out_specs=vmem,
        compiler_params=pltpu.CompilerParams(vmem_limit_bytes=VMEM_SMALL),
        name="join",
    )(at, *parts)


def attend_kernel(mask_ref, *refs, sets, pieces, begun, tiles, first_set, first_tile, heads, tile, dim):
    queries = refs[:sets]
    sources = refs[sets : sets + pieces]
    starts = refs[sets + pieces : sets + pieces + begun]
    refs = refs[sets + pieces + begun :]
    outs = refs[:sets]
    pool, held, turned_q, turned_v, max_ref, sum_ref, acc_ref, of_query, of_key = refs[sets : sets + 9]
    rest = refs[sets + 9 :]
    score_refs = (rest[:BATCH], rest[BATCH : 2 * BATCH])
    top_refs = (rest[2 * BATCH : 3 * BATCH], rest[3 * BATCH : 4 * BATCH])
    sems = rest[4 * BATCH]
    count_q = sets * heads * 2

    copies = []
    for n in range(sets):
        copies.append(pltpu.make_async_copy(queries[n].at[pl.ds(0, 2 * tile)], held.at[n], sems.at[n]))
    at = 0
    for source in sources:
        for r in range(source.shape[1] // tile):
            copies.append(
                pltpu.make_async_copy(source.at[:, pl.ds(r * tile, tile)], pool.at[at], sems.at[sets + at])
            )
            at += 1
    for copy in copies:
        copy.start()

    def list_pairs_of(s, count):
        for j in range(tiles):
            of_query[count] = s
            of_key[count] = j
            count = count + mask_ref[(first_set * heads * 2 + s) * POOL + first_tile + j]
        return count

    count = lax.fori_loop(0, count_q, list_pairs_of, 0)
    for i in range(4 * BATCH):
        of_query[count + i] = count_q
        of_key[count + i] = 0
    scale = dim**-0.5
    factor = scale * math.log2(math.e)
    width = heads * dim
    if begun:
        sum_ref[...] = jnp.full_like(sum_ref, 0.125)
        for n in range(sets):
            for h in range(heads):
                lse = starts[n][width + 3 * h : width + 3 * h + 1, :]
                for i in range(1, 3):
                    lse = lse + starts[n][width + 3 * h + i : width + 3 * h + i + 1, :]
                for p in range(2):
                    s = (n * heads + h) * 2 + p
                    at = slice(p * tile, (p + 1) * tile)
                    max_ref[s, :1, :] = lse[:, at] / scale
                    acc_ref[s] = starts[n][h * dim : (h + 1) * dim, at]
        max_ref[count_q] = jnp.zeros((8, tile), jnp.float32)
        acc_ref[count_q] = jnp.zeros((dim, tile), jnp.float32)
    else:
        max_ref[...] = jnp.full_like(max_ref, FAR)
        sum_ref[...] = jnp.zeros_like(sum_ref)
        acc_ref[...] = jnp.zeros_like(acc_ref)
    for copy in copies:
        copy.wait()
    for n in range(sets):
        for h in range(heads):
            for p in range(2):
                turned_q[(n * heads + h) * 2 + p] = jnp.transpose(
                    held[n, p * tile : (p + 1) * tile, h * dim : (h + 1) * dim]
                )
    turned_q[count_q] = turned_q[0]
    for h in range(heads):
        for j in range(tiles):
            turned_v[h * tiles + j] = jnp.transpose(pool[j, 1, :, h * dim : (h + 1) * dim])

    def score(i, out_ref, top_ref):
        s, j = of_query[i], of_key[i]
        h = lax.rem(s // 2, heads)
        keys = pool[j, 0, :, pl.ds(pl.multiple_of(h * dim, dim), dim)]
        scores = jnp.dot(keys, turned_q[s], preferred_element_type=jnp.float32)
        out_ref[...] = scores
        top_ref[...] = jnp.max(scores.reshape(tile // 8, 8, tile), axis=0)

    def weigh(i, in_ref, top_ref):
        s, j = of_query[i], of_key[i]
        h = lax.rem(s // 2, heads)
        old = max_ref[s, :1, :]
        new = jnp.maximum(old, jnp.max(top_ref[...], axis=0, keepdims=True))
        shrink = jnp.exp2((old - new) * factor)
        max_ref[s, :1, :] = new
        weights = jnp.exp2((in_ref[...] - new) * factor)
        sum_ref[s] = sum_ref[s] * shrink + jnp.sum(weights.reshape(tile // 8, 8, tile), axis=0)
        acc_ref[s] = acc_ref[s] * shrink + jnp.dot(
            turned_v[h * tiles + j], weights.astype(jnp.bfloat16), preferred_element_type=jnp.float32
        )

    for u in range(BATCH):
        score(u, score_refs[0][u], top_refs[0][u])

    def step(t, carry):
        for half in range(2):
            base = (2 * t + half) * BATCH
            for u in range(BATCH):
                score(base + BATCH + u, score_refs[1 - half][u], top_refs[1 - half][u])
            for u in range(BATCH):
                weigh(base + u, score_refs[half][u], top_refs[half][u])
        return carry

    lax.fori_loop(0, (count + 2 * BATCH - 1) // (2 * BATCH), step, 0)

    for n in range(sets):
        outs[n][width : width + EXTRA, :] = jnp.zeros((EXTRA, 2 * tile), outs[n].dtype)
        for h in range(heads):
            for p in range(2):
                s = (n * heads + h) * 2 + p
                at = slice(p * tile, (p + 1) * tile)
                total = jnp.maximum(jnp.sum(sum_ref[s], axis=0, keepdims=True), 1e-30)
                outs[n][h * dim : (h + 1) * dim, at] = (acc_ref[s] / total).astype(outs[n].dtype)
                left = max_ref[s, :1, :] * scale + jnp.log(total)
                for i in range(3):
                    part = left.astype(outs[n].dtype)
                    outs[n][width + 3 * h + i : width + 3 * h + i + 1, at] = part
                    left = left - part.astype(jnp.float32)


def attend(mask, queries, sources, starts, heads, first_set, first_tile, out_dtype):
    sets = len(queries)
    brick, width = queries[0].shape[0] - EXTRA, queries[0].shape[1]
    tile = brick // 2
    dim = width // heads
    tiles = sum(source.shape[1] for source in sources) // tile
    count_q = sets * heads * 2
    hbm = pl.BlockSpec(memory_space=pl.ANY)
    vmem = pl.BlockSpec(memory_space=pltpu.VMEM)
    return pl.pallas_call(
        functools.partial(
            attend_kernel,
            sets=sets,
            pieces=len(sources),
            begun=len(starts),
            tiles=tiles,
            first_set=first_set,
            first_tile=first_tile,
            heads=heads,
            tile=tile,
            dim=dim,
        ),
        out_shape=[jax.ShapeDtypeStruct((width + EXTRA, brick), out_dtype)] * sets,
        in_specs=[pl.BlockSpec(memory_space=pltpu.SMEM)] + [hbm] * (sets + len(sources)) + [vmem] * len(starts),
        out_specs=[vmem] * sets,
        scratch_shapes=[
            pltpu.VMEM((tiles, 2, tile, width), jnp.bfloat16),
            pltpu.VMEM((sets, brick, width), jnp.bfloat16),
            pltpu.VMEM((count_q + 1, dim, tile), jnp.bfloat16),
            pltpu.VMEM((tiles * heads, dim, tile), jnp.bfloat16),
            pltpu.VMEM((count_q + 1, 8, tile), jnp.float32),
            pltpu.VMEM((count_q + 1, 8, tile), jnp.float32),
            pltpu.VMEM((count_q + 1, dim, tile), jnp.float32),
            pltpu.SMEM((count_q * tiles + 8 * BATCH,), jnp.int32),
            pltpu.SMEM((count_q * tiles + 8 * BATCH,), jnp.int32),
        ]
        + [pltpu.VMEM((tile, tile), jnp.float32)] * (2 * BATCH)
        + [pltpu.VMEM((8, tile), jnp.float32)] * (2 * BATCH)
        + [pltpu.SemaphoreType.DMA((sets + tiles,))],
        compiler_params=pltpu.CompilerParams(vmem_limit_bytes=VMEM_LIMIT),
        name=f"attend_{sets}_{tiles}",
    )(mask, *queries, *sources, *starts)


def merge_kernel(valid_ref, *refs, heads):
    parts, outs = refs[:3], refs[3:]
    width, brick = parts[0].shape[0] - EXTRA, parts[0].shape[1]
    dim = width // heads
    quarter = brick // 4
    for h in range(heads):
        lse = []
        for i in range(3):
            rows = parts[i][width : width + EXTRA, :].astype(jnp.float32)
            lse.append(rows[3 * h : 3 * h + 1] + rows[3 * h + 1 : 3 * h + 2] + rows[3 * h + 2 : 3 * h + 3])
        lse[1] = jnp.where(valid_ref[0] > 0, lse[1], FAR)
        lse[2] = jnp.where(valid_ref[1] > 0, lse[2], FAR)
        top = jnp.maximum(jnp.maximum(lse[0], lse[1]), lse[2])
        shares = [jnp.exp(x - top) for x in lse]
        total = shares[0] + shares[1] + shares[2]
        lanes = slice(h * dim, (h + 1) * dim)
        merged = parts[0][lanes, :].astype(jnp.float32) * (shares[0] / total)
        merged += parts[1][lanes, :].astype(jnp.float32) * (shares[1] / total)
        merged += parts[2][lanes, :].astype(jnp.float32) * (shares[2] / total)
        merged = jnp.transpose(merged).astype(jnp.bfloat16)
        for k in range(4):
            outs[k][:, lanes] = merged[k * quarter : (k + 1) * quarter, :]


def merge(valid, parts, heads):
    width, brick = parts[0].shape[0] - EXTRA, parts[0].shape[1]
    vmem = pl.BlockSpec(memory_space=pltpu.VMEM)
    return pl.pallas_call(
        functools.partial(merge_kernel, heads=heads),
        out_shape=[jax.ShapeDtypeStruct((brick // 4, width), jnp.bfloat16)] * 4,
        in_specs=[pl.BlockSpec(memory_space=pltpu.SMEM)] + [vmem] * 3,
        out_specs=[vmem] * 4,
        compiler_params=pltpu.CompilerParams(vmem_limit_bytes=VMEM_SMALL),
        name="merge",
    )(valid, *parts)


def named(lists, column, pair, time, xh):
    tile_time = lists // 2 % TIME_TILES
    tile_pair = lists // (2 * TIME_TILES) % 2
    tile_column = lists // (4 * TIME_TILES)
    beside = jnp.where(tile_column == column + 1 - 2 * (column % 2), 1, 2)
    column_slot = jnp.where(tile_column == column, 0, beside)
    slot = jnp.where(tile_pair == pair, column_slot * 2 + ((lists % 2) ^ xh), 6 + column_slot)
    slot = jnp.where((lists >= 0) & (tile_time == time), slot, -1)
    mask = jnp.any(slot[..., None] == jnp.arange(POOL, dtype=jnp.int32), axis=-2)
    return jnp.where(xh == 1, mask[..., ::-1, :], mask)


def local(qkv, key_tiles):
    heads = key_tiles.shape[0]
    seq = lax.axis_index("seq")
    head = lax.axis_index("head")
    y, xh, z = seq // 16, seq // 8 % 2, seq % 8
    core = head % 2
    pair, time = z // TIME_TILES, z % TIME_TILES
    at = head.astype(jnp.int32).reshape(1)
    place = ((1 - pair) ^ xh).astype(jnp.int32).reshape(1)
    valid = jnp.stack([time > 0, time < TIME_TILES - 1])

    entries = key_tiles.size
    names = key_tiles.astype(jnp.bfloat16).reshape(1, entries)
    names = jnp.pad(names, ((0, EXTRA - 1), (0, qkv.shape[2] // 4 - entries)))
    pieces = split(at, qkv, names)
    parts = [send(pieces[k], spread_pairs(k)) for k in range(4)]
    q_own, kv_own, edge = stack(place, parts)
    q_prev = send(q_own, time_pairs(1))
    q_next = send(q_own, time_pairs(-1))
    lists = jnp.stack([q[-EXTRA, :entries] for q in (q_own, q_prev, q_next)])
    lists = lists.astype(jnp.int32).reshape((3,) + key_tiles.shape)
    mask = named(lists, 2 * y + core, pair, time, xh)
    here = jnp.concatenate([jnp.ones((1,), bool), valid])
    mask = (mask & here[:, None, None, None]).astype(jnp.int32).reshape(-1)
    edge_own = send(edge, edge_pairs())
    bodies = (kv_own, send(kv_own, core_pairs()), send(kv_own, column_pairs()))

    begun = attend(mask, (q_own, q_prev, q_next), bodies, (), heads, 0, 0, jnp.float32)
    begun, edge_own = lax.optimization_barrier((begun, edge_own))
    edges = (edge_own, send(edge_own, core_pairs()), send(edge_own, column_pairs()))
    o_prev, o_next = attend(mask, (q_prev, q_next), edges, begun[1:], heads, 1, 6, jnp.bfloat16)
    o_before = send(o_next, time_pairs(1))
    o_after = send(o_prev, time_pairs(-1))
    (o_own,) = attend(mask, (q_own,), edges, begun[:1], heads, 0, 6, jnp.float32)

    chunks = merge(valid.astype(jnp.int32), (o_own, o_before, o_after), heads)
    home = [send(chunks[k], gather_pairs(k)) for k in range(4)]
    return join(at, home)


def solution(mesh):
    placed = (P(None, ("seq", "head"), None), P("head", "seq", None))
    return jax.shard_map(
        local, mesh=mesh, in_specs=placed, out_specs=P(("seq", "head"), None), check_vma=False
    )
```

```python
import functools
import math

import jax
import jax.numpy as jnp
from jax import lax
from jax.experimental import pallas as pl
from jax.experimental.pallas import tpu as pltpu
from jax.sharding import PartitionSpec as P

TIME_TILES = 4
AXES = ("seq", "head")
FAR = -1e30
VMEM_LIMIT = 28 * 2**20
VMEM_SMALL = 12 * 2**20
BATCH = 2
EXTRA = 16
POOL = 9


def linear(y, xh, z, xl, core):
    return ((y * 2 + xh) * 8 + z) * 4 + xl * 2 + core


def devices():
    for y in range(4):
        for xh in range(2):
            for z in range(8):
                for xl in range(2):
                    for core in range(2):
                        yield y, xh, z, xl, core


def spread_pairs(k):
    pairs = []
    for y, xh, z, xl, core in devices():
        group = (2 * xl + core) ^ k
        pairs.append((linear(y, xh, z, xl, core), linear(y, group >> 1, z, group & 1, xh)))
    return pairs


def gather_pairs(k):
    return [(b, a) for a, b in spread_pairs(k)]


def edge_pairs():
    return [(linear(y, xh, z, xl, c), linear(y, xh, z ^ 4, xl, c)) for y, xh, z, xl, c in devices()]


def core_pairs():
    return [(linear(y, xh, z, xl, c), linear(y, xh, z, xl, 1 - c)) for y, xh, z, xl, c in devices()]


def column_pairs():
    pairs = []
    for y, xh, z, xl, core in devices():
        to = y + (1 if core == 1 else -1)
        if 0 <= to < 4:
            pairs.append((linear(y, xh, z, xl, core), linear(to, xh, z, xl, 1 - core)))
    return pairs


def time_pairs(by):
    pairs = []
    for y, xh, z, xl, core in devices():
        if 0 <= z % TIME_TILES + by < TIME_TILES:
            pairs.append((linear(y, xh, z, xl, core), linear(y, xh, z + by, xl, core)))
    return pairs


def send(x, pairs):
    return lax.ppermute(x, AXES, pairs)


def split_kernel(at_ref, qkv_ref, names_ref, *outs):
    width = outs[0].shape[-1]
    rows = qkv_ref.shape[1]
    for k in range(4):
        lanes = pl.ds(pl.multiple_of((at_ref[0] ^ k) * width, 128), width)
        outs[k][:rows, :] = qkv_ref[0, :, lanes]
        outs[k][rows:, :] = names_ref[...]
        outs[4 + k][...] = qkv_ref[1:3, :, lanes]


def split(at, qkv, names):
    _, rows, columns = qkv.shape
    width = columns // 4
    vmem = pl.BlockSpec(memory_space=pltpu.VMEM)
    shapes = [jax.ShapeDtypeStruct((rows + EXTRA, width), qkv.dtype)] * 4
    shapes += [jax.ShapeDtypeStruct((2, rows, width), qkv.dtype)] * 4
    return pl.pallas_call(
        split_kernel,
        out_shape=shapes,
        in_specs=[pl.BlockSpec(memory_space=pltpu.SMEM), vmem, vmem],
        out_specs=[vmem] * 8,
        compiler_params=pltpu.CompilerParams(vmem_limit_bytes=VMEM_SMALL),
        name="split",
    )(at, qkv, names)


def stack_kernel(place_ref, *refs):
    parts, kv_ref, edge_ref, sems = refs[:4], refs[4], refs[5], refs[6]
    rows = parts[0].shape[1]
    copies = []
    for k in range(4):
        copies.append(pltpu.make_async_copy(parts[k], kv_ref.at[:, pl.ds(k * rows, rows)], sems.at[k]))
    for copy in copies:
        copy.start()
    for copy in copies:
        copy.wait()
    edge_ref[...] = kv_ref[:, pl.ds(pl.multiple_of(place_ref[0] * (2 * rows), 128), 2 * rows), :]


def stack(place, parts):
    _, rows, width = parts[0].shape
    vmem = pl.BlockSpec(memory_space=pltpu.VMEM)
    return pl.pallas_call(
        stack_kernel,
        out_shape=[
            jax.ShapeDtypeStruct((2, 4 * rows, width), parts[0].dtype),
            jax.ShapeDtypeStruct((2, 2 * rows, width), parts[0].dtype),
        ],
        in_specs=[pl.BlockSpec(memory_space=pltpu.SMEM)] + [pl.BlockSpec(memory_space=pl.ANY)] * 4,
        out_specs=[vmem] * 2,
        scratch_shapes=[pltpu.SemaphoreType.DMA((4,))],
        compiler_params=pltpu.CompilerParams(vmem_limit_bytes=VMEM_SMALL),
        name="stack",
    )(place, *parts)


def stack_queries_kernel(*refs):
    parts, q_ref, sems = refs[:4], refs[4], refs[5]
    rows = parts[0].shape[0] - EXTRA
    copies = []
    for k in range(4):
        into = q_ref.at[pl.ds(k * rows, rows)]
        copies.append(pltpu.make_async_copy(parts[k].at[pl.ds(0, rows)], into, sems.at[k]))
    into = q_ref.at[pl.ds(4 * rows, EXTRA)]
    copies.append(pltpu.make_async_copy(parts[0].at[pl.ds(rows, EXTRA)], into, sems.at[4]))
    for copy in copies:
        copy.start()
    for copy in copies:
        copy.wait()


def stack_queries(parts):
    rows, width = parts[0].shape[0] - EXTRA, parts[0].shape[1]
    return pl.pallas_call(
        stack_queries_kernel,
        out_shape=jax.ShapeDtypeStruct((4 * rows + EXTRA, width), parts[0].dtype),
        in_specs=[pl.BlockSpec(memory_space=pl.ANY)] * 4,
        out_specs=pl.BlockSpec(memory_space=pltpu.VMEM),
        scratch_shapes=[pltpu.SemaphoreType.DMA((5,))],
        compiler_params=pltpu.CompilerParams(vmem_limit_bytes=VMEM_SMALL),
        name="stack_queries",
    )(*parts)


def join_kernel(at_ref, *refs):
    parts, out_ref = refs[:4], refs[4]
    width = parts[0].shape[-1]
    for k in range(4):
        out_ref[:, pl.ds(pl.multiple_of((at_ref[0] ^ k) * width, 128), width)] = parts[k][...]


def join(at, parts):
    rows, width = parts[0].shape
    vmem = pl.BlockSpec(memory_space=pltpu.VMEM)
    return pl.pallas_call(
        join_kernel,
        out_shape=jax.ShapeDtypeStruct((rows, 4 * width), parts[0].dtype),
        in_specs=[pl.BlockSpec(memory_space=pltpu.SMEM)] + [vmem] * 4,
        out_specs=vmem,
        compiler_params=pltpu.CompilerParams(vmem_limit_bytes=VMEM_SMALL),
        name="join",
    )(at, *parts)


def attend_kernel(mask_ref, *refs, sets, pieces, begun, tiles, first_set, first_tile, heads, tile, dim):
    queries = refs[:sets]
    sources = refs[sets : sets + pieces]
    starts = refs[sets + pieces : sets + pieces + begun]
    refs = refs[sets + pieces + begun :]
    outs = refs[:sets]
    pool, held, turned_q, turned_v, max_ref, sum_ref, acc_ref, of_query, of_key = refs[sets : sets + 9]
    rest = refs[sets + 9 :]
    score_refs = (rest[:BATCH], rest[BATCH : 2 * BATCH])
    top_refs = (rest[2 * BATCH : 3 * BATCH], rest[3 * BATCH : 4 * BATCH])
    sems = rest[4 * BATCH]
    count_q = sets * heads * 2

    copies = []
    for n in range(sets):
        copies.append(pltpu.make_async_copy(queries[n].at[pl.ds(0, 2 * tile)], held.at[n], sems.at[n]))
    at = 0
    for source in sources:
        for r in range(source.shape[1] // tile):
            copies.append(
                pltpu.make_async_copy(source.at[:, pl.ds(r * tile, tile)], pool.at[at], sems.at[sets + at])
            )
            at += 1
    for copy in copies:
        copy.start()

    def list_pairs_of(s, count):
        for j in range(tiles):
            of_query[count] = s
            of_key[count] = j
            count = count + mask_ref[(first_set * heads * 2 + s) * POOL + first_tile + j]
        return count

    count = lax.fori_loop(0, count_q, list_pairs_of, 0)
    for i in range(4 * BATCH):
        of_query[count + i] = count_q
        of_key[count + i] = 0
    scale = dim**-0.5
    factor = scale * math.log2(math.e)
    width = heads * dim
    if begun:
        sum_ref[...] = jnp.full_like(sum_ref, 0.125)
        for n in range(sets):
            for h in range(heads):
                lse = starts[n][width + 3 * h : width + 3 * h + 1, :]
                for i in range(1, 3):
                    lse = lse + starts[n][width + 3 * h + i : width + 3 * h + i + 1, :]
                for p in range(2):
                    s = (n * heads + h) * 2 + p
                    at = slice(p * tile, (p + 1) * tile)
                    max_ref[s, :1, :] = lse[:, at] / scale
                    acc_ref[s] = starts[n][h * dim : (h + 1) * dim, at]
        max_ref[count_q] = jnp.zeros((8, tile), jnp.float32)
        acc_ref[count_q] = jnp.zeros((dim, tile), jnp.float32)
    else:
        max_ref[...] = jnp.full_like(max_ref, FAR)
        sum_ref[...] = jnp.zeros_like(sum_ref)
        acc_ref[...] = jnp.zeros_like(acc_ref)
    for copy in copies:
        copy.wait()
    for n in range(sets):
        for h in range(heads):
            for p in range(2):
                turned_q[(n * heads + h) * 2 + p] = jnp.transpose(
                    held[n, p * tile : (p + 1) * tile, h * dim : (h + 1) * dim]
                )
    turned_q[count_q] = turned_q[0]
    for h in range(heads):
        for j in range(tiles):
            turned_v[h * tiles + j] = jnp.transpose(pool[j, 1, :, h * dim : (h + 1) * dim])

    def score(i, out_ref, top_ref):
        s, j = of_query[i], of_key[i]
        h = lax.rem(s // 2, heads)
        keys = pool[j, 0, :, pl.ds(pl.multiple_of(h * dim, dim), dim)]
        scores = jnp.dot(keys, turned_q[s], preferred_element_type=jnp.float32)
        out_ref[...] = scores
        top_ref[...] = jnp.max(scores.reshape(tile // 8, 8, tile), axis=0)

    def weigh(i, in_ref, top_ref):
        s, j = of_query[i], of_key[i]
        h = lax.rem(s // 2, heads)
        old = max_ref[s, :1, :]
        new = jnp.maximum(old, jnp.max(top_ref[...], axis=0, keepdims=True))
        shrink = jnp.exp2((old - new) * factor)
        max_ref[s, :1, :] = new
        weights = jnp.exp2((in_ref[...] - new) * factor)
        sum_ref[s] = sum_ref[s] * shrink + jnp.sum(weights.reshape(tile // 8, 8, tile), axis=0)
        acc_ref[s] = acc_ref[s] * shrink + jnp.dot(
            turned_v[h * tiles + j], weights.astype(jnp.bfloat16), preferred_element_type=jnp.float32
        )

    for u in range(BATCH):
        score(u, score_refs[0][u], top_refs[0][u])

    def step(t, carry):
        for half in range(2):
            base = (2 * t + half) * BATCH
            for u in range(BATCH):
                score(base + BATCH + u, score_refs[1 - half][u], top_refs[1 - half][u])
            for u in range(BATCH):
                weigh(base + u, score_refs[half][u], top_refs[half][u])
        return carry

    lax.fori_loop(0, (count + 2 * BATCH - 1) // (2 * BATCH), step, 0)

    for n in range(sets):
        outs[n][width : width + EXTRA, :] = jnp.zeros((EXTRA, 2 * tile), outs[n].dtype)
        for h in range(heads):
            for p in range(2):
                s = (n * heads + h) * 2 + p
                at = slice(p * tile, (p + 1) * tile)
                total = jnp.maximum(jnp.sum(sum_ref[s], axis=0, keepdims=True), 1e-30)
                outs[n][h * dim : (h + 1) * dim, at] = (acc_ref[s] / total).astype(outs[n].dtype)
                left = max_ref[s, :1, :] * scale + jnp.log(total)
                for i in range(3):
                    part = left.astype(outs[n].dtype)
                    outs[n][width + 3 * h + i : width + 3 * h + i + 1, at] = part
                    left = left - part.astype(jnp.float32)


def attend(mask, queries, sources, starts, heads, first_set, first_tile, out_dtype):
    sets = len(queries)
    brick, width = queries[0].shape[0] - EXTRA, queries[0].shape[1]
    tile = brick // 2
    dim = width // heads
    tiles = sum(source.shape[1] for source in sources) // tile
    count_q = sets * heads * 2
    hbm = pl.BlockSpec(memory_space=pl.ANY)
    vmem = pl.BlockSpec(memory_space=pltpu.VMEM)
    return pl.pallas_call(
        functools.partial(
            attend_kernel,
            sets=sets,
            pieces=len(sources),
            begun=len(starts),
            tiles=tiles,
            first_set=first_set,
            first_tile=first_tile,
            heads=heads,
            tile=tile,
            dim=dim,
        ),
        out_shape=[jax.ShapeDtypeStruct((width + EXTRA, brick), out_dtype)] * sets,
        in_specs=[pl.BlockSpec(memory_space=pltpu.SMEM)] + [hbm] * (sets + len(sources)) + [vmem] * len(starts),
        out_specs=[vmem] * sets,
        scratch_shapes=[
            pltpu.VMEM((tiles, 2, tile, width), jnp.bfloat16),
            pltpu.VMEM((sets, brick, width), jnp.bfloat16),
            pltpu.VMEM((count_q + 1, dim, tile), jnp.bfloat16),
            pltpu.VMEM((tiles * heads, dim, tile), jnp.bfloat16),
            pltpu.VMEM((count_q + 1, 8, tile), jnp.float32),
            pltpu.VMEM((count_q + 1, 8, tile), jnp.float32),
            pltpu.VMEM((count_q + 1, dim, tile), jnp.float32),
            pltpu.SMEM((count_q * tiles + 8 * BATCH,), jnp.int32),
            pltpu.SMEM((count_q * tiles + 8 * BATCH,), jnp.int32),
        ]
        + [pltpu.VMEM((tile, tile), jnp.float32)] * (2 * BATCH)
        + [pltpu.VMEM((8, tile), jnp.float32)] * (2 * BATCH)
        + [pltpu.SemaphoreType.DMA((sets + tiles,))],
        compiler_params=pltpu.CompilerParams(vmem_limit_bytes=VMEM_LIMIT),
        name=f"attend_{sets}_{tiles}",
    )(mask, *queries, *sources, *starts)


def merge_kernel(valid_ref, *refs, heads):
    parts, outs = refs[:3], refs[3:]
    width, brick = parts[0].shape[0] - EXTRA, parts[0].shape[1]
    dim = width // heads
    quarter = brick // 4
    for h in range(heads):
        lse = []
        for i in range(3):
            rows = parts[i][width : width + EXTRA, :].astype(jnp.float32)
            lse.append(rows[3 * h : 3 * h + 1] + rows[3 * h + 1 : 3 * h + 2] + rows[3 * h + 2 : 3 * h + 3])
        lse[1] = jnp.where(valid_ref[0] > 0, lse[1], FAR)
        lse[2] = jnp.where(valid_ref[1] > 0, lse[2], FAR)
        top = jnp.maximum(jnp.maximum(lse[0], lse[1]), lse[2])
        shares = [jnp.exp(x - top) for x in lse]
        total = shares[0] + shares[1] + shares[2]
        lanes = slice(h * dim, (h + 1) * dim)
        merged = parts[0][lanes, :].astype(jnp.float32) * (shares[0] / total)
        merged += parts[1][lanes, :].astype(jnp.float32) * (shares[1] / total)
        merged += parts[2][lanes, :].astype(jnp.float32) * (shares[2] / total)
        merged = jnp.transpose(merged).astype(jnp.bfloat16)
        for k in range(4):
            outs[k][:, lanes] = merged[k * quarter : (k + 1) * quarter, :]


def merge(valid, parts, heads):
    width, brick = parts[0].shape[0] - EXTRA, parts[0].shape[1]
    vmem = pl.BlockSpec(memory_space=pltpu.VMEM)
    return pl.pallas_call(
        functools.partial(merge_kernel, heads=heads),
        out_shape=[jax.ShapeDtypeStruct((brick // 4, width), jnp.bfloat16)] * 4,
        in_specs=[pl.BlockSpec(memory_space=pltpu.SMEM)] + [vmem] * 3,
        out_specs=[vmem] * 4,
        compiler_params=pltpu.CompilerParams(vmem_limit_bytes=VMEM_SMALL),
        name="merge",
    )(valid, *parts)


def named(lists, column, pair, time, xh):
    tile_time = lists // 2 % TIME_TILES
    tile_pair = lists // (2 * TIME_TILES) % 2
    tile_column = lists // (4 * TIME_TILES)
    beside = jnp.where(tile_column == column + 1 - 2 * (column % 2), 1, 2)
    column_slot = jnp.where(tile_column == column, 0, beside)
    slot = jnp.where(tile_pair == pair, column_slot * 2 + ((lists % 2) ^ xh), 6 + column_slot)
    slot = jnp.where((lists >= 0) & (tile_time == time), slot, -1)
    mask = jnp.any(slot[..., None] == jnp.arange(POOL, dtype=jnp.int32), axis=-2)
    return jnp.where(xh == 1, mask[..., ::-1, :], mask)


def local(qkv, key_tiles):
    heads = key_tiles.shape[0]
    seq = lax.axis_index("seq")
    head = lax.axis_index("head")
    y, xh, z = seq // 16, seq // 8 % 2, seq % 8
    core = head % 2
    pair, time = z // TIME_TILES, z % TIME_TILES
    at = head.astype(jnp.int32).reshape(1)
    place = ((1 - pair) ^ xh).astype(jnp.int32).reshape(1)
    valid = jnp.stack([time > 0, time < TIME_TILES - 1])

    entries = key_tiles.size
    names = key_tiles.astype(jnp.bfloat16).reshape(1, entries)
    names = jnp.pad(names, ((0, EXTRA - 1), (0, qkv.shape[2] // 4 - entries)))
    pieces = split(at, qkv, names)
    q_parts = [send(pieces[k], spread_pairs(k)) for k in range(4)]
    kv_pieces = list(pieces[4:])
    for k in range(1, 4):
        q_parts[k], kv_pieces[k] = lax.optimization_barrier((q_parts[k], kv_pieces[k]))
    kv_parts = [send(kv_pieces[k], spread_pairs(k)) for k in range(4)]
    q_own = stack_queries(q_parts)
    q_prev = send(q_own, time_pairs(1))
    q_next = send(q_own, time_pairs(-1))
    place, q_prev, q_next = lax.optimization_barrier((place, q_prev, q_next))
    lists = jnp.stack([q[-EXTRA, :entries] for q in (q_own, q_prev, q_next)])
    lists = lists.astype(jnp.int32).reshape((3,) + key_tiles.shape)
    mask = named(lists, 2 * y + core, pair, time, xh)
    here = jnp.concatenate([jnp.ones((1,), bool), valid])
    mask = (mask & here[:, None, None, None]).astype(jnp.int32).reshape(-1)
    kv_own, edge = stack(place, kv_parts)
    edge_own = send(edge, edge_pairs())
    bodies = (kv_own, send(kv_own, core_pairs()), send(kv_own, column_pairs()))

    begun = attend(mask, (q_prev, q_next), bodies, (), heads, 1, 0, jnp.float32)
    begun, edge_own = lax.optimization_barrier((begun, edge_own))
    edges = (edge_own, send(edge_own, core_pairs()), send(edge_own, column_pairs()))
    o_prev, o_next = attend(mask, (q_prev, q_next), edges, begun, heads, 1, 6, jnp.bfloat16)
    o_before = send(o_next, time_pairs(1))
    o_after = send(o_prev, time_pairs(-1))
    (o_own,) = attend(mask, (q_own,), bodies + edges, (), heads, 0, 0, jnp.float32)

    chunks = merge(valid.astype(jnp.int32), (o_own, o_before, o_after), heads)
    home = [send(chunks[k], gather_pairs(k)) for k in range(4)]
    return join(at, home)


def solution(mesh):
    placed = (P(None, ("seq", "head"), None), P("head", "seq", None))
    return jax.shard_map(
        local, mesh=mesh, in_specs=placed, out_specs=P(("seq", "head"), None), check_vma=False
    )
```

```python
import functools
import math

import jax
import jax.numpy as jnp
from jax import lax
from jax.experimental import pallas as pl
from jax.experimental.pallas import tpu as pltpu
from jax.sharding import PartitionSpec as P

TIME_TILES = 4
AXES = ("seq", "head")
FAR = -1e30
VMEM_LIMIT = 28 * 2**20
VMEM_SMALL = 12 * 2**20
BATCH = 2
EXTRA = 16
POOL = 9


def linear(y, xh, z, xl, core):
    return ((y * 2 + xh) * 8 + z) * 4 + xl * 2 + core


def devices():
    for y in range(4):
        for xh in range(2):
            for z in range(8):
                for xl in range(2):
                    for core in range(2):
                        yield y, xh, z, xl, core


def spread_pairs(k):
    pairs = []
    for y, xh, z, xl, core in devices():
        group = (2 * xl + core) ^ k
        pairs.append((linear(y, xh, z, xl, core), linear(y, group >> 1, z, group & 1, xh)))
    return pairs


def gather_pairs(k):
    return [(b, a) for a, b in spread_pairs(k)]


def edge_pairs():
    return [(linear(y, xh, z, xl, c), linear(y, xh, z ^ 4, xl, c)) for y, xh, z, xl, c in devices()]


def core_pairs():
    return [(linear(y, xh, z, xl, c), linear(y, xh, z, xl, 1 - c)) for y, xh, z, xl, c in devices()]


def column_pairs():
    pairs = []
    for y, xh, z, xl, core in devices():
        to = y + (1 if core == 1 else -1)
        if 0 <= to < 4:
            pairs.append((linear(y, xh, z, xl, core), linear(to, xh, z, xl, 1 - core)))
    return pairs


def time_pairs(by):
    pairs = []
    for y, xh, z, xl, core in devices():
        if 0 <= z % TIME_TILES + by < TIME_TILES:
            pairs.append((linear(y, xh, z, xl, core), linear(y, xh, z + by, xl, core)))
    return pairs


def send(x, pairs):
    return lax.ppermute(x, AXES, pairs)


def split_kernel(at_ref, qkv_ref, names_ref, *outs):
    width = outs[0].shape[-1]
    rows = qkv_ref.shape[1]
    for k in range(4):
        lanes = pl.ds(pl.multiple_of((at_ref[0] ^ k) * width, 128), width)
        outs[k][:rows, :] = qkv_ref[0, :, lanes]
        outs[k][rows:, :] = names_ref[...]
        outs[4 + k][...] = qkv_ref[1:3, :, lanes]


def split(at, qkv, names):
    _, rows, columns = qkv.shape
    width = columns // 4
    vmem = pl.BlockSpec(memory_space=pltpu.VMEM)
    shapes = [jax.ShapeDtypeStruct((rows + EXTRA, width), qkv.dtype)] * 4
    shapes += [jax.ShapeDtypeStruct((2, rows, width), qkv.dtype)] * 4
    return pl.pallas_call(
        split_kernel,
        out_shape=shapes,
        in_specs=[pl.BlockSpec(memory_space=pltpu.SMEM), vmem, vmem],
        out_specs=[vmem] * 8,
        compiler_params=pltpu.CompilerParams(vmem_limit_bytes=VMEM_SMALL),
        name="split",
    )(at, qkv, names)


def stack_kernel(place_ref, *refs):
    parts, kv_ref, edge_ref, sems = refs[:4], refs[4], refs[5], refs[6]
    rows = parts[0].shape[1]
    copies = []
    for k in range(4):
        copies.append(pltpu.make_async_copy(parts[k], kv_ref.at[:, pl.ds(k * rows, rows)], sems.at[k]))
    for copy in copies:
        copy.start()
    for copy in copies:
        copy.wait()
    edge_ref[...] = kv_ref[:, pl.ds(pl.multiple_of(place_ref[0] * (2 * rows), 128), 2 * rows), :]


def stack(place, parts):
    _, rows, width = parts[0].shape
    vmem = pl.BlockSpec(memory_space=pltpu.VMEM)
    return pl.pallas_call(
        stack_kernel,
        out_shape=[
            jax.ShapeDtypeStruct((2, 4 * rows, width), parts[0].dtype),
            jax.ShapeDtypeStruct((2, 2 * rows, width), parts[0].dtype),
        ],
        in_specs=[pl.BlockSpec(memory_space=pltpu.SMEM)] + [pl.BlockSpec(memory_space=pl.ANY)] * 4,
        out_specs=[vmem] * 2,
        scratch_shapes=[pltpu.SemaphoreType.DMA((4,))],
        compiler_params=pltpu.CompilerParams(vmem_limit_bytes=VMEM_SMALL),
        name="stack",
    )(place, *parts)


def stack_queries_kernel(*refs):
    parts, q_ref, sems = refs[:4], refs[4], refs[5]
    rows = parts[0].shape[0] - EXTRA
    copies = []
    for k in range(4):
        into = q_ref.at[pl.ds(k * rows, rows)]
        copies.append(pltpu.make_async_copy(parts[k].at[pl.ds(0, rows)], into, sems.at[k]))
    into = q_ref.at[pl.ds(4 * rows, EXTRA)]
    copies.append(pltpu.make_async_copy(parts[0].at[pl.ds(rows, EXTRA)], into, sems.at[4]))
    for copy in copies:
        copy.start()
    for copy in copies:
        copy.wait()


def stack_queries(parts):
    rows, width = parts[0].shape[0] - EXTRA, parts[0].shape[1]
    return pl.pallas_call(
        stack_queries_kernel,
        out_shape=jax.ShapeDtypeStruct((4 * rows + EXTRA, width), parts[0].dtype),
        in_specs=[pl.BlockSpec(memory_space=pl.ANY)] * 4,
        out_specs=pl.BlockSpec(memory_space=pltpu.VMEM),
        scratch_shapes=[pltpu.SemaphoreType.DMA((5,))],
        compiler_params=pltpu.CompilerParams(vmem_limit_bytes=VMEM_SMALL),
        name="stack_queries",
    )(*parts)


def join_kernel(at_ref, *refs):
    parts, out_ref = refs[:4], refs[4]
    width = parts[0].shape[-1]
    for k in range(4):
        out_ref[:, pl.ds(pl.multiple_of((at_ref[0] ^ k) * width, 128), width)] = parts[k][...]


def join(at, parts):
    rows, width = parts[0].shape
    vmem = pl.BlockSpec(memory_space=pltpu.VMEM)
    return pl.pallas_call(
        join_kernel,
        out_shape=jax.ShapeDtypeStruct((rows, 4 * width), parts[0].dtype),
        in_specs=[pl.BlockSpec(memory_space=pltpu.SMEM)] + [vmem] * 4,
        out_specs=vmem,
        compiler_params=pltpu.CompilerParams(vmem_limit_bytes=VMEM_SMALL),
        name="join",
    )(at, *parts)


def attend_kernel(mask_ref, *refs, sets, pieces, begun, tiles, first_set, first_tile, heads, tile, dim):
    queries = refs[:sets]
    sources = refs[sets : sets + pieces]
    starts = refs[sets + pieces : sets + pieces + begun]
    refs = refs[sets + pieces + begun :]
    outs = refs[:sets]
    pool, held, turned_q, turned_v, max_ref, sum_ref, acc_ref, of_query, of_key = refs[sets : sets + 9]
    rest = refs[sets + 9 :]
    score_refs = (rest[:BATCH], rest[BATCH : 2 * BATCH])
    top_refs = (rest[2 * BATCH : 3 * BATCH], rest[3 * BATCH : 4 * BATCH])
    sems = rest[4 * BATCH]
    count_q = sets * heads * 2

    copies = []
    for n in range(sets):
        copies.append(pltpu.make_async_copy(queries[n].at[pl.ds(0, 2 * tile)], held.at[n], sems.at[n]))
    at = 0
    for source in sources:
        for r in range(source.shape[1] // tile):
            copies.append(
                pltpu.make_async_copy(source.at[:, pl.ds(r * tile, tile)], pool.at[at], sems.at[sets + at])
            )
            at += 1
    for copy in copies:
        copy.start()

    def list_pairs_of(s, count):
        for j in range(tiles):
            of_query[count] = s
            of_key[count] = j
            count = count + mask_ref[(first_set * heads * 2 + s) * POOL + first_tile + j]
        return count

    count = lax.fori_loop(0, count_q, list_pairs_of, 0)
    for i in range(4 * BATCH):
        of_query[count + i] = count_q
        of_key[count + i] = 0
    scale = dim**-0.5
    factor = scale * math.log2(math.e)
    width = heads * dim
    if begun:
        sum_ref[...] = jnp.full_like(sum_ref, 0.125)
        for n in range(sets):
            for h in range(heads):
                lse = starts[n][width + 3 * h : width + 3 * h + 1, :]
                for i in range(1, 3):
                    lse = lse + starts[n][width + 3 * h + i : width + 3 * h + i + 1, :]
                for p in range(2):
                    s = (n * heads + h) * 2 + p
                    at = slice(p * tile, (p + 1) * tile)
                    max_ref[s, :1, :] = lse[:, at] / scale
                    acc_ref[s] = starts[n][h * dim : (h + 1) * dim, at]
        max_ref[count_q] = jnp.zeros((8, tile), jnp.float32)
        acc_ref[count_q] = jnp.zeros((dim, tile), jnp.float32)
    else:
        max_ref[...] = jnp.full_like(max_ref, FAR)
        sum_ref[...] = jnp.zeros_like(sum_ref)
        acc_ref[...] = jnp.zeros_like(acc_ref)
    for copy in copies:
        copy.wait()
    for n in range(sets):
        for h in range(heads):
            for p in range(2):
                turned_q[(n * heads + h) * 2 + p] = jnp.transpose(
                    held[n, p * tile : (p + 1) * tile, h * dim : (h + 1) * dim]
                )
    turned_q[count_q] = turned_q[0]
    for h in range(heads):
        for j in range(tiles):
            turned_v[h * tiles + j] = jnp.transpose(pool[j, 1, :, h * dim : (h + 1) * dim])

    def score(i, out_ref, top_ref):
        s, j = of_query[i], of_key[i]
        h = lax.rem(s // 2, heads)
        keys = pool[j, 0, :, pl.ds(pl.multiple_of(h * dim, dim), dim)]
        scores = jnp.dot(keys, turned_q[s], preferred_element_type=jnp.float32)
        out_ref[...] = scores
        top_ref[...] = jnp.max(scores.reshape(tile // 8, 8, tile), axis=0)

    def weigh(i, in_ref, top_ref):
        s, j = of_query[i], of_key[i]
        h = lax.rem(s // 2, heads)
        old = max_ref[s, :1, :]
        new = jnp.maximum(old, jnp.max(top_ref[...], axis=0, keepdims=True))
        shrink = jnp.exp2((old - new) * factor)
        max_ref[s, :1, :] = new
        weights = jnp.exp2((in_ref[...] - new) * factor)
        sum_ref[s] = sum_ref[s] * shrink + jnp.sum(weights.reshape(tile // 8, 8, tile), axis=0)
        acc_ref[s] = acc_ref[s] * shrink + jnp.dot(
            turned_v[h * tiles + j], weights.astype(jnp.bfloat16), preferred_element_type=jnp.float32
        )

    for u in range(BATCH):
        score(u, score_refs[0][u], top_refs[0][u])

    def step(t, carry):
        for half in range(2):
            base = (2 * t + half) * BATCH
            for u in range(BATCH):
                score(base + BATCH + u, score_refs[1 - half][u], top_refs[1 - half][u])
            for u in range(BATCH):
                weigh(base + u, score_refs[half][u], top_refs[half][u])
        return carry

    lax.fori_loop(0, (count + 2 * BATCH - 1) // (2 * BATCH), step, 0)

    for n in range(sets):
        outs[n][width : width + EXTRA, :] = jnp.zeros((EXTRA, 2 * tile), outs[n].dtype)
        for h in range(heads):
            for p in range(2):
                s = (n * heads + h) * 2 + p
                at = slice(p * tile, (p + 1) * tile)
                total = jnp.maximum(jnp.sum(sum_ref[s], axis=0, keepdims=True), 1e-30)
                outs[n][h * dim : (h + 1) * dim, at] = (acc_ref[s] / total).astype(outs[n].dtype)
                left = max_ref[s, :1, :] * scale + jnp.log(total)
                for i in range(3):
                    part = left.astype(outs[n].dtype)
                    outs[n][width + 3 * h + i : width + 3 * h + i + 1, at] = part
                    left = left - part.astype(jnp.float32)


def attend(mask, queries, sources, starts, heads, first_set, first_tile, out_dtype):
    sets = len(queries)
    brick, width = queries[0].shape[0] - EXTRA, queries[0].shape[1]
    tile = brick // 2
    dim = width // heads
    tiles = sum(source.shape[1] for source in sources) // tile
    count_q = sets * heads * 2
    hbm = pl.BlockSpec(memory_space=pl.ANY)
    vmem = pl.BlockSpec(memory_space=pltpu.VMEM)
    return pl.pallas_call(
        functools.partial(
            attend_kernel,
            sets=sets,
            pieces=len(sources),
            begun=len(starts),
            tiles=tiles,
            first_set=first_set,
            first_tile=first_tile,
            heads=heads,
            tile=tile,
            dim=dim,
        ),
        out_shape=[jax.ShapeDtypeStruct((width + EXTRA, brick), out_dtype)] * sets,
        in_specs=[pl.BlockSpec(memory_space=pltpu.SMEM)] + [hbm] * (sets + len(sources)) + [vmem] * len(starts),
        out_specs=[vmem] * sets,
        scratch_shapes=[
            pltpu.VMEM((tiles, 2, tile, width), jnp.bfloat16),
            pltpu.VMEM((sets, brick, width), jnp.bfloat16),
            pltpu.VMEM((count_q + 1, dim, tile), jnp.bfloat16),
            pltpu.VMEM((tiles * heads, dim, tile), jnp.bfloat16),
            pltpu.VMEM((count_q + 1, 8, tile), jnp.float32),
            pltpu.VMEM((count_q + 1, 8, tile), jnp.float32),
            pltpu.VMEM((count_q + 1, dim, tile), jnp.float32),
            pltpu.SMEM((count_q * tiles + 8 * BATCH,), jnp.int32),
            pltpu.SMEM((count_q * tiles + 8 * BATCH,), jnp.int32),
        ]
        + [pltpu.VMEM((tile, tile), jnp.float32)] * (2 * BATCH)
        + [pltpu.VMEM((8, tile), jnp.float32)] * (2 * BATCH)
        + [pltpu.SemaphoreType.DMA((sets + tiles,))],
        compiler_params=pltpu.CompilerParams(vmem_limit_bytes=VMEM_LIMIT),
        name=f"attend_{sets}_{tiles}",
    )(mask, *queries, *sources, *starts)


def merge_kernel(valid_ref, *refs, heads):
    parts, outs = refs[:3], refs[3:]
    width, brick = parts[0].shape[0] - EXTRA, parts[0].shape[1]
    dim = width // heads
    quarter = brick // 4
    for h in range(heads):
        lse = []
        for i in range(3):
            rows = parts[i][width : width + EXTRA, :].astype(jnp.float32)
            lse.append(rows[3 * h : 3 * h + 1] + rows[3 * h + 1 : 3 * h + 2] + rows[3 * h + 2 : 3 * h + 3])
        lse[1] = jnp.where(valid_ref[0] > 0, lse[1], FAR)
        lse[2] = jnp.where(valid_ref[1] > 0, lse[2], FAR)
        top = jnp.maximum(jnp.maximum(lse[0], lse[1]), lse[2])
        shares = [jnp.exp(x - top) for x in lse]
        total = shares[0] + shares[1] + shares[2]
        lanes = slice(h * dim, (h + 1) * dim)
        merged = parts[0][lanes, :].astype(jnp.float32) * (shares[0] / total)
        merged += parts[1][lanes, :].astype(jnp.float32) * (shares[1] / total)
        merged += parts[2][lanes, :].astype(jnp.float32) * (shares[2] / total)
        merged = jnp.transpose(merged).astype(jnp.bfloat16)
        for k in range(4):
            outs[k][:, lanes] = merged[k * quarter : (k + 1) * quarter, :]


def merge(valid, parts, heads):
    width, brick = parts[0].shape[0] - EXTRA, parts[0].shape[1]
    vmem = pl.BlockSpec(memory_space=pltpu.VMEM)
    return pl.pallas_call(
        functools.partial(merge_kernel, heads=heads),
        out_shape=[jax.ShapeDtypeStruct((brick // 4, width), jnp.bfloat16)] * 4,
        in_specs=[pl.BlockSpec(memory_space=pltpu.SMEM)] + [vmem] * 3,
        out_specs=[vmem] * 4,
        compiler_params=pltpu.CompilerParams(vmem_limit_bytes=VMEM_SMALL),
        name="merge",
    )(valid, *parts)


def named(lists, column, pair, time, xh):
    tile_time = lists // 2 % TIME_TILES
    tile_pair = lists // (2 * TIME_TILES) % 2
    tile_column = lists // (4 * TIME_TILES)
    beside = jnp.where(tile_column == column + 1 - 2 * (column % 2), 1, 2)
    column_slot = jnp.where(tile_column == column, 0, beside)
    slot = jnp.where(tile_pair == pair, column_slot * 2 + ((lists % 2) ^ xh), 6 + column_slot)
    slot = jnp.where((lists >= 0) & (tile_time == time), slot, -1)
    mask = jnp.any(slot[..., None] == jnp.arange(POOL, dtype=jnp.int32), axis=-2)
    return jnp.where(xh == 1, mask[..., ::-1, :], mask)


def local(qkv, key_tiles):
    heads = key_tiles.shape[0]
    seq = lax.axis_index("seq")
    head = lax.axis_index("head")
    y, xh, z = seq // 16, seq // 8 % 2, seq % 8
    core = head % 2
    pair, time = z // TIME_TILES, z % TIME_TILES
    at = head.astype(jnp.int32).reshape(1)
    place = ((1 - pair) ^ xh).astype(jnp.int32).reshape(1)
    valid = jnp.stack([time > 0, time < TIME_TILES - 1])

    entries = key_tiles.size
    names = key_tiles.astype(jnp.bfloat16).reshape(1, entries)
    names = jnp.pad(names, ((0, EXTRA - 1), (0, qkv.shape[2] // 4 - entries)))
    pieces = split(at, qkv, names)
    kv_parts = [send(pieces[4 + k], spread_pairs(k)) for k in range(4)]
    kv_parts[0], q_pieces = lax.optimization_barrier((kv_parts[0], pieces[:4]))
    q_parts = [send(q_pieces[k], spread_pairs(k)) for k in range(4)]
    kv_own, edge = stack(place, kv_parts)
    edge_own = send(edge, edge_pairs())
    bodies = (kv_own, send(kv_own, core_pairs()), send(kv_own, column_pairs()))
    q_own = stack_queries(q_parts)
    q_prev = send(q_own, time_pairs(1))
    q_next = send(q_own, time_pairs(-1))

    def masks(queries):
        lists = jnp.stack([q[-EXTRA, :entries] for q in queries])
        lists = lists.astype(jnp.int32).reshape((len(queries),) + key_tiles.shape)
        return named(lists, 2 * y + core, pair, time, xh)

    mask_own = masks((q_own,)).astype(jnp.int32).reshape(-1)
    mask_away = (masks((q_prev, q_next)) & valid[:, None, None, None]).astype(jnp.int32).reshape(-1)

    begun = attend(mask_own, (q_own,), bodies, (), heads, 0, 0, jnp.float32)
    begun, edge_own = lax.optimization_barrier((begun, edge_own))
    edges = (edge_own, send(edge_own, core_pairs()), send(edge_own, column_pairs()))
    o_prev, o_next = attend(mask_away, (q_prev, q_next), bodies + edges, (), heads, 0, 0, jnp.bfloat16)
    o_before = send(o_next, time_pairs(1))
    o_after = send(o_prev, time_pairs(-1))
    (o_own,) = attend(mask_own, (q_own,), edges, begun, heads, 0, 6, jnp.float32)

    chunks = merge(valid.astype(jnp.int32), (o_own, o_before, o_after), heads)
    home = [send(chunks[k], gather_pairs(k)) for k in range(4)]
    return join(at, home)


def solution(mesh):
    placed = (P(None, ("seq", "head"), None), P("head", "seq", None))
    return jax.shard_map(
        local, mesh=mesh, in_specs=placed, out_specs=P(("seq", "head"), None), check_vma=False
    )
```

```python
import functools
import math

import jax
import jax.numpy as jnp
from jax import lax
from jax.experimental import pallas as pl
from jax.experimental.pallas import tpu as pltpu
from jax.sharding import PartitionSpec as P

TIME_TILES = 4
AXES = ("seq", "head")
FAR = -1e30
VMEM_LIMIT = 28 * 2**20
VMEM_SMALL = 12 * 2**20
BATCH = 2
EXTRA = 16
POOL = 9


def linear(y, xh, z, xl, core):
    return ((y * 2 + xh) * 8 + z) * 4 + xl * 2 + core


def devices():
    for y in range(4):
        for xh in range(2):
            for z in range(8):
                for xl in range(2):
                    for core in range(2):
                        yield y, xh, z, xl, core


def spread_pairs(k):
    pairs = []
    for y, xh, z, xl, core in devices():
        group = (2 * xl + core) ^ k
        pairs.append((linear(y, xh, z, xl, core), linear(y, group >> 1, z, group & 1, xh)))
    return pairs


def gather_pairs(k):
    return [(b, a) for a, b in spread_pairs(k)]


def edge_pairs():
    return [(linear(y, xh, z, xl, c), linear(y, xh, z ^ 4, xl, c)) for y, xh, z, xl, c in devices()]


def core_pairs():
    return [(linear(y, xh, z, xl, c), linear(y, xh, z, xl, 1 - c)) for y, xh, z, xl, c in devices()]


def column_pairs():
    pairs = []
    for y, xh, z, xl, core in devices():
        to = y + (1 if core == 1 else -1)
        if 0 <= to < 4:
            pairs.append((linear(y, xh, z, xl, core), linear(to, xh, z, xl, 1 - core)))
    return pairs


def time_pairs(by):
    pairs = []
    for y, xh, z, xl, core in devices():
        if 0 <= z % TIME_TILES + by < TIME_TILES:
            pairs.append((linear(y, xh, z, xl, core), linear(y, xh, z + by, xl, core)))
    return pairs


def send(x, pairs):
    return lax.ppermute(x, AXES, pairs)


def split_kernel(at_ref, qkv_ref, names_ref, *outs):
    width = outs[0].shape[-1]
    rows = qkv_ref.shape[1]
    for k in range(4):
        lanes = pl.ds(pl.multiple_of((at_ref[0] ^ k) * width, 128), width)
        outs[k][:rows, :] = qkv_ref[0, :, lanes]
        outs[k][rows:, :] = names_ref[...]
        outs[4 + k][...] = qkv_ref[1:3, :, lanes]


def split(at, qkv, names):
    _, rows, columns = qkv.shape
    width = columns // 4
    vmem = pl.BlockSpec(memory_space=pltpu.VMEM)
    shapes = [jax.ShapeDtypeStruct((rows + EXTRA, width), qkv.dtype)] * 4
    shapes += [jax.ShapeDtypeStruct((2, rows, width), qkv.dtype)] * 4
    return pl.pallas_call(
        split_kernel,
        out_shape=shapes,
        in_specs=[pl.BlockSpec(memory_space=pltpu.SMEM), vmem, vmem],
        out_specs=[vmem] * 8,
        compiler_params=pltpu.CompilerParams(vmem_limit_bytes=VMEM_SMALL),
        name="split",
    )(at, qkv, names)


def stack_kernel(place_ref, *refs):
    parts, kv_ref, edge_ref, sems = refs[:4], refs[4], refs[5], refs[6]
    rows = parts[0].shape[1]
    copies = []
    for k in range(4):
        copies.append(pltpu.make_async_copy(parts[k], kv_ref.at[:, pl.ds(k * rows, rows)], sems.at[k]))
    for copy in copies:
        copy.start()
    for copy in copies:
        copy.wait()
    edge_ref[...] = kv_ref[:, pl.ds(pl.multiple_of(place_ref[0] * (2 * rows), 128), 2 * rows), :]


def stack(place, parts):
    _, rows, width = parts[0].shape
    vmem = pl.BlockSpec(memory_space=pltpu.VMEM)
    return pl.pallas_call(
        stack_kernel,
        out_shape=[
            jax.ShapeDtypeStruct((2, 4 * rows, width), parts[0].dtype),
            jax.ShapeDtypeStruct((2, 2 * rows, width), parts[0].dtype),
        ],
        in_specs=[pl.BlockSpec(memory_space=pltpu.SMEM)] + [pl.BlockSpec(memory_space=pl.ANY)] * 4,
        out_specs=[vmem] * 2,
        scratch_shapes=[pltpu.SemaphoreType.DMA((4,))],
        compiler_params=pltpu.CompilerParams(vmem_limit_bytes=VMEM_SMALL),
        name="stack",
    )(place, *parts)


def stack_queries_kernel(*refs):
    parts, q_ref, sems = refs[:4], refs[4], refs[5]
    rows = parts[0].shape[0] - EXTRA
    copies = []
    for k in range(4):
        into = q_ref.at[pl.ds(k * rows, rows)]
        copies.append(pltpu.make_async_copy(parts[k].at[pl.ds(0, rows)], into, sems.at[k]))
    into = q_ref.at[pl.ds(4 * rows, EXTRA)]
    copies.append(pltpu.make_async_copy(parts[0].at[pl.ds(rows, EXTRA)], into, sems.at[4]))
    for copy in copies:
        copy.start()
    for copy in copies:
        copy.wait()


def stack_queries(parts):
    rows, width = parts[0].shape[0] - EXTRA, parts[0].shape[1]
    return pl.pallas_call(
        stack_queries_kernel,
        out_shape=jax.ShapeDtypeStruct((4 * rows + EXTRA, width), parts[0].dtype),
        in_specs=[pl.BlockSpec(memory_space=pl.ANY)] * 4,
        out_specs=pl.BlockSpec(memory_space=pltpu.VMEM),
        scratch_shapes=[pltpu.SemaphoreType.DMA((5,))],
        compiler_params=pltpu.CompilerParams(vmem_limit_bytes=VMEM_SMALL),
        name="stack_queries",
    )(*parts)


def join_kernel(at_ref, *refs):
    parts, out_ref = refs[:4], refs[4]
    width = parts[0].shape[-1]
    for k in range(4):
        out_ref[:, pl.ds(pl.multiple_of((at_ref[0] ^ k) * width, 128), width)] = parts[k][...]


def join(at, parts):
    rows, width = parts[0].shape
    vmem = pl.BlockSpec(memory_space=pltpu.VMEM)
    return pl.pallas_call(
        join_kernel,
        out_shape=jax.ShapeDtypeStruct((rows, 4 * width), parts[0].dtype),
        in_specs=[pl.BlockSpec(memory_space=pltpu.SMEM)] + [vmem] * 4,
        out_specs=vmem,
        compiler_params=pltpu.CompilerParams(vmem_limit_bytes=VMEM_SMALL),
        name="join",
    )(at, *parts)


def attend_kernel(mask_ref, *refs, sets, pieces, begun, tiles, first_set, first_tile, heads, tile, dim):
    queries = refs[:sets]
    sources = refs[sets : sets + pieces]
    starts = refs[sets + pieces : sets + pieces + begun]
    refs = refs[sets + pieces + begun :]
    outs = refs[:sets]
    pool, held, turned_q, turned_v, max_ref, sum_ref, acc_ref, of_query, of_key = refs[sets : sets + 9]
    rest = refs[sets + 9 :]
    score_refs = (rest[:BATCH], rest[BATCH : 2 * BATCH])
    top_refs = (rest[2 * BATCH : 3 * BATCH], rest[3 * BATCH : 4 * BATCH])
    sems = rest[4 * BATCH]
    count_q = sets * heads * 2

    copies = []
    for n in range(sets):
        copies.append(pltpu.make_async_copy(queries[n].at[pl.ds(0, 2 * tile)], held.at[n], sems.at[n]))
    at = 0
    for source in sources:
        for r in range(source.shape[1] // tile):
            copies.append(
                pltpu.make_async_copy(source.at[:, pl.ds(r * tile, tile)], pool.at[at], sems.at[sets + at])
            )
            at += 1
    for copy in copies:
        copy.start()

    def list_pairs_of(s, count):
        for j in range(tiles):
            of_query[count] = s
            of_key[count] = j
            count = count + mask_ref[(first_set * heads * 2 + s) * POOL + first_tile + j]
        return count

    count = lax.fori_loop(0, count_q, list_pairs_of, 0)
    for i in range(4 * BATCH):
        of_query[count + i] = count_q
        of_key[count + i] = 0
    scale = dim**-0.5
    factor = scale * math.log2(math.e)
    width = heads * dim
    if begun:
        sum_ref[...] = jnp.full_like(sum_ref, 0.125)
        for n in range(sets):
            for h in range(heads):
                lse = starts[n][width + 3 * h : width + 3 * h + 1, :]
                for i in range(1, 3):
                    lse = lse + starts[n][width + 3 * h + i : width + 3 * h + i + 1, :]
                for p in range(2):
                    s = (n * heads + h) * 2 + p
                    at = slice(p * tile, (p + 1) * tile)
                    max_ref[s, :1, :] = lse[:, at] / scale
                    acc_ref[s] = starts[n][h * dim : (h + 1) * dim, at]
        max_ref[count_q] = jnp.zeros((8, tile), jnp.float32)
        acc_ref[count_q] = jnp.zeros((dim, tile), jnp.float32)
    else:
        max_ref[...] = jnp.full_like(max_ref, FAR)
        sum_ref[...] = jnp.zeros_like(sum_ref)
        acc_ref[...] = jnp.zeros_like(acc_ref)
    for copy in copies:
        copy.wait()
    for n in range(sets):
        for h in range(heads):
            for p in range(2):
                turned_q[(n * heads + h) * 2 + p] = jnp.transpose(
                    held[n, p * tile : (p + 1) * tile, h * dim : (h + 1) * dim]
                )
    turned_q[count_q] = turned_q[0]
    for h in range(heads):
        for j in range(tiles):
            turned_v[h * tiles + j] = jnp.transpose(pool[j, 1, :, h * dim : (h + 1) * dim])

    def score(i, out_ref, top_ref):
        s, j = of_query[i], of_key[i]
        h = lax.rem(s // 2, heads)
        keys = pool[j, 0, :, pl.ds(pl.multiple_of(h * dim, dim), dim)]
        scores = jnp.dot(keys, turned_q[s], preferred_element_type=jnp.float32)
        out_ref[...] = scores
        top_ref[...] = jnp.max(scores.reshape(tile // 8, 8, tile), axis=0)

    def weigh(i, in_ref, top_ref):
        s, j = of_query[i], of_key[i]
        h = lax.rem(s // 2, heads)
        old = max_ref[s, :1, :]
        new = jnp.maximum(old, jnp.max(top_ref[...], axis=0, keepdims=True))
        shrink = jnp.exp2((old - new) * factor)
        max_ref[s, :1, :] = new
        weights = jnp.exp2((in_ref[...] - new) * factor)
        sum_ref[s] = sum_ref[s] * shrink + jnp.sum(weights.reshape(tile // 8, 8, tile), axis=0)
        acc_ref[s] = acc_ref[s] * shrink + jnp.dot(
            turned_v[h * tiles + j], weights.astype(jnp.bfloat16), preferred_element_type=jnp.float32
        )

    for u in range(BATCH):
        score(u, score_refs[0][u], top_refs[0][u])

    def step(t, carry):
        for half in range(2):
            base = (2 * t + half) * BATCH
            for u in range(BATCH):
                score(base + BATCH + u, score_refs[1 - half][u], top_refs[1 - half][u])
            for u in range(BATCH):
                weigh(base + u, score_refs[half][u], top_refs[half][u])
        return carry

    lax.fori_loop(0, (count + 2 * BATCH - 1) // (2 * BATCH), step, 0)

    for n in range(sets):
        outs[n][width : width + EXTRA, :] = jnp.zeros((EXTRA, 2 * tile), outs[n].dtype)
        for h in range(heads):
            for p in range(2):
                s = (n * heads + h) * 2 + p
                at = slice(p * tile, (p + 1) * tile)
                total = jnp.maximum(jnp.sum(sum_ref[s], axis=0, keepdims=True), 1e-30)
                outs[n][h * dim : (h + 1) * dim, at] = (acc_ref[s] / total).astype(outs[n].dtype)
                left = max_ref[s, :1, :] * scale + jnp.log(total)
                for i in range(3):
                    part = left.astype(outs[n].dtype)
                    outs[n][width + 3 * h + i : width + 3 * h + i + 1, at] = part
                    left = left - part.astype(jnp.float32)


def attend(mask, queries, sources, starts, heads, first_set, first_tile, out_dtype):
    sets = len(queries)
    brick, width = queries[0].shape[0] - EXTRA, queries[0].shape[1]
    tile = brick // 2
    dim = width // heads
    tiles = sum(source.shape[1] for source in sources) // tile
    count_q = sets * heads * 2
    hbm = pl.BlockSpec(memory_space=pl.ANY)
    vmem = pl.BlockSpec(memory_space=pltpu.VMEM)
    return pl.pallas_call(
        functools.partial(
            attend_kernel,
            sets=sets,
            pieces=len(sources),
            begun=len(starts),
            tiles=tiles,
            first_set=first_set,
            first_tile=first_tile,
            heads=heads,
            tile=tile,
            dim=dim,
        ),
        out_shape=[jax.ShapeDtypeStruct((width + EXTRA, brick), out_dtype)] * sets,
        in_specs=[pl.BlockSpec(memory_space=pltpu.SMEM)] + [hbm] * (sets + len(sources)) + [vmem] * len(starts),
        out_specs=[vmem] * sets,
        scratch_shapes=[
            pltpu.VMEM((tiles, 2, tile, width), jnp.bfloat16),
            pltpu.VMEM((sets, brick, width), jnp.bfloat16),
            pltpu.VMEM((count_q + 1, dim, tile), jnp.bfloat16),
            pltpu.VMEM((tiles * heads, dim, tile), jnp.bfloat16),
            pltpu.VMEM((count_q + 1, 8, tile), jnp.float32),
            pltpu.VMEM((count_q + 1, 8, tile), jnp.float32),
            pltpu.VMEM((count_q + 1, dim, tile), jnp.float32),
            pltpu.SMEM((count_q * tiles + 8 * BATCH,), jnp.int32),
            pltpu.SMEM((count_q * tiles + 8 * BATCH,), jnp.int32),
        ]
        + [pltpu.VMEM((tile, tile), jnp.float32)] * (2 * BATCH)
        + [pltpu.VMEM((8, tile), jnp.float32)] * (2 * BATCH)
        + [pltpu.SemaphoreType.DMA((sets + tiles,))],
        compiler_params=pltpu.CompilerParams(vmem_limit_bytes=VMEM_LIMIT),
        name=f"attend_{sets}_{tiles}",
    )(mask, *queries, *sources, *starts)


def merge_kernel(valid_ref, *refs, heads):
    parts, outs = refs[:3], refs[3:]
    width, brick = parts[0].shape[0] - EXTRA, parts[0].shape[1]
    dim = width // heads
    quarter = brick // 4
    for h in range(heads):
        lse = []
        for i in range(3):
            rows = parts[i][width : width + EXTRA, :].astype(jnp.float32)
            lse.append(rows[3 * h : 3 * h + 1] + rows[3 * h + 1 : 3 * h + 2] + rows[3 * h + 2 : 3 * h + 3])
        lse[1] = jnp.where(valid_ref[0] > 0, lse[1], FAR)
        lse[2] = jnp.where(valid_ref[1] > 0, lse[2], FAR)
        top = jnp.maximum(jnp.maximum(lse[0], lse[1]), lse[2])
        shares = [jnp.exp(x - top) for x in lse]
        total = shares[0] + shares[1] + shares[2]
        lanes = slice(h * dim, (h + 1) * dim)
        merged = parts[0][lanes, :].astype(jnp.float32) * (shares[0] / total)
        merged += parts[1][lanes, :].astype(jnp.float32) * (shares[1] / total)
        merged += parts[2][lanes, :].astype(jnp.float32) * (shares[2] / total)
        merged = jnp.transpose(merged).astype(jnp.bfloat16)
        for k in range(4):
            outs[k][:, lanes] = merged[k * quarter : (k + 1) * quarter, :]


def merge(valid, parts, heads):
    width, brick = parts[0].shape[0] - EXTRA, parts[0].shape[1]
    vmem = pl.BlockSpec(memory_space=pltpu.VMEM)
    return pl.pallas_call(
        functools.partial(merge_kernel, heads=heads),
        out_shape=[jax.ShapeDtypeStruct((brick // 4, width), jnp.bfloat16)] * 4,
        in_specs=[pl.BlockSpec(memory_space=pltpu.SMEM)] + [vmem] * 3,
        out_specs=[vmem] * 4,
        compiler_params=pltpu.CompilerParams(vmem_limit_bytes=VMEM_SMALL),
        name="merge",
    )(valid, *parts)


def named(lists, column, pair, time, xh):
    tile_time = lists // 2 % TIME_TILES
    tile_pair = lists // (2 * TIME_TILES) % 2
    tile_column = lists // (4 * TIME_TILES)
    beside = jnp.where(tile_column == column + 1 - 2 * (column % 2), 1, 2)
    column_slot = jnp.where(tile_column == column, 0, beside)
    slot = jnp.where(tile_pair == pair, column_slot * 2 + ((lists % 2) ^ xh), 6 + column_slot)
    slot = jnp.where((lists >= 0) & (tile_time == time), slot, -1)
    mask = jnp.any(slot[..., None] == jnp.arange(POOL, dtype=jnp.int32), axis=-2)
    return jnp.where(xh == 1, mask[..., ::-1, :], mask)


def local(qkv, key_tiles):
    heads = key_tiles.shape[0]
    seq = lax.axis_index("seq")
    head = lax.axis_index("head")
    y, xh, z = seq // 16, seq // 8 % 2, seq % 8
    core = head % 2
    pair, time = z // TIME_TILES, z % TIME_TILES
    at = head.astype(jnp.int32).reshape(1)
    place = ((1 - pair) ^ xh).astype(jnp.int32).reshape(1)
    valid = jnp.stack([time > 0, time < TIME_TILES - 1])

    entries = key_tiles.size
    names = key_tiles.astype(jnp.bfloat16).reshape(1, entries)
    names = jnp.pad(names, ((0, EXTRA - 1), (0, qkv.shape[2] // 4 - entries)))
    pieces = split(at, qkv, names)
    q_parts = [send(pieces[k], spread_pairs(k)) for k in range(4)]
    kv_pieces = list(pieces[4:])
    for k in range(1, 4):
        q_parts[k], kv_pieces[k] = lax.optimization_barrier((q_parts[k], kv_pieces[k]))
    kv_parts = [send(kv_pieces[k], spread_pairs(k)) for k in range(4)]
    q_own = stack_queries(q_parts)
    q_own, kv_parts[0] = lax.optimization_barrier((q_own, kv_parts[0]))
    q_prev = send(q_own, time_pairs(1))
    q_next = send(q_own, time_pairs(-1))
    place, q_prev, q_next = lax.optimization_barrier((place, q_prev, q_next))
    lists = jnp.stack([q[-EXTRA, :entries] for q in (q_own, q_prev, q_next)])
    lists = lists.astype(jnp.int32).reshape((3,) + key_tiles.shape)
    mask = named(lists, 2 * y + core, pair, time, xh)
    here = jnp.concatenate([jnp.ones((1,), bool), valid])
    mask = (mask & here[:, None, None, None]).astype(jnp.int32).reshape(-1)
    kv_own, edge = stack(place, kv_parts)
    edge_own = send(edge, edge_pairs())
    bodies = (kv_own, send(kv_own, core_pairs()), send(kv_own, column_pairs()))

    begun = attend(mask, (q_prev, q_next), bodies, (), heads, 1, 0, jnp.float32)
    begun, edge_own = lax.optimization_barrier((begun, edge_own))
    edges = (edge_own, send(edge_own, core_pairs()), send(edge_own, column_pairs()))
    o_prev, o_next = attend(mask, (q_prev, q_next), edges, begun, heads, 1, 6, jnp.bfloat16)
    o_before = send(o_next, time_pairs(1))
    o_after = send(o_prev, time_pairs(-1))
    (o_own,) = attend(mask, (q_own,), bodies + edges, (), heads, 0, 0, jnp.float32)

    chunks = merge(valid.astype(jnp.int32), (o_own, o_before, o_after), heads)
    home = [send(chunks[k], gather_pairs(k)) for k in range(4)]
    return join(at, home)


def solution(mesh):
    placed = (P(None, ("seq", "head"), None), P("head", "seq", None))
    return jax.shard_map(
        local, mesh=mesh, in_specs=placed, out_specs=P(("seq", "head"), None), check_vma=False
    )
```
